128 devices in a mesh: row: 8 (over z_lo, y), col: 16 (over z_hi, x, core).
Axes of the slice: x: 4, y: 4, z: 4 (z_hi: 2, z_lo: 2; z = z_hi * 2 + z_lo), core: 2. Of those that a mesh axis runs over, the one named last changes fastest.
Arguments:
- front: float32 [16384, 16384], P('row', 'col'), as said below
- child_updates: bfloat16 [8, 4096, 4096], P('row', 'col'), as said below
- child_maps: int32 [8, 16], replicated, may hold values from 0 to 63, as said below
- fill_mask: int32 [64, 64], replicated, may hold values from 0 to 1, as said below
Outputs:
- factored: float32 [16384, 16384], P('row', 'col')
The draws below stay inside these ranges and needn't reach their ends.
Inputs may be any that keep to these rules, and one draw needn't show every extreme that they name: front is symmetric. `child_updates`: each child's matrix is symmetric. `child_maps`: each row lists 16 distinct block indices in ascending order; in every aligned run of 4 indices a row names at most 2, and exactly 2 in some run; in every aligned run of 8 indices at most 4, and exactly 4 in some run. `fill_mask`: symmetric, ones on the diagonal.
All inputs are finite; a program needn't handle non-finite values.
Results may differ from the reference program's by a relative error of at most 0.0003.
Values may be sent and summed in bfloat16 or wider, within the bound.
A program may use at most 192 MiB of HBM per device.

```python
import math
import jax
import jax.numpy as jnp
from jax import lax

BS = 256
NB = 64
CB = 16
PB = 2
STEPS = 2
N_ROW = 8
N_COL = 16


def symmetric_entries(key, count, leading):
    entry_key = jax.random.fold_in(key, 11)
    entries = jax.random.truncated_normal(entry_key, -4.0, 4.0, leading + (count, count), jnp.float32)
    return (entries + jnp.swapaxes(entries, -1, -2)) * 0.7071


def diagonal_values(key, count, leading, low, high):
    diag_key = jax.random.fold_in(key, 13)
    values = jax.random.uniform(diag_key, leading + (count,), jnp.float32, low, high)
    return values


def draw_front(key, part):
    count = NB * BS
    region = STEPS * PB * BS
    indices = jnp.arange(count)
    rough = jax.random.uniform(jax.random.fold_in(key, 17), (count,), jnp.float32, 0.8, 1.2)
    scales = (1.0 + 2.0 * indices.astype(jnp.float32) / count) * rough
    spread = 0.06 / math.sqrt(region)
    random_part = symmetric_entries(key, count, ()) * spread * (scales[:, None] * scales[None, :])
    weak_links = jax.random.uniform(jax.random.fold_in(key, 19), (count,), jnp.float32, 0.03, 0.05)
    strong_links = jax.random.uniform(jax.random.fold_in(key, 23), (count,), jnp.float32, 0.2, 0.3)
    links = jnp.where(indices < region - 1, strong_links, weak_links)
    previous_links = jnp.concatenate([jnp.zeros((1,), jnp.float32), links[:-1]])
    above = indices[None, :] == indices[:, None] + 1
    below = indices[:, None] == indices[None, :] + 1
    coupled = jnp.where(above, -links[:, None], jnp.where(below, -links[None, :], random_part))
    outer_diagonal = diagonal_values(key, count, (), 0.4, 0.6)
    nugget = diagonal_values(jax.random.fold_in(key, 29), count, (), 0.3, 0.4)
    lead_diagonal = previous_links + links + nugget
    diagonal_value = jnp.where(indices < region, lead_diagonal, outer_diagonal)
    diagonal_flag = indices[:, None] == indices[None, :]
    return jnp.where(diagonal_flag, diagonal_value[:, None], coupled)


def draw_child_updates(key, part):
    count = CB * BS
    spread = 0.06 / math.sqrt(count)
    symmetric = symmetric_entries(key, count, (N_ROW,)) * spread
    diagonal_value = diagonal_values(key, count, (N_ROW,), 0.05, 0.15)
    indices = jnp.arange(count)
    diagonal_flag = indices[:, None] == indices[None, :]
    return jnp.where(diagonal_flag, diagonal_value[..., :, None], symmetric).astype(jnp.bfloat16)


def draw_child_maps(key, part):
    runs_per_row = N_COL // N_ROW
    per_col = NB // N_COL

    def draw_child(child_key):
        pick_key = jax.random.fold_in(child_key, 1)
        rank_key = jax.random.fold_in(child_key, 2)
        run_of_col = jnp.arange(N_COL) // runs_per_row
        if CB == N_COL:
            chosen = jax.random.permutation(pick_key, N_ROW)
            counts = jnp.where(run_of_col == chosen[0], 2, jnp.where(run_of_col == chosen[1], 0, 1)).astype(jnp.int32)
        else:
            counts = jnp.full((N_COL,), 2, jnp.int32)
        rankings = jax.vmap(lambda col_key: jax.random.permutation(col_key, per_col))(jax.random.split(rank_key, N_COL))
        picked = (rankings < counts[:, None]).reshape(-1).astype(jnp.int32)
        positions = jnp.cumsum(picked) - 1
        targets = jnp.where(picked == 1, positions, CB).astype(jnp.int32)
        return jnp.zeros((CB + 1,), jnp.int32).at[targets].set(jnp.arange(NB, dtype=jnp.int32))[:CB]
    child_keys = jax.random.split(jax.random.fold_in(key, 5), N_ROW)
    return jax.vmap(draw_child)(child_keys)


def draw_fill_mask(key, part):
    coin_flips = jax.random.randint(jax.random.fold_in(key, 3), (NB, NB), 0, 2)
    indices = jnp.arange(NB)
    symmetric = jnp.where(indices[:, None] > indices[None, :], coin_flips, coin_flips.T)
    return jnp.where(indices[:, None] == indices[None, :], 1, symmetric).astype(jnp.int32)


def setup_inputs(seed: int = 0) -> dict:
    seeds = jax.random.split(jax.random.key(seed), 5)
    front = draw_front(jax.random.fold_in(seeds[4], 71), 0)
    child_updates = draw_child_updates(jax.random.fold_in(seeds[4], 71), 0)
    child_maps = draw_child_maps(jax.random.fold_in(seeds[4], 71), 0)
    fill_mask = draw_fill_mask(jax.random.fold_in(seeds[4], 71), 0)
    return {"front": front, "child_updates": child_updates, "child_maps": child_maps, "fill_mask": fill_mask}


def reference(front, child_updates, child_maps, fill_mask):
    front_order = NB * BS
    child_order = CB * BS
    panel_width = PB * BS
    offsets = jnp.arange(child_order, dtype=jnp.int32)

    def add_child(child_index, summed):
        block_map = lax.dynamic_index_in_dim(child_maps, child_index, 0, keepdims=False)
        targets = (block_map[offsets // BS] * BS + offsets % BS).astype(jnp.int32)
        update_piece = lax.dynamic_index_in_dim(child_updates, child_index, 0, keepdims=False).astype(jnp.float32)
        return summed.at[targets[:, None], targets[None, :]].add(update_piece)
    extended = lax.fori_loop(0, N_ROW, add_child, jnp.zeros((front_order, front_order), jnp.float32))
    fill_float = fill_mask.astype(jnp.float32)
    mask_full = jnp.broadcast_to(fill_float[:, None, :, None], (NB, BS, NB, BS)).reshape(front_order, front_order)
    working = (front + extended) * mask_full
    columns = jnp.arange(front_order)
    blocks = columns // BS
    for step_index in range(STEPS):
        first_col = step_index * panel_width
        finish = first_col + panel_width
        factor = jnp.linalg.cholesky(working[first_col:finish, first_col:finish])
        solved = jax.scipy.linalg.solve_triangular(factor, working[:, first_col:finish].T, lower=True).T
        solved = solved.at[first_col:finish].set(factor)
        product = jnp.dot(solved, solved.T, precision=lax.Precision.HIGHEST)
        working = jnp.where(columns[None, :] >= finish, working - product * mask_full, working)
        working = working.at[:, first_col:finish].set(solved)
    return jnp.where(blocks[:, None] >= blocks[None, :], working, 0.0)
```

```python
import functools

import jax
import jax.numpy as jnp
from jax import lax
from jax.experimental import pallas as pl
from jax.experimental.pallas import tpu as pltpu
from jax.sharding import PartitionSpec as P

BS = 256
NR = 8
NC = 16
MESH = pl.DeviceIdType.MESH
HI = lax.Precision.HIGHEST
f32 = jnp.float32
bf16 = jnp.bfloat16
ANY = pl.BlockSpec(memory_space=pl.ANY)
VM = pl.BlockSpec(memory_space=pltpu.VMEM)
SM = pl.BlockSpec(memory_space=pltpu.SMEM)


def dot(a, b, precision=HI):
    return lax.dot_general(
        a, b, (((1,), (0,)), ((), ())), precision=precision, preferred_element_type=f32
    )


def dot_t(a, b, precision=HI):
    return lax.dot_general(
        a, b, (((1,), (1,)), ((), ())), precision=precision, preferred_element_type=f32
    )


def t_dot(a, b, precision=HI):
    return lax.dot_general(
        a, b, (((0,), (0,)), ((), ())), precision=precision, preferred_element_type=f32
    )


def row_of(x, k):
    return jnp.broadcast_to(x[k : k + 1, :], (8, 128))


def lane_of(x, k):
    return jnp.broadcast_to(x[:, k : k + 1], (8, 128))


def factor_128(m_ref, ahead=3):
    sub = lax.broadcasted_iota(jnp.int32, (8, 128), 0)
    lane = lax.broadcasted_iota(jnp.int32, (8, 128), 1)
    held = {}
    for s in range(16):
        last = min(s + ahead + 1, 16)
        for q in range(s, last):
            if q not in held:
                held[q] = (m_ref[8 * q : 8 * q + 8, :128], m_ref[8 * q : 8 * q + 8, 128:])
        left, right = held.pop(s)
        v = [lane_of(left, 8 * s + j) for j in range(8)]
        z = [jnp.where(sub == j, 1.0, 0.0).astype(f32) for j in range(8)]
        scale = jnp.zeros((8, 128), f32)
        rows, inverses = [], []
        for k in range(8):
            root = lax.rsqrt(row_of(v[k], k))
            scale = jnp.where(sub == k, root, scale)
            inverse = root * root
            inverses.append(inverse)
            below = jnp.where(sub > k, v[k], 0.0) * inverse
            row = {}
            for j in range(k + 1, 8):
                row[j] = row_of(v[j], k)
                v[j] = v[j] - below * row[j]
            rows.append(row)
            if k < 7:
                for j in range(k + 1):
                    z[j] = z[j] - below * row_of(z[j], k)
        new_left = z[0] * row_of(left, 0)
        new_right = z[0] * row_of(right, 0)
        for j in range(1, 8):
            new_left = new_left + z[j] * row_of(left, j)
            new_right = new_right + z[j] * row_of(right, j)
        new_left = jnp.where(lane >= 8 * s + sub, new_left, 0.0)
        rows_left = [row_of(new_left, k) for k in range(8)]
        rows_right = [row_of(new_right, k) for k in range(8)]
        for q in range(s + 1, last):
            x, y = held[q]
            w = [lane_of(x, 8 * s + j) for j in range(8)]
            for k in range(8):
                times = w[k] * inverses[k]
                for j in range(k + 1, 8):
                    w[j] = w[j] - times * rows[k][j]
                x = x - times * rows_left[k]
                y = y - times * rows_right[k]
            held[q] = (x, y)
        new_left = new_left * scale
        new_right = new_right * scale
        m_ref[8 * s : 8 * s + 8, :128] = new_left
        m_ref[8 * s : 8 * s + 8, 128:] = new_right
        low = 8 * last
        if low < 128:
            update = t_dot(new_left, jnp.concatenate([new_left, new_right], axis=1))
            m_ref[low:, :] = m_ref[low:, :] - update[low:, :]


def identity(count, dtype=f32):
    row = lax.broadcasted_iota(jnp.int32, (count, count), 0)
    lane = lax.broadcasted_iota(jnp.int32, (count, count), 1)
    return jnp.where(row == lane, 1.0, 0.0).astype(dtype)


def eliminate(wide, small, r_ref, width):
    def step(p, carry):
        at = pl.multiple_of(p * 128, 128)
        small[:, :128] = wide[pl.ds(at, 128), pl.ds(at, 128)]
        small[:, 128:] = identity(128)
        factor_128(small)
        r_ref[:, :width] = dot(small[:, 128:], wide[pl.ds(at, 128), :width])
        wide[pl.ds(at, 128), :width] = r_ref[:, :width]

        def trail(q, carry):
            down = pl.multiple_of(q * 128, 128)
            wide[pl.ds(down, 128), :width] = wide[pl.ds(down, 128), :width] - t_dot(
                r_ref[:, pl.ds(down, 128)], r_ref[:, :width]
            )
            return carry

        lax.fori_loop(p + 1, 4, trail, 0)
        return carry

    lax.fori_loop(0, 4, step, 0)


def factor_pivots(x_in, x_out, fm, wide, small, r_ref):
    for p in range(8):
        wide[64 * p : 64 * p + 64, 0:512] = x_in[p, 0]
        wide[64 * p : 64 * p + 64, 512:1024] = x_in[p, 1]
    wide[:, 1024:] = identity(512)
    eliminate(wide, small, r_ref, 1536)
    for p in range(8):
        x_out[p, 0] = wide[64 * p : 64 * p + 64, 1024:]
        x_out[p, 1] = wide[64 * p : 64 * p + 64, 512:1024]
    u = wide[:, 512:1024]
    for i in range(2):
        product = t_dot(u[:, 256 * i : 256 * i + 256], u)
        for j in range(2):
            keep = fm[2 + i, 2 + j].astype(f32)
            for p in range(4):
                wide[256 * i + 64 * p : 256 * i + 64 * p + 64, 256 * j : 256 * j + 256] = (
                    x_in[4 * i + p, 2, :, 256 * j : 256 * j + 256]
                    - keep * product[64 * p : 64 * p + 64, 256 * j : 256 * j + 256]
                )
    wide[:, 512:1024] = identity(512)
    eliminate(wide, small, r_ref, 1024)
    for p in range(8):
        x_out[p, 2] = wide[64 * p : 64 * p + 64, 512:1024]


def exchange_kernel(
    tab, fm, child, front, kids, ar, ac, x3, panel,
    blocks, turned, e1s, e1r, e2s, bs, br, pf, pb, xs,
    e1_s, e1_r, e2_s, e2_r, b_s, b_r, c1_s, c1_r, c2_s, c2_r, c3_s, c3_r,
    d1_s, d1_r, d2_s, d2_r, x1_s, x1_r, x2_s, x2_r, x3_s, x3_r, here,
):
    r = lax.axis_index("row")
    c = lax.axis_index("col")
    h = c // 2
    core = lax.rem(c, 2)
    sibling = c + 1 - 2 * core

    def send(src, dst, ss, rs, row, col):
        return pltpu.make_async_remote_copy(
            src_ref=src, dst_ref=dst, send_sem=ss, recv_sem=rs,
            device_id=(row, col), device_id_type=MESH,
        )

    def each(low, high, body):
        def run(i, carry):
            body(i)
            return carry

        lax.fori_loop(low, high, run, 0)

    def greet(row, col):
        pl.semaphore_signal(
            pltpu.get_barrier_semaphore(), inc=1, device_id=(row, col), device_id_type=MESH
        )

    each(1, NR, lambda d: greet(lax.rem(r + d, NR), c))
    each(1, NC, lambda d: greet(r, lax.rem(c + d, NC)))

    @pl.when(c < 2)
    def _():
        each(1, NR, lambda d: greet(lax.rem(r + d, NR), 1 - c))

    @pl.when(c == 0)
    def _():
        pltpu.make_async_copy(front, pf, here.at[0]).start()

    pl.semaphore_wait(pltpu.get_barrier_semaphore(), jnp.where(c < 2, 29, 22))

    for a in range(16):
        blocks[a] = child[:, BS * a : BS * a + BS]

    @pl.when(c < 2)
    def _():
        one = identity(BS, bf16)

        def turn(a):
            turned[a] = dot_t(one, blocks[a], None).astype(bf16)

        each(0, 16, turn)

        def give(d):
            q = lax.rem(r + d, NR)
            for n in range(4):
                bs[q, n] = turned[tab[q] + n]

            @pl.when((q != r) | (c == 1))
            def _():
                send(bs.at[q], br.at[pl.ds(8 * r + 4 * c, 4)], b_s.at[q], b_r.at[2 * r + c], q, 0).start()

            @pl.when((q == r) & (c == 0))
            def _():
                for n in range(4):
                    br[8 * r + n] = bs[q, n]

        each(1, NR + 1, give)

    def to_col(d):
        q = lax.rem(c + d, NC)

        @pl.when((q >= 1) & (q <= h + 8))
        def _():
            @pl.when(q != c)
            def _():
                for n in range(2):
                    e1s[q, :, BS * n : BS * n + BS] = blocks[tab[8 + q] + n]
                send(e1s.at[q], e1r.at[c], e1_s.at[q], e1_r.at[c], r, q).start()

            @pl.when(q == c)
            def _():
                for n in range(2):
                    e1r[c, :, BS * n : BS * n + BS] = blocks[tab[8 + q] + n]

    each(1, NC + 1, to_col)

    @pl.when(c == 0)
    def _():
        pltpu.make_async_copy(front, pf, here.at[0]).wait()

        def arrive(k):
            @pl.when(k != 2 * r)
            def _():
                send(
                    bs.at[0], br.at[pl.ds(4 * k, 4)], b_s.at[0], b_r.at[k], k // 2, lax.rem(k, 2)
                ).wait_recv()

        each(0, 16, arrive)

        def assemble(i):
            def add(k):
                for j in range(4):
                    times = (tab[120 + 8 * k + i] * tab[184 + 4 * k + j]).astype(f32)
                    block = br[8 * k + 4 * tab[88 + 4 * k + j] + tab[24 + 8 * k + i]]
                    at = pl.ds(j * BS, BS)
                    pf[i, :, at] = pf[i, :, at] + times * block.astype(f32)

            each(0, NR, add)
            for j in range(4):
                at = pl.ds(j * BS, BS)
                kept = pf[i, :, at] * fm[8 * r + i, j].astype(f32)
                pf[i, :, at] = kept
                pb[i, 0, :, at] = kept[:128].astype(bf16)
                pb[i, 1, :, at] = kept[128:].astype(bf16)

        each(0, 8, assemble)
        pltpu.make_async_copy(pf, panel, here.at[0]).start()

        @pl.when(r == 0)
        def _():
            for p in range(8):
                i, low = p // 4, 64 * (p % 4)
                xs[p, 0] = pf[i, low : low + 64, 0:512]
                xs[p, 1] = pf[i, low : low + 64, 512:1024]
                xs[p, 2] = pf[i + 2, low : low + 64, 512:1024]

            each(1, NR, lambda q: send(xs.at[q], x3.at[q], x1_s.at[q], x1_r, q, 0).start())
            each(1, NC, lambda q: send(xs.at[0], x3.at[0], x2_s.at[q], x2_r, 0, q).start())
            each(1, NR, lambda q: send(xs.at[0], x3.at[0], x3_s.at[q], x3_r.at[0], q, 0).start())
            pltpu.make_async_copy(xs, x3, here.at[1]).start()

        each(
            1, NC,
            lambda q: send(
                pb.at[q // 2, lax.rem(q, 2)], ar.at[q // 2, lax.rem(q, 2)], c1_s.at[q], c1_r, r, q
            ).start(),
        )
        each(
            1, 8,
            lambda q: send(pb.at[0, 0], ar.at[0, 0], c2_s.at[q], c2_r.at[0], r, 2 * q).start(),
        )
        each(
            0, 8,
            lambda q: send(pb.at[q, 0], ar.at[q, 0], c3_s.at[q], c3_r.at[q], r, 1).start(),
        )

        @pl.when(r > 0)
        def _():
            send(x3.at[r], x3.at[r], x1_s.at[0], x1_r, 0, 0).wait_recv()
            each(1, NC, lambda q: send(x3.at[r], x3.at[r], x2_s.at[q], x2_r, r, q).start())

            def on(q):
                @pl.when(q != r)
                def _():
                    send(x3.at[r], x3.at[r], x3_s.at[q], x3_r.at[r], q, 0).start()

            each(1, NR, on)

    @pl.when(c > 0)
    def _():
        def arrive(a):
            @pl.when(a != c)
            def _():
                send(e1s.at[0], e1r.at[a], e1_s.at[0], e1_r.at[a], r, a).wait_recv()

        each(jnp.maximum(2 * (c - 8), 0), NC, arrive)

        def to_row(d):
            q = lax.rem(r + d, NR)

            @pl.when(q >= h)
            def _():
                for n in range(4):
                    e2s[q, n] = e1r[tab[q] + n]

                @pl.when(q != r)
                def _():
                    send(e2s.at[q], kids.at[r], e2_s.at[q], e2_r.at[r], q, c).start()

                @pl.when(q == r)
                def _():
                    pltpu.make_async_copy(e2s.at[q], kids.at[r], here.at[2]).start()

        each(1, NR + 1, to_row)

        send(ar.at[h, core], ar.at[h, core], c1_s.at[0], c1_r, r, 0).wait_recv()

        def spread(d):
            q = lax.rem(h + d, 8)

            @pl.when((q != 0) | (core != 0))
            def _():
                send(
                    ar.at[h, core], ar.at[h, core], c2_s.at[q], c2_r.at[h], r, 2 * q + core
                ).start()

        each(1, 8, spread)

        def across(q):
            @pl.when(c != 1)
            def _():
                send(ar.at[q, core], ar.at[q, core], c3_s.at[q], c3_r.at[q], r, sibling).start()

        across(h)

        send(x3.at[r], x3.at[r], x2_s.at[0], x2_r, r, 0).wait_recv()
        each(
            1, NR,
            lambda d: send(
                x3.at[r], x3.at[r], x3_s.at[lax.rem(r + d, NR)], x3_r.at[r], lax.rem(r + d, NR), c
            ).start(),
        )

        def collect(d):
            q = lax.rem(h + d, 8)
            send(
                ar.at[q, core], ar.at[q, core], c2_s.at[q], c2_r.at[q], r, 2 * q + core
            ).wait_recv()
            across(q)

        each(1, 8, collect)
        each(
            0, 8,
            lambda q: send(
                ar.at[q, 1 - core], ar.at[q, 1 - core], c3_s.at[q], c3_r.at[q], r, sibling
            ).wait_recv(),
        )

        @pl.when(r == h)
        def _():
            pltpu.make_async_copy(ar.at[pl.ds(4 * core, 4)], ac, here.at[3]).start()

            def scatter(d):
                q = lax.rem(r + d, NR)
                send(
                    ar.at[4 * core + q // 2, lax.rem(q, 2)], ac.at[q // 2, lax.rem(q, 2)],
                    d1_s.at[q], d1_r, q, c,
                ).start()

            each(1, NR, scatter)
            each(
                r + 1, NR,
                lambda q: send(
                    ar.at[4 * core + r // 2, lax.rem(r, 2)], ac.at[r // 2, lax.rem(r, 2)],
                    d2_s.at[q], d2_r.at[r], q, c,
                ).start(),
            )

        @pl.when(r != h)
        def _():
            mine = ac.at[r // 2, lax.rem(r, 2)]
            send(mine, mine, d1_s.at[0], d1_r, h, c).wait_recv()

            def on(q):
                @pl.when(q != r)
                def _():
                    send(mine, mine, d2_s.at[q], d2_r.at[r], q, c).start()

            each(h + 1, NR, on)

        @pl.when(r > h)
        def _():
            def arrive(q):
                @pl.when(q != r)
                def _():
                    at = ac.at[q // 2, lax.rem(q, 2)]
                    send(at, at, d2_s.at[q], d2_r.at[q], q, c).wait_recv()

            each(0, NR, arrive)

        @pl.when(r >= h)
        def _():
            def arrive(q):
                @pl.when(q != r)
                def _():
                    send(e2s.at[0], kids.at[q], e2_s.at[0], e2_r.at[q], q, c).wait_recv()

            each(0, NR, arrive)

    @pl.when((c > 0) | (r > 0))
    def _():
        def arrive(q):
            @pl.when(q != r)
            def _():
                send(x3.at[q], x3.at[q], x3_s.at[q], x3_r.at[q], q, c).wait_recv()

        each(0, NR, arrive)

    def sent(buffer, sem):
        send(buffer, buffer, sem, c1_r, r, sibling).wait_send()

    @pl.when(c < 2)
    def _():
        def left(q):
            @pl.when((q != r) | (c == 1))
            def _():
                sent(bs.at[q], b_s.at[q])

        each(0, NR, left)

    def left_col(q):
        @pl.when((q >= 1) & (q <= h + 8) & (q != c))
        def _():
            sent(e1s.at[q], e1_s.at[q])

    each(0, NC, left_col)

    @pl.when(c == 0)
    def _():
        pltpu.make_async_copy(pf, panel, here.at[0]).wait()

        @pl.when(r == 0)
        def _():
            pltpu.make_async_copy(xs, x3, here.at[1]).wait()
            each(1, NR, lambda q: sent(xs.at[q], x1_s.at[q]))

        each(1, NC, lambda q: sent(pb.at[0, 0], c1_s.at[q]))
        each(1, 8, lambda q: sent(pb.at[0, 0], c2_s.at[q]))
        each(0, 8, lambda q: sent(pb.at[q, 0], c3_s.at[q]))
        each(1, NC, lambda q: sent(xs.at[0], x2_s.at[q]))

        def left(q):
            @pl.when(q != r)
            def _():
                sent(xs.at[0], x3_s.at[q])

        each(1, NR, left)

    @pl.when(c > 0)
    def _():
        def left_row(q):
            @pl.when(q != r)
            def _():
                sent(e2s.at[q], e2_s.at[q])

            @pl.when(q == r)
            def _():
                pltpu.make_async_copy(e2s.at[q], kids.at[r], here.at[2]).wait()

        each(h, NR, left_row)

        def left_spread(q):
            @pl.when((q != h) & ((q != 0) | (core != 0)))
            def _():
                sent(ar.at[0, 0], c2_s.at[q])

        each(0, 8, left_spread)

        @pl.when(c != 1)
        def _():
            each(0, 8, lambda q: sent(ar.at[0, 0], c3_s.at[q]))

        each(1, NR, lambda d: sent(x3.at[0], x3_s.at[lax.rem(r + d, NR)]))

        @pl.when(r == h)
        def _():
            pltpu.make_async_copy(ar.at[pl.ds(4 * core, 4)], ac, here.at[3]).wait()
            each(1, NR, lambda d: sent(ar.at[0, 0], d1_s.at[lax.rem(r + d, NR)]))
            each(r + 1, NR, lambda q: sent(ar.at[0, 0], d2_s.at[q]))

        @pl.when(r != h)
        def _():
            def left(q):
                @pl.when(q != r)
                def _():
                    sent(ac.at[0, 0], d2_s.at[q])

            each(h + 1, NR, left)


def exchange(tab, fm, child, front):
    dma = pltpu.SemaphoreType.DMA
    sds = jax.ShapeDtypeStruct
    return pl.pallas_call(
        exchange_kernel,
        in_specs=[SM, SM, VM, ANY],
        out_specs=[ANY] * 5,
        out_shape=[
            sds((NR, 4, BS, 2 * BS), bf16),
            sds((8, 2, 128, 1024), bf16),
            sds((4, 2, 128, 1024), bf16),
            sds((8, 3, 64, 512), f32),
            sds((8, BS, 1024), f32),
        ],
        scratch_shapes=[
            pltpu.VMEM((16, BS, BS), bf16),
            pltpu.VMEM((16, BS, BS), bf16),
            pltpu.VMEM((NC, BS, 2 * BS), bf16),
            pltpu.VMEM((NC, BS, 2 * BS), bf16),
            pltpu.VMEM((NR, 4, BS, 2 * BS), bf16),
            pltpu.VMEM((NR, 4, BS, BS), bf16),
            pltpu.VMEM((64, BS, BS), bf16),
            pltpu.VMEM((8, BS, 1024), f32),
            pltpu.VMEM((8, 2, 128, 1024), bf16),
            pltpu.VMEM((8, 3, 64, 512), f32),
            dma((NC,)), dma((NC,)), dma((NR,)), dma((NR,)), dma((NR,)), dma((16,)),
            dma((NC,)), dma, dma((8,)), dma((8,)), dma((8,)), dma((8,)),
            dma((NR,)), dma, dma((NR,)), dma((NR,)),
            dma((NR,)), dma, dma((NC,)), dma, dma((NR,)), dma((NR,)), dma((4,)),
        ],
        compiler_params=pltpu.CompilerParams(
            collective_id=1, has_side_effects=True, vmem_limit_bytes=56 << 20
        ),
        cost_estimate=pl.CostEstimate(flops=0, bytes_accessed=400_000_000, transcendentals=0),
        name="exchange",
    )(tab, fm, child, front)


def pivots(fm, x3):
    return pl.pallas_call(
        factor_pivots_kernel,
        in_specs=[SM, VM],
        out_specs=VM,
        out_shape=jax.ShapeDtypeStruct((8, 3, 64, 512), f32),
        scratch_shapes=[
            pltpu.VMEM((512, 1536), f32),
            pltpu.VMEM((128, 256), f32),
            pltpu.VMEM((128, 1536), f32),
        ],
        compiler_params=pltpu.CompilerParams(vmem_limit_bytes=32 << 20),
        name="pivots",
    )(fm, x3)


def factor_pivots_kernel(fm, x_in, x_out, wide, small, r_ref):
    factor_pivots(x_in, x_out, fm, wide, small, r_ref)


def update_kernel(
    tab, fm, front, panel, ar, ac, x3, kids, out, inv0, low, inv1, wc,
):
    r = lax.axis_index("row")
    c = lax.axis_index("col")
    i = pl.program_id(0)
    g = 8 * r + i
    active = g >= 4 * c

    def gather(n, dtype):
        return jnp.concatenate([x3[p, n] for p in range(8)], axis=0).astype(dtype)

    def solve(rows0, rows1, block_row):
        first = dot_t(rows0, inv0[...], None).astype(bf16)
        across = dot(first, low[...], None)
        second = jnp.concatenate(
            [
                rows1[:, BS * j : BS * j + BS].astype(f32)
                - fm[block_row, 2 + j].astype(f32) * across[:, BS * j : BS * j + BS]
                for j in range(2)
            ],
            axis=1,
        ).astype(bf16)
        return first, dot_t(second, inv1[...], None).astype(bf16)

    @pl.when((i == 0) & (c > 0) & (h_of(c) <= r))
    def _():
        inv0[...] = gather(0, bf16)
        low[...] = gather(1, bf16)
        inv1[...] = gather(2, bf16)
        for j in range(4):
            block = jnp.concatenate([ac[j, 0], ac[j, 1]], axis=0)
            first, second = solve(block[:, :512], block[:, 512:], 4 * c + j)
            wc[BS * j : BS * j + BS, :512] = first
            wc[BS * j : BS * j + BS, 512:] = second

    @pl.when(jnp.logical_not(active))
    def _():
        out[...] = jnp.zeros_like(out)

    @pl.when(active & (c == 0))
    def _():
        first = dot_t(panel[0, :, :512], gather(0, f32))
        across = dot(first, gather(1, f32))
        second = jnp.concatenate(
            [
                panel[0, :, 512 + BS * j : 768 + BS * j]
                - fm[g, 2 + j].astype(f32) * across[:, BS * j : BS * j + BS]
                for j in range(2)
            ],
            axis=1,
        )
        second = dot_t(second, gather(2, f32))
        row = g * BS + lax.broadcasted_iota(jnp.int32, (BS, 512), 0)
        lane = lax.broadcasted_iota(jnp.int32, (BS, 512), 1)
        out[:, :512] = jnp.where(row >= lane, first, 0.0)
        out[:, 512:] = jnp.where(row >= lane + 512, second, 0.0)

    @pl.when(active & (c > 0))
    def _():
        block = jnp.concatenate([ar[0, 0], ar[0, 1]], axis=0)
        first, second = solve(block[:, :512], block[:, 512:], g)
        for j in range(4):
            at = pl.ds(BS * j, BS)
            keep = (fm[g, 4 * c + j] != 0) & (g >= 4 * c + j)

            @pl.when(keep)
            def _():
                product = dot_t(first, wc[BS * j : BS * j + BS, :512], None) + dot_t(
                    second, wc[BS * j : BS * j + BS, 512:], None
                )
                times = fm[g, 4 * c + j].astype(f32)
                out[:, at] = (front[:, at] - product) * times

                for k in range(NR):
                    slot = tab[24 + 8 * k + i]
                    side = tab[88 + 4 * k + j]

                    @pl.when(tab[120 + 8 * k + i] * tab[184 + 4 * k + j] > 0)
                    def _():
                        from_col = pl.multiple_of(side * BS, BS)
                        out[:, at] = out[:, at] + times * kids[
                            k, slot, :, pl.ds(from_col, BS)
                        ].astype(f32)

            @pl.when(jnp.logical_not(keep))
            def _():
                out[:, at] = jnp.zeros((BS, BS), f32)


def h_of(c):
    return c // 2


def update(tab, fm, front, panel, ar, ac, x3, kids):
    whole = lambda shape: pl.BlockSpec(
        shape, lambda i: (0,) * len(shape), pipeline_mode=pl.Buffered(1)
    )
    return pl.pallas_call(
        update_kernel,
        grid=(8,),
        in_specs=[
            SM, SM,
            pl.BlockSpec((BS, 1024), lambda i: (i, 0)),
            pl.BlockSpec((1, BS, 1024), lambda i: (i, 0, 0)),
            pl.BlockSpec((1, 2, 128, 1024), lambda i: (i, 0, 0, 0)),
            whole((4, 2, 128, 1024)),
            whole((8, 3, 64, 512)),
            whole((NR, 4, BS, 2 * BS)),
        ],
        out_specs=pl.BlockSpec((BS, 1024), lambda i: (i, 0)),
        out_shape=jax.ShapeDtypeStruct((2048, 1024), f32),
        scratch_shapes=[
            pltpu.VMEM((512, 512), bf16),
            pltpu.VMEM((512, 512), bf16),
            pltpu.VMEM((512, 512), bf16),
            pltpu.VMEM((1024, 1024), bf16),
        ],
        compiler_params=pltpu.CompilerParams(vmem_limit_bytes=48 << 20),
        name="update",
    )(tab, fm, front, panel, ar, ac, x3, kids)


def tables(maps, r, c):
    own = lax.dynamic_index_in_dim(maps, r, 0, keepdims=False)
    row_start = jnp.minimum(jnp.sum(own[:, None] < 8 * jnp.arange(NR), axis=0), 12)
    col_start = jnp.minimum(jnp.sum(own[:, None] < 4 * jnp.arange(NC), axis=0), 14)
    index = jnp.arange(16)
    rows = maps[:, None, :] == 8 * r + jnp.arange(8)[None, :, None]
    row_first = jnp.minimum(jnp.sum(maps < 8 * r, axis=1), 12)
    row_slot = jnp.sum(rows * (index - row_first[:, None, None] + 1), axis=-1) - 1
    cols = maps[:, None, :] == 4 * c + jnp.arange(4)[None, :, None]
    col_first = jnp.minimum(jnp.sum(maps < 4 * c, axis=1), 14)
    col_slot = jnp.sum(cols * (index - col_first[:, None, None] + 1), axis=-1) - 1
    parts = [
        row_start,
        col_start,
        jnp.maximum(row_slot, 0).reshape(-1),
        jnp.maximum(col_slot, 0).reshape(-1),
        (row_slot >= 0).reshape(-1),
        (col_slot >= 0).reshape(-1),
    ]
    parts = [part.astype(jnp.int32) for part in parts]
    return jnp.concatenate(parts)


def local(front, child_updates, child_maps, fill_mask):
    r = lax.axis_index("row")
    c = lax.axis_index("col")
    tab = tables(child_maps, r, c)
    kids, ar, ac, x3, panel = exchange(
        tab, fill_mask, child_updates[0], front.reshape(8, BS, 1024)
    )
    x3 = pivots(fill_mask, x3)
    return update(tab, fill_mask, front, panel, ar, ac, x3, kids)


def solution(mesh):
    placed = (P("row", "col"), P("row", "col", None), P(), P())
    return jax.shard_map(
        local, mesh=mesh, in_specs=placed, out_specs=P("row", "col"), check_vma=False
    )
```

```python
import functools

import jax
import jax.numpy as jnp
from jax import lax
from jax.experimental import pallas as pl
from jax.experimental.pallas import tpu as pltpu
from jax.sharding import PartitionSpec as P

BS = 256
NR = 8
NC = 16
MESH = pl.DeviceIdType.MESH
HI = lax.Precision.HIGHEST
f32 = jnp.float32
bf16 = jnp.bfloat16
ANY = pl.BlockSpec(memory_space=pl.ANY)
VM = pl.BlockSpec(memory_space=pltpu.VMEM)
SM = pl.BlockSpec(memory_space=pltpu.SMEM)


def dot(a, b, precision=HI):
    return lax.dot_general(
        a, b, (((1,), (0,)), ((), ())), precision=precision, preferred_element_type=f32
    )


def dot_t(a, b, precision=HI):
    return lax.dot_general(
        a, b, (((1,), (1,)), ((), ())), precision=precision, preferred_element_type=f32
    )


def t_dot(a, b, precision=HI):
    return lax.dot_general(
        a, b, (((0,), (0,)), ((), ())), precision=precision, preferred_element_type=f32
    )


def row_of(x, k):
    return jnp.broadcast_to(x[k : k + 1, :], (8, 128))


def lane_of(x, k):
    return jnp.broadcast_to(x[:, k : k + 1], (8, 128))


def factor_128(m_ref, ahead=3):
    sub = lax.broadcasted_iota(jnp.int32, (8, 128), 0)
    lane = lax.broadcasted_iota(jnp.int32, (8, 128), 1)
    held = {}
    for s in range(16):
        last = min(s + ahead + 1, 16)
        for q in range(s, last):
            if q not in held:
                held[q] = (m_ref[8 * q : 8 * q + 8, :128], m_ref[8 * q : 8 * q + 8, 128:])
        left, right = held.pop(s)
        v = [lane_of(left, 8 * s + j) for j in range(8)]
        z = [jnp.where(sub == j, 1.0, 0.0).astype(f32) for j in range(8)]
        scale = jnp.zeros((8, 128), f32)
        rows, inverses = [], []
        for k in range(8):
            root = lax.rsqrt(row_of(v[k], k))
            scale = jnp.where(sub == k, root, scale)
            inverse = root * root
            inverses.append(inverse)
            below = jnp.where(sub > k, v[k], 0.0) * inverse
            row = {}
            for j in range(k + 1, 8):
                row[j] = row_of(v[j], k)
                v[j] = v[j] - below * row[j]
            rows.append(row)
            if k < 7:
                for j in range(k + 1):
                    z[j] = z[j] - below * row_of(z[j], k)
        new_left = z[0] * row_of(left, 0)
        new_right = z[0] * row_of(right, 0)
        for j in range(1, 8):
            new_left = new_left + z[j] * row_of(left, j)
            new_right = new_right + z[j] * row_of(right, j)
        new_left = jnp.where(lane >= 8 * s + sub, new_left, 0.0)
        rows_left = [row_of(new_left, k) for k in range(8)]
        rows_right = [row_of(new_right, k) for k in range(8)]
        for q in range(s + 1, last):
            x, y = held[q]
            w = [lane_of(x, 8 * s + j) for j in range(8)]
            for k in range(8):
                times = w[k] * inverses[k]
                for j in range(k + 1, 8):
                    w[j] = w[j] - times * rows[k][j]
                x = x - times * rows_left[k]
                y = y - times * rows_right[k]
            held[q] = (x, y)
        new_left = new_left * scale
        new_right = new_right * scale
        m_ref[8 * s : 8 * s + 8, :128] = new_left
        m_ref[8 * s : 8 * s + 8, 128:] = new_right
        low = 8 * last
        if low < 128:
            update = t_dot(new_left, jnp.concatenate([new_left, new_right], axis=1))
            m_ref[low:, :] = m_ref[low:, :] - update[low:, :]


def identity(count, dtype=f32):
    row = lax.broadcasted_iota(jnp.int32, (count, count), 0)
    lane = lax.broadcasted_iota(jnp.int32, (count, count), 1)
    return jnp.where(row == lane, 1.0, 0.0).astype(dtype)


def eliminate(wide, small, r_ref, width):
    def step(p, carry):
        at = pl.multiple_of(p * 128, 128)
        small[:, :128] = wide[pl.ds(at, 128), pl.ds(at, 128)]
        small[:, 128:] = identity(128)
        factor_128(small)
        r_ref[:, :width] = dot(small[:, 128:], wide[pl.ds(at, 128), :width])
        wide[pl.ds(at, 128), :width] = r_ref[:, :width]

        def trail(q, carry):
            down = pl.multiple_of(q * 128, 128)
            wide[pl.ds(down, 128), :width] = wide[pl.ds(down, 128), :width] - t_dot(
                r_ref[:, pl.ds(down, 128)], r_ref[:, :width]
            )
            return carry

        lax.fori_loop(p + 1, 4, trail, 0)
        return carry

    lax.fori_loop(0, 4, step, 0)


def first_pivot(x3, wide, small, r_ref):
    for p in range(8):
        wide[64 * p : 64 * p + 64, 0:512] = x3[p, 0]
        wide[64 * p : 64 * p + 64, 512:1024] = x3[p, 1]
    wide[:, 1024:] = identity(512)
    eliminate(wide, small, r_ref, 1536)
    for p in range(8):
        x3[p, 0] = wide[64 * p : 64 * p + 64, 1024:]
        x3[p, 1] = wide[64 * p : 64 * p + 64, 512:1024]


def second_matrix(x3, fm, wide):
    u = wide[:, 512:1024]
    for i in range(2):
        product = t_dot(u[:, 256 * i : 256 * i + 256], u)
        for j in range(2):
            keep = fm[2 + i, 2 + j].astype(f32)
            for p in range(4):
                wide[256 * i + 64 * p : 256 * i + 64 * p + 64, 256 * j : 256 * j + 256] = (
                    x3[4 * i + p, 2, :, 256 * j : 256 * j + 256]
                    - keep * product[64 * p : 64 * p + 64, 256 * j : 256 * j + 256]
                )
    wide[:, 512:1024] = identity(512)


def second_pivot(x3, wide, small, r_ref):
    eliminate(wide, small, r_ref, 1024)
    for p in range(8):
        x3[p, 2] = wide[64 * p : 64 * p + 64, 512:1024]


def exchange_kernel(
    tab, fm, child, front, kids, ar_out, ac_out, xb_out, x3_out, panel,
    blocks, turned, e1s, e1r, wide_kids, bs, pf, ar, ac, x3, xb, wide, small, r_ref,
    k_s, k_r, e1_s, e1_r, e2_s, e2_r, b_s, b_r, c1_s, c1_r, c2_s, c2_r, c3_s, c3_r,
    d1_s, d1_r, d2_s, d2_r, x1_s, x1_r, x2_s, x2_r, x3_s, x3_r, here,
):
    r = lax.axis_index("row")
    c = lax.axis_index("col")
    h = c // 2
    core = lax.rem(c, 2)
    sibling = c + 1 - 2 * core
    root = (r == 0) & (c == 0)
    barrier = pltpu.get_barrier_semaphore()

    def send(src, dst, ss, rs, row, col):
        return pltpu.make_async_remote_copy(
            src_ref=src, dst_ref=dst, send_sem=ss, recv_sem=rs,
            device_id=(row, col), device_id_type=MESH,
        )

    def move(src, dst, n):
        return pltpu.make_async_copy(src, dst, here.at[n])

    def each(low, high, body):
        def run(i, carry):
            body(i)
            return carry

        lax.fori_loop(low, high, run, 0)

    def when(condition, body):
        pl.when(condition)(body)

    def greet(row, col):
        pl.semaphore_signal(barrier, inc=1, device_id=(row, col), device_id_type=MESH)

    each(1, NR, lambda d: greet(lax.rem(r + d, NR), c))
    each(1, NC, lambda d: greet(r, lax.rem(c + d, NC)))

    @pl.when(c < 2)
    def _():
        each(1, NR, lambda d: greet(lax.rem(r + d, NR), 1 - c))

    @pl.when(c == 0)
    def _():
        move(front.at[pl.ds(0, 4)], pf.at[pl.ds(0, 4)], 0).start()
        move(front.at[pl.ds(4, 4)], pf.at[pl.ds(4, 4)], 3).start()

    for a in range(16):
        blocks[a] = child[:, BS * a : BS * a + BS]

    def turn(a):
        turned[a] = dot_t(identity(BS, bf16), blocks[a], None).astype(bf16)

    when(c < 2, lambda: each(0, 16, turn))
    pl.semaphore_wait(barrier, jnp.where(c < 2, 29, 22))

    @pl.when((c < 2) & jnp.logical_not(root))
    def _():
        send(turned.at[pl.ds(0, 2)], e1r.at[2 * r + c], k_s, k_r.at[2 * r + c], 0, 0).start()

    @pl.when(root)
    def _():
        for n in range(2):
            e1r[0, n] = turned[n]

    @pl.when(c < 2)
    def _():
        def give(d):
            q = lax.rem(r + d, NR)
            for n in range(4):
                bs[q, n] = turned[tab[q] + n]

            @pl.when((q != r) | (c == 1))
            def _():
                send(
                    bs.at[q], wide_kids.at[pl.ds(8 * r + 4 * c, 4)],
                    b_s.at[q], b_r.at[2 * r + c], q, 0,
                ).start()

            @pl.when((q == r) & (c == 0))
            def _():
                for n in range(4):
                    wide_kids[8 * r + n] = bs[q, n]

        each(1, NR + 1, give)

    def to_col(d):
        q = lax.rem(c + d, NC)

        @pl.when((q >= 1) & (q <= h + 8))
        def _():
            @pl.when(q != c)
            def _():
                for n in range(2):
                    e1s[q, n] = blocks[tab[8 + q] + n]
                send(e1s.at[q], e1r.at[c], e1_s.at[q], e1_r.at[c], r, q).start()

            @pl.when(q == c)
            def _():
                for n in range(2):
                    e1r[c, n] = blocks[tab[8 + q] + n]

    each(1, NC + 1, to_col)

    def assemble_panel():
        move(front.at[pl.ds(0, 4)], pf.at[pl.ds(0, 4)], 3).wait()

        def arrive(k):
            @pl.when(k != 2 * r)
            def _():
                send(
                    bs.at[0], wide_kids.at[pl.ds(4 * k, 4)],
                    b_s.at[0], b_r.at[k], k // 2, lax.rem(k, 2),
                ).wait_recv()

        each(0, 16, arrive)

        def assemble(i):
            def add(k):
                for j in range(4):
                    times = (tab[120 + 8 * k + i] * tab[184 + 4 * k + j]).astype(f32)
                    block = wide_kids[8 * k + 4 * tab[88 + 4 * k + j] + tab[24 + 8 * k + i]]
                    at = pl.ds(j * BS, BS)
                    pf[i, :, at] = pf[i, :, at] + times * block.astype(f32)

            each(0, NR, add)
            for j in range(4):
                at = pl.ds(j * BS, BS)
                kept = pf[i, :, at] * fm[8 * r + i, j].astype(f32)
                pf[i, :, at] = kept
                ar[i, 0, :, at] = kept[:128].astype(bf16)
                ar[i, 1, :, at] = kept[128:].astype(bf16)

        each(0, 8, assemble)
        move(pf, panel, 0).start()

    @pl.when(root)
    def _():
        move(front.at[pl.ds(0, 4)], pf.at[pl.ds(0, 4)], 0).wait()
        each(1, 16, lambda k: send(
            turned.at[pl.ds(0, 2)], e1r.at[k], k_s, k_r.at[k], k // 2, lax.rem(k, 2)
        ).wait_recv())
        for n, rows, cols in ((0, 0, 0), (1, 0, 2), (2, 2, 2)):
            for i in range(2):
                for j in range(2):
                    for p in range(4):
                        x3[4 * i + p, n, :, BS * j : BS * j + BS] = pf[
                            rows + i, 64 * p : 64 * p + 64,
                            BS * (cols + j) : BS * (cols + j) + BS,
                        ]

                    def add(k):
                        times = (
                            tab[120 + 8 * k + rows + i] * tab[184 + 4 * k + cols + j]
                        ).astype(f32)
                        block = e1r[
                            2 * k + tab[88 + 4 * k + cols + j], tab[24 + 8 * k + rows + i]
                        ].astype(f32) * times
                        for p in range(4):
                            at = pl.ds(BS * j, BS)
                            x3[4 * i + p, n, :, at] = (
                                x3[4 * i + p, n, :, at] + block[64 * p : 64 * p + 64]
                            )

                    each(0, NR, add)
                    keep = fm[rows + i, cols + j].astype(f32)
                    for p in range(4):
                        at = pl.ds(BS * j, BS)
                        x3[4 * i + p, n, :, at] = x3[4 * i + p, n, :, at] * keep
        first_pivot(x3, wide, small, r_ref)
        second_matrix(x3, fm, wide)
        assemble_panel()
        send(ar, ar, c1_s.at[1], c1_r, 0, 1).start()
        second_pivot(x3, wide, small, r_ref)
        each(1, NR, lambda q: send(x3.at[q], x3.at[q], x1_s.at[q], x1_r, q, 0).start())

    @pl.when((c == 0) & (r > 0))
    def _():
        move(front.at[pl.ds(0, 4)], pf.at[pl.ds(0, 4)], 0).wait()
        assemble_panel()
        each(1, NC, lambda q: send(
            ar.at[q // 2, lax.rem(q, 2)], ar.at[q // 2, lax.rem(q, 2)], c1_s.at[q], c1_r, r, q
        ).start())
        each(1, 8, lambda q: send(
            ar.at[0, 0], ar.at[0, 0], c2_s.at[q], c2_r.at[0], r, 2 * q
        ).start())
        each(0, 8, lambda q: send(
            ar.at[q, 0], ar.at[q, 0], c3_s.at[q], c3_r.at[q], r, 1
        ).start())
        send(x3.at[r], x3.at[r], x1_s.at[0], x1_r, 0, 0).wait_recv()

    @pl.when(c == 0)
    def _():
        xb[r] = x3[r].astype(bf16)
        each(1, NC, lambda q: send(xb.at[r], xb.at[r], x2_s.at[q], x2_r, r, q).start())

        def on(q):
            @pl.when(q != r)
            def _():
                send(x3.at[r], x3.at[r], x3_s.at[q], x3_r.at[r], q, 0).start()

        each(1, NR, on)

    @pl.when(c > 0)
    def _():
        def arrive(a):
            @pl.when(a != c)
            def _():
                send(e1s.at[0], e1r.at[a], e1_s.at[0], e1_r.at[a], r, a).wait_recv()

        each(jnp.maximum(2 * (c - 8), 0), NC, arrive)

        def to_row(d):
            q = lax.rem(r + ORDER(d), NR)

            @pl.when(q >= h)
            def _():
                for n in range(4):
                    for m in range(2):
                        wide_kids[8 * q + 4 * m + n] = e1r[tab[q] + n, m]

                @pl.when(q != r)
                def _():
                    send(
                        wide_kids.at[pl.ds(8 * q, 8)], kids.at[r], e2_s.at[q], e2_r.at[r], q, c
                    ).start()

                @pl.when(q == r)
                def _():
                    move(wide_kids.at[pl.ds(8 * q, 8)], kids.at[r], 2).start()

        each(1, NR + 1, to_row)

    @pl.when((r == 0) & (c == 1))
    def _():
        send(ar, ar, c1_s.at[0], c1_r, 0, 0).wait_recv()

    def across(q):
        @pl.when(c != 1)
        def _():
            send(ar.at[q, core], ar.at[q, core], c3_s.at[q], c3_r.at[q], r, sibling).start()

    @pl.when((c > 0) & (r > 0))
    def _():
        send(ar.at[h, core], ar.at[h, core], c1_s.at[0], c1_r, r, 0).wait_recv()

        def spread(d):
            q = lax.rem(h + d, 8)

            @pl.when((q != 0) | (core != 0))
            def _():
                send(
                    ar.at[h, core], ar.at[h, core], c2_s.at[q], c2_r.at[h], r, 2 * q + core
                ).start()

        each(1, 8, spread)
        across(h)

        def collect(d):
            q = lax.rem(h + d, 8)
            send(
                ar.at[q, core], ar.at[q, core], c2_s.at[q], c2_r.at[q], r, 2 * q + core
            ).wait_recv()
            across(q)

        each(1, 8, collect)
        each(0, 8, lambda q: send(
            ar.at[q, 1 - core], ar.at[q, 1 - core], c3_s.at[q], c3_r.at[q], r, sibling
        ).wait_recv())

    @pl.when(c > 0)
    def _():
        @pl.when(r >= h)
        def _():
            move(ar, ar_out, 3).start()

        @pl.when(r == h)
        def _():
            move(ar.at[pl.ds(4 * core, 4)], ac_out, 4).start()

            def scatter(d):
                q = lax.rem(r + d, NR)
                send(
                    ar.at[4 * core + q // 2, lax.rem(q, 2)], ac.at[q // 2, lax.rem(q, 2)],
                    d1_s.at[q], d1_r, q, c,
                ).start()

            each(1, NR, scatter)
            each(r + 1, NR, lambda q: send(
                ar.at[4 * core + r // 2, lax.rem(r, 2)], ac.at[r // 2, lax.rem(r, 2)],
                d2_s.at[q], d2_r.at[r], q, c,
            ).start())

        @pl.when(r != h)
        def _():
            mine = ac.at[r // 2, lax.rem(r, 2)]
            send(mine, mine, d1_s.at[0], d1_r, h, c).wait_recv()

            def on(q):
                @pl.when(q != r)
                def _():
                    send(mine, mine, d2_s.at[q], d2_r.at[r], q, c).start()

            each(h + 1, NR, on)

        send(xb.at[r], xb.at[r], x2_s.at[0], x2_r, r, 0).wait_recv()
        each(1, NR, lambda d: send(
            xb.at[r], xb.at[r], x3_s.at[lax.rem(r + d, NR)], x3_r.at[r], lax.rem(r + d, NR), c
        ).start())

        @pl.when(r > h)
        def _():
            def arrive(q):
                @pl.when(q != r)
                def _():
                    at = ac.at[q // 2, lax.rem(q, 2)]
                    send(at, at, d2_s.at[q], d2_r.at[q], q, c).wait_recv()

            each(0, NR, arrive)
            move(ac, ac_out, 4).start()

        @pl.when(r >= h)
        def _():
            def arrive(q):
                @pl.when(q != r)
                def _():
                    send(
                        wide_kids.at[pl.ds(0, 8)], kids.at[q], e2_s.at[0], e2_r.at[q], q, c
                    ).wait_recv()

            each(0, NR, arrive)

        def pieces(q):
            @pl.when(q != r)
            def _():
                send(xb.at[q], xb.at[q], x3_s.at[q], x3_r.at[q], q, c).wait_recv()

        each(0, NR, pieces)
        move(xb, xb_out, 1).start()

    @pl.when(c == 0)
    def _():
        def pieces(q):
            @pl.when((q != r) & (r > 0))
            def _():
                send(x3.at[q], x3.at[q], x3_s.at[q], x3_r.at[q], q, c).wait_recv()

        each(0, NR, pieces)
        move(x3, x3_out, 1).start()

    def sent(buffer, sem):
        send(buffer, buffer, sem, c1_r, r, sibling).wait_send()

    def unless(condition, body):
        pl.when(jnp.logical_not(condition))(body)

    @pl.when(c < 2)
    def _():
        unless(root, lambda: sent(turned.at[pl.ds(0, 2)], k_s))
        each(0, NR, lambda q: when(
            (q != r) | (c == 1), lambda: sent(bs.at[q], b_s.at[q])
        ))

    each(1, NC, lambda q: when(
        (q <= h + 8) & (q != c), lambda: sent(e1s.at[q], e1_s.at[q])
    ))

    @pl.when(c == 0)
    def _():
        move(pf, panel, 0).wait()
        move(x3, x3_out, 1).wait()

        @pl.when(r == 0)
        def _():
            sent(ar, c1_s.at[1])
            each(1, NR, lambda q: sent(x3.at[q], x1_s.at[q]))

        @pl.when(r > 0)
        def _():
            each(1, NC, lambda q: sent(ar.at[0, 0], c1_s.at[q]))
            each(1, 8, lambda q: sent(ar.at[0, 0], c2_s.at[q]))
            each(0, 8, lambda q: sent(ar.at[q, 0], c3_s.at[q]))

        each(1, NC, lambda q: sent(xb.at[0], x2_s.at[q]))
        each(1, NR, lambda q: when(q != r, lambda: sent(x3.at[0], x3_s.at[q])))

    @pl.when(c > 0)
    def _():
        def left_row(q):
            when(q != r, lambda: sent(wide_kids.at[pl.ds(8 * q, 8)], e2_s.at[q]))
            when(q == r, lambda: move(wide_kids.at[pl.ds(8 * q, 8)], kids.at[r], 2).wait())

        each(h, NR, left_row)

        @pl.when(r > 0)
        def _():
            each(0, 8, lambda q: when(
                (q != h) & ((q != 0) | (core != 0)), lambda: sent(ar.at[0, 0], c2_s.at[q])
            ))
            when(c != 1, lambda: each(0, 8, lambda q: sent(ar.at[0, 0], c3_s.at[q])))

        each(1, NR, lambda d: sent(xb.at[0], x3_s.at[lax.rem(r + d, NR)]))
        move(xb, xb_out, 1).wait()

        @pl.when(r >= h)
        def _():
            move(ar, ar_out, 3).wait()
            move(ac, ac_out, 4).wait()

        @pl.when(r == h)
        def _():
            each(1, NR, lambda d: sent(ar.at[0, 0], d1_s.at[lax.rem(r + d, NR)]))
            each(r + 1, NR, lambda q: sent(ar.at[0, 0], d2_s.at[q]))

        when(r != h, lambda: each(h + 1, NR, lambda q: when(
            q != r, lambda: sent(ac.at[0, 0], d2_s.at[q])
        )))


def ORDER(d):
    return d


def exchange(tab, fm, child, front):
    dma = pltpu.SemaphoreType.DMA
    sds = jax.ShapeDtypeStruct
    return pl.pallas_call(
        exchange_kernel,
        in_specs=[SM, SM, VM, ANY],
        out_specs=[ANY] * 6,
        out_shape=[
            sds((NR, 8, BS, BS), bf16),
            sds((8, 2, 128, 1024), bf16),
            sds((4, 2, 128, 1024), bf16),
            sds((8, 3, 64, 512), bf16),
            sds((8, 3, 64, 512), f32),
            sds((8, BS, 1024), f32),
        ],
        scratch_shapes=[
            pltpu.VMEM((16, BS, BS), bf16),
            pltpu.VMEM((16, BS, BS), bf16),
            pltpu.VMEM((NC, 2, BS, BS), bf16),
            pltpu.VMEM((NC, 2, BS, BS), bf16),
            pltpu.VMEM((64, BS, BS), bf16),
            pltpu.VMEM((NR, 4, BS, BS), bf16),
            pltpu.VMEM((8, BS, 1024), f32),
            pltpu.VMEM((8, 2, 128, 1024), bf16),
            pltpu.VMEM((4, 2, 128, 1024), bf16),
            pltpu.VMEM((8, 3, 64, 512), f32),
            pltpu.VMEM((8, 3, 64, 512), bf16),
            pltpu.VMEM((512, 1536), f32),
            pltpu.VMEM((128, 256), f32),
            pltpu.VMEM((128, 1536), f32),
            dma, dma((16,)),
            dma((NC,)), dma((NC,)), dma((NR,)), dma((NR,)), dma((NR,)), dma((16,)),
            dma((NC,)), dma, dma((8,)), dma((8,)), dma((8,)), dma((8,)),
            dma((NR,)), dma, dma((NR,)), dma((NR,)),
            dma((NR,)), dma, dma((NC,)), dma, dma((NR,)), dma((NR,)), dma((5,)),
        ],
        compiler_params=pltpu.CompilerParams(
            collective_id=1, has_side_effects=True, vmem_limit_bytes=56 << 20
        ),
        cost_estimate=pl.CostEstimate(flops=0, bytes_accessed=400_000_000, transcendentals=0),
        name="exchange",
    )(tab, fm, child, front)


def split(x):
    high = x.astype(bf16)
    return high, (x - high.astype(f32)).astype(bf16)


def update_kernel(
    tab, fm, front, panel, ar, ac, xb, x3, kids, out, inv0, low, inv1, low0, low1, low2, wc,
):
    r = lax.axis_index("row")
    c = lax.axis_index("col")
    i = pl.program_id(0)
    g = 8 * r + i
    active = g >= 4 * c

    def gather(ref, n):
        return jnp.concatenate([ref[p, n] for p in range(8)], axis=0)

    def solve(rows0, rows1, block_row):
        first = dot_t(rows0, inv0[...], None).astype(bf16)
        across = dot(first, low[...], None)
        second = jnp.concatenate(
            [
                rows1[:, BS * j : BS * j + BS].astype(f32)
                - fm[block_row, 2 + j].astype(f32) * across[:, BS * j : BS * j + BS]
                for j in range(2)
            ],
            axis=1,
        ).astype(bf16)
        return first, dot_t(second, inv1[...], None).astype(bf16)

    def thrice(product, x, high, rest):
        a, b = split(x)
        return (
            product(a, high[...], None) + product(a, rest[...], None) + product(b, high[...], None)
        )

    @pl.when((i == 0) & (c > 0) & (c // 2 <= r))
    def _():
        inv0[...] = gather(xb, 0)
        low[...] = gather(xb, 1)
        inv1[...] = gather(xb, 2)
        for j in range(4):
            block = jnp.concatenate([ac[j, 0], ac[j, 1]], axis=0)
            first, second = solve(block[:, :512], block[:, 512:], 4 * c + j)
            wc[BS * j : BS * j + BS, :512] = first
            wc[BS * j : BS * j + BS, 512:] = second

    @pl.when((i == 0) & (c == 0))
    def _():
        for n, (high, rest) in enumerate(((inv0, low0), (low, low1), (inv1, low2))):
            high[...], rest[...] = split(gather(x3, n))

    @pl.when(jnp.logical_not(active))
    def _():
        out[...] = jnp.zeros_like(out)

    @pl.when(active & (c == 0))
    def _():
        first = thrice(dot_t, panel[0, :, :512], inv0, low0)
        across = thrice(dot, first, low, low1)
        second = jnp.concatenate(
            [
                panel[0, :, 512 + BS * j : 768 + BS * j]
                - fm[g, 2 + j].astype(f32) * across[:, BS * j : BS * j + BS]
                for j in range(2)
            ],
            axis=1,
        )
        second = thrice(dot_t, second, inv1, low2)
        row = g * BS + lax.broadcasted_iota(jnp.int32, (BS, 512), 0)
        lane = lax.broadcasted_iota(jnp.int32, (BS, 512), 1)
        out[:, :512] = jnp.where(row >= lane, first, 0.0)
        out[:, 512:] = jnp.where(row >= lane + 512, second, 0.0)

    @pl.when(active & (c > 0))
    def _():
        block = jnp.concatenate([ar[0, 0], ar[0, 1]], axis=0)
        first, second = solve(block[:, :512], block[:, 512:], g)
        for j in range(4):
            at = pl.ds(BS * j, BS)
            keep = (fm[g, 4 * c + j] != 0) & (g >= 4 * c + j)

            @pl.when(keep)
            def _():
                product = dot_t(first, wc[BS * j : BS * j + BS, :512], None) + dot_t(
                    second, wc[BS * j : BS * j + BS, 512:], None
                )
                times = fm[g, 4 * c + j].astype(f32)
                out[:, at] = (front[:, at] - product) * times

                for k in range(NR):
                    slot = tab[24 + 8 * k + i]
                    side = tab[88 + 4 * k + j]

                    @pl.when(tab[120 + 8 * k + i] * tab[184 + 4 * k + j] > 0)
                    def _():
                        out[:, at] = out[:, at] + times * kids[k, 4 * side + slot].astype(f32)

            @pl.when(jnp.logical_not(keep))
            def _():
                out[:, at] = jnp.zeros((BS, BS), f32)


def update(tab, fm, front, panel, ar, ac, xb, x3, kids):
    whole = lambda shape: pl.BlockSpec(
        shape, lambda i: (0,) * len(shape), pipeline_mode=pl.Buffered(1)
    )
    return pl.pallas_call(
        update_kernel,
        grid=(8,),
        in_specs=[
            SM, SM,
            pl.BlockSpec((BS, 1024), lambda i: (i, 0)),
            pl.BlockSpec((1, BS, 1024), lambda i: (i, 0, 0)),
            pl.BlockSpec((1, 2, 128, 1024), lambda i: (i, 0, 0, 0)),
            whole((4, 2, 128, 1024)),
            whole((8, 3, 64, 512)),
            whole((8, 3, 64, 512)),
            whole((NR, 8, BS, BS)),
        ],
        out_specs=pl.BlockSpec((BS, 1024), lambda i: (i, 0)),
        out_shape=jax.ShapeDtypeStruct((2048, 1024), f32),
        scratch_shapes=[pltpu.VMEM((512, 512), bf16)] * 6 + [pltpu.VMEM((1024, 1024), bf16)],
        compiler_params=pltpu.CompilerParams(vmem_limit_bytes=48 << 20),
        name="update",
    )(tab, fm, front, panel, ar, ac, xb, x3, kids)


def tables(maps, r, c):
    own = lax.dynamic_index_in_dim(maps, r, 0, keepdims=False)
    row_start = jnp.minimum(jnp.sum(own[:, None] < 8 * jnp.arange(NR), axis=0), 12)
    col_start = jnp.minimum(jnp.sum(own[:, None] < 4 * jnp.arange(NC), axis=0), 14)
    index = jnp.arange(16)
    rows = maps[:, None, :] == 8 * r + jnp.arange(8)[None, :, None]
    row_first = jnp.minimum(jnp.sum(maps < 8 * r, axis=1), 12)
    row_slot = jnp.sum(rows * (index - row_first[:, None, None] + 1), axis=-1) - 1
    cols = maps[:, None, :] == 4 * c + jnp.arange(4)[None, :, None]
    col_first = jnp.minimum(jnp.sum(maps < 4 * c, axis=1), 14)
    col_slot = jnp.sum(cols * (index - col_first[:, None, None] + 1), axis=-1) - 1
    parts = [
        row_start,
        col_start,
        jnp.maximum(row_slot, 0).reshape(-1),
        jnp.maximum(col_slot, 0).reshape(-1),
        (row_slot >= 0).reshape(-1),
        (col_slot >= 0).reshape(-1),
    ]
    return jnp.concatenate([part.astype(jnp.int32) for part in parts])


def local(front, child_updates, child_maps, fill_mask):
    r = lax.axis_index("row")
    c = lax.axis_index("col")
    tab = tables(child_maps, r, c)
    kids, ar, ac, xb, x3, panel = exchange(
        tab, fill_mask, child_updates[0], front.reshape(8, BS, 1024)
    )
    return update(tab, fill_mask, front, panel, ar, ac, xb, x3, kids)


def solution(mesh):
    placed = (P("row", "col"), P("row", "col", None), P(), P())
    return jax.shard_map(
        local, mesh=mesh, in_specs=placed, out_specs=P("row", "col"), check_vma=False
    )
```

```python
import functools

import jax
import jax.numpy as jnp
from jax import lax
from jax.experimental import pallas as pl
from jax.experimental.pallas import tpu as pltpu
from jax.sharding import PartitionSpec as P

BS = 256
NR = 8
NC = 16
MESH = pl.DeviceIdType.MESH
HI = lax.Precision.HIGHEST
f32 = jnp.float32
bf16 = jnp.bfloat16
ANY = pl.BlockSpec(memory_space=pl.ANY)
VM = pl.BlockSpec(memory_space=pltpu.VMEM)
SM = pl.BlockSpec(memory_space=pltpu.SMEM)


def dot(a, b, precision=HI):
    return lax.dot_general(
        a, b, (((1,), (0,)), ((), ())), precision=precision, preferred_element_type=f32
    )


def dot_t(a, b, precision=HI):
    return lax.dot_general(
        a, b, (((1,), (1,)), ((), ())), precision=precision, preferred_element_type=f32
    )


def t_dot(a, b, precision=HI):
    return lax.dot_general(
        a, b, (((0,), (0,)), ((), ())), precision=precision, preferred_element_type=f32
    )


def row_of(x, k):
    return jnp.broadcast_to(x[k : k + 1, :], (8, 128))


def lane_of(x, k):
    return jnp.broadcast_to(x[:, k : k + 1], (8, 128))


def factor_128(m_ref, ahead=3):
    sub = lax.broadcasted_iota(jnp.int32, (8, 128), 0)
    lane = lax.broadcasted_iota(jnp.int32, (8, 128), 1)
    held = {}
    for s in range(16):
        last = min(s + ahead + 1, 16)
        for q in range(s, last):
            if q not in held:
                held[q] = (m_ref[8 * q : 8 * q + 8, :128], m_ref[8 * q : 8 * q + 8, 128:])
        left, right = held.pop(s)
        v = [lane_of(left, 8 * s + j) for j in range(8)]
        z = [jnp.where(sub == j, 1.0, 0.0).astype(f32) for j in range(8)]
        scale = jnp.zeros((8, 128), f32)
        rows, inverses = [], []
        for k in range(8):
            root = lax.rsqrt(row_of(v[k], k))
            scale = jnp.where(sub == k, root, scale)
            inverse = root * root
            inverses.append(inverse)
            below = jnp.where(sub > k, v[k], 0.0) * inverse
            row = {}
            for j in range(k + 1, 8):
                row[j] = row_of(v[j], k)
                v[j] = v[j] - below * row[j]
            rows.append(row)
            if k < 7:
                for j in range(k + 1):
                    z[j] = z[j] - below * row_of(z[j], k)
        new_left = z[0] * row_of(left, 0)
        new_right = z[0] * row_of(right, 0)
        for j in range(1, 8):
            new_left = new_left + z[j] * row_of(left, j)
            new_right = new_right + z[j] * row_of(right, j)
        new_left = jnp.where(lane >= 8 * s + sub, new_left, 0.0)
        rows_left = [row_of(new_left, k) for k in range(8)]
        rows_right = [row_of(new_right, k) for k in range(8)]
        for q in range(s + 1, last):
            x, y = held[q]
            w = [lane_of(x, 8 * s + j) for j in range(8)]
            for k in range(8):
                times = w[k] * inverses[k]
                for j in range(k + 1, 8):
                    w[j] = w[j] - times * rows[k][j]
                x = x - times * rows_left[k]
                y = y - times * rows_right[k]
            held[q] = (x, y)
        new_left = new_left * scale
        new_right = new_right * scale
        m_ref[8 * s : 8 * s + 8, :128] = new_left
        m_ref[8 * s : 8 * s + 8, 128:] = new_right
        low = 8 * last
        if low < 128:
            update = t_dot(new_left, jnp.concatenate([new_left, new_right], axis=1))
            m_ref[low:, :] = m_ref[low:, :] - update[low:, :]


def identity(count, dtype=f32):
    row = lax.broadcasted_iota(jnp.int32, (count, count), 0)
    lane = lax.broadcasted_iota(jnp.int32, (count, count), 1)
    return jnp.where(row == lane, 1.0, 0.0).astype(dtype)


def eliminate(wide, small, r_ref, width):
    def step(p, carry):
        at = pl.multiple_of(p * 128, 128)
        small[:, :128] = wide[pl.ds(at, 128), pl.ds(at, 128)]
        small[:, 128:] = identity(128)
        factor_128(small)
        r_ref[:, :width] = dot(small[:, 128:], wide[pl.ds(at, 128), :width])
        wide[pl.ds(at, 128), :width] = r_ref[:, :width]

        def trail(q, carry):
            down = pl.multiple_of(q * 128, 128)
            wide[pl.ds(down, 128), :width] = wide[pl.ds(down, 128), :width] - t_dot(
                r_ref[:, pl.ds(down, 128)], r_ref[:, :width]
            )
            return carry

        lax.fori_loop(p + 1, 4, trail, 0)
        return carry

    lax.fori_loop(0, 4, step, 0)


def first_pivot(x3, wide, small, r_ref):
    for p in range(8):
        wide[64 * p : 64 * p + 64, 0:512] = x3[p, 0]
        wide[64 * p : 64 * p + 64, 512:1024] = x3[p, 1]
    wide[:, 1024:] = identity(512)
    eliminate(wide, small, r_ref, 1536)
    for p in range(8):
        x3[p, 0] = wide[64 * p : 64 * p + 64, 1024:]
        x3[p, 1] = wide[64 * p : 64 * p + 64, 512:1024]


def second_matrix(x3, fm, wide):
    u = wide[:, 512:1024]
    for i in range(2):
        product = t_dot(u[:, 256 * i : 256 * i + 256], u)
        for j in range(2):
            keep = fm[2 + i, 2 + j].astype(f32)
            for p in range(4):
                wide[256 * i + 64 * p : 256 * i + 64 * p + 64, 256 * j : 256 * j + 256] = (
                    x3[4 * i + p, 2, :, 256 * j : 256 * j + 256]
                    - keep * product[64 * p : 64 * p + 64, 256 * j : 256 * j + 256]
                )
    wide[:, 512:1024] = identity(512)


def second_pivot(x3, wide, small, r_ref):
    eliminate(wide, small, r_ref, 1024)
    for p in range(8):
        x3[p, 2] = wide[64 * p : 64 * p + 64, 512:1024]


def exchange_kernel(
    tab, fm, child, front, kids, ar_out, ac_out, xb_out, x3_out, panel,
    blocks, turned, corners, e1s, e1r_0, e1r_1, wide_kids, bs, pf, ar, ac, x3, xb, wide, small, r_ref,
    k_s, k_r, e1_s, e1_r, e2_s, e2_r, b_s, b_r, c1_s, c1_r, c2_s, c2_r, c3_s, c3_r,
    d1_s, d1_r, d2_s, d2_r, dz_s, dz_r, x1_s, x1_r, x2_s, x2_r, x3_s, x3_r, here,
):
    r = lax.axis_index("row")
    c = lax.axis_index("col")
    h = c // 2
    core = lax.rem(c, 2)
    sibling = c + 1 - 2 * core
    e1r = (e1r_0, e1r_1)
    z = r // 4
    y = lax.rem(r, 4)
    partner = lax.rem(r + 4, NR)
    root = (r == 0) & (c == 0)
    barrier = pltpu.get_barrier_semaphore()

    def send(src, dst, ss, rs, row, col):
        return pltpu.make_async_remote_copy(
            src_ref=src, dst_ref=dst, send_sem=ss, recv_sem=rs,
            device_id=(row, col), device_id_type=MESH,
        )

    def move(src, dst, n):
        return pltpu.make_async_copy(src, dst, here.at[n])

    def each(low, high, body):
        def run(i, carry):
            body(i)
            return carry

        lax.fori_loop(low, high, run, 0)

    def when(condition, body):
        pl.when(condition)(body)

    def greet(row, col):
        pl.semaphore_signal(barrier, inc=1, device_id=(row, col), device_id_type=MESH)

    each(1, NR, lambda d: greet(lax.rem(r + d, NR), c))
    each(1, NC, lambda d: greet(r, lax.rem(c + d, NC)))

    @pl.when(c < 2)
    def _():
        each(1, NR, lambda d: greet(lax.rem(r + d, NR), 1 - c))

    @pl.when(c == 0)
    def _():
        move(front.at[pl.ds(0, 4)], pf.at[pl.ds(0, 4)], 0).start()
        move(front.at[pl.ds(4, 4)], pf.at[pl.ds(4, 4)], 3).start()

    for a in range(16):
        blocks[a] = child[:, BS * a : BS * a + BS]

    def turn(a):
        turned[a] = dot_t(identity(BS, bf16), blocks[a], None).astype(bf16)

    when(c < 2, lambda: each(0, 16, turn))
    pl.semaphore_wait(barrier, jnp.where(c < 2, 29, 22))

    @pl.when((c < 2) & jnp.logical_not(root))
    def _():
        send(turned.at[pl.ds(0, 2)], corners.at[2 * r + c], k_s, k_r.at[2 * r + c], 0, 0).start()

    @pl.when(root)
    def _():
        for n in range(2):
            corners[0, n] = turned[n]

    @pl.when(c < 2)
    def _():
        def give(d):
            q = lax.rem(r + d, NR)
            for n in range(4):
                bs[q, n] = turned[tab[q] + n]

            @pl.when((q != r) | (c == 1))
            def _():
                send(
                    bs.at[q], wide_kids.at[pl.ds(8 * r + 4 * c, 4)],
                    b_s.at[q], b_r.at[2 * r + c], q, 0,
                ).start()

            @pl.when((q == r) & (c == 0))
            def _():
                for n in range(4):
                    wide_kids[8 * r + n] = bs[q, n]

        each(1, NR + 1, give)

    def to_col(m):
        def run(d):
            q = lax.rem(c + d, NC)

            @pl.when((q >= 1) & (q <= h + 8))
            def _():
                @pl.when(q != c)
                def _():
                    e1s[q, m] = blocks[tab[8 + q] + m]
                    send(
                        e1s.at[q, m], e1r[m].at[c], e1_s.at[16 * m + q], e1_r.at[16 * m + c], r, q
                    ).start()

                @pl.when(q == c)
                def _():
                    e1r[m][c] = blocks[tab[8 + q] + m]

        each(1, NC + 1, run)

    def left_col(m):
        each(1, NC, lambda q: when(
            (q <= h + 8) & (q != c), lambda: sent(e1s.at[q, m], e1_s.at[16 * m + q])
        ))

    def sent(buffer, sem):
        send(buffer, buffer, sem, c1_r, r, sibling).wait_send()

    to_col(0)
    when(c == 0, lambda: to_col(1))

    def assemble_panel():
        move(front.at[pl.ds(0, 4)], pf.at[pl.ds(0, 4)], 3).wait()

        def arrive(k):
            @pl.when(k != 2 * r)
            def _():
                send(
                    bs.at[0], wide_kids.at[pl.ds(4 * k, 4)],
                    b_s.at[0], b_r.at[k], k // 2, lax.rem(k, 2),
                ).wait_recv()

        each(0, 16, arrive)

        def assemble(i):
            for j in range(4):
                at = pl.ds(j * BS, BS)
                keep = fm[8 * r + i, j].astype(f32)
                pairs = []
                for k in range(NR):
                    pairs.append((
                        (tab[120 + 8 * k + i] * tab[184 + 4 * k + j]).astype(f32),
                        8 * k + 4 * tab[88 + 4 * k + j] + tab[24 + 8 * k + i],
                    ))
                for n in range(4):
                    low = 64 * n
                    total = pf[i, low : low + 64, at]
                    for times, from_slot in pairs:
                        total = total + times * wide_kids[from_slot, low : low + 64, :].astype(f32)
                    total = total * keep
                    pf[i, low : low + 64, at] = total
                    ar[i, n // 2, low % 128 : low % 128 + 64, at] = total.astype(bf16)

        each(0, 8, assemble)
        move(pf, panel, 0).start()

    def part(ref, q, t):
        return ref.at[q, pl.ds(2 * t, 2 - t)]

    def pivots_from_root(t):
        each(1, NR, lambda q: send(
            part(x3, q, t), part(x3, q, t), x1_s.at[8 * t + q], x1_r.at[t], q, 0
        ).start())

    def pivots_out(t):
        for n in ((0, 1), (2,))[t]:
            xb[r, n] = x3[r, n].astype(bf16)
        each(1, NC, lambda q: send(
            part(xb, r, t), part(xb, r, t), x2_s.at[16 * t + q], x2_r.at[t], r, q
        ).start())
        each(1, NR, lambda q: when(q != r, lambda: send(
            part(x3, r, t), part(x3, r, t), x3_s.at[12 * t + q], x3_r.at[8 * t + r], q, 0
        ).start()))

    @pl.when(root)
    def _():
        move(front.at[pl.ds(0, 4)], pf.at[pl.ds(0, 4)], 0).wait()
        each(1, 16, lambda k: send(
            turned.at[pl.ds(0, 2)], corners.at[k], k_s, k_r.at[k], k // 2, lax.rem(k, 2)
        ).wait_recv())
        for n, rows, cols in ((0, 0, 0), (1, 0, 2), (2, 2, 2)):

            def corner(i):
                for j in range(2):
                    keep = fm[rows + i, cols + j].astype(f32)
                    pairs = []
                    for k in range(NR):
                        pairs.append((
                            (tab[120 + 8 * k + rows + i] * tab[184 + 4 * k + cols + j]).astype(f32),
                            2 * k + tab[88 + 4 * k + cols + j],
                            tab[24 + 8 * k + rows + i],
                        ))
                    for p in range(4):
                        total = pf[
                            rows + i, 64 * p : 64 * p + 64,
                            BS * (cols + j) : BS * (cols + j) + BS,
                        ]
                        for times, side, slot in pairs:
                            total = total + times * corners[
                                side, slot, 64 * p : 64 * p + 64, :
                            ].astype(f32)
                        x3[4 * i + p, n, :, BS * j : BS * j + BS] = total * keep

            each(0, 2, corner)
        first_pivot(x3, wide, small, r_ref)
        pivots_from_root(0)
        pivots_out(0)
        second_matrix(x3, fm, wide)
        assemble_panel()
        send(ar, ar, c1_s.at[1], c1_r, 0, 1).start()
        second_pivot(x3, wide, small, r_ref)
        pivots_from_root(1)
        pivots_out(1)

    @pl.when((c == 0) & (r > 0))
    def _():
        move(front.at[pl.ds(0, 4)], pf.at[pl.ds(0, 4)], 0).wait()
        assemble_panel()
        each(1, NC, lambda q: send(
            ar.at[q // 2, lax.rem(q, 2)], ar.at[q // 2, lax.rem(q, 2)], c1_s.at[q], c1_r, r, q
        ).start())
        each(1, 8, lambda q: send(
            ar.at[0, 0], ar.at[0, 0], c2_s.at[q], c2_r.at[0], r, 2 * q
        ).start())
        each(0, 8, lambda q: send(
            ar.at[q, 0], ar.at[q, 0], c3_s.at[q], c3_r.at[q], r, 1
        ).start())
        for t in range(2):
            send(part(x3, r, t), part(x3, r, t), x1_s.at[0], x1_r.at[t], 0, 0).wait_recv()
            pivots_out(t)

    def to_row(m):
        def arrive(a):
            @pl.when(a != c)
            def _():
                send(
                    e1s.at[0, m], e1r[m].at[a], e1_s.at[0], e1_r.at[16 * m + a], r, a
                ).wait_recv()

        each(jnp.maximum(2 * (c - 8), 0), NC, arrive)

        def run(d):
            q = lax.rem(r + d, NR)
            mine = wide_kids.at[pl.ds(8 * q + 4 * m, 4)]
            there = kids.at[r, pl.ds(4 * m, 4)]

            @pl.when(q >= h)
            def _():
                for n in range(4):
                    wide_kids[8 * q + 4 * m + n] = e1r[m][tab[q] + n]

                @pl.when(q != r)
                def _():
                    send(mine, there, e2_s.at[8 * m + q], e2_r.at[8 * m + r], q, c).start()

                @pl.when(q == r)
                def _():
                    move(mine, there, 5 + m).start()

        for d in (4, 5, 6, 7, 1, 3, 2, 8):
            run(d)

    @pl.when(c > 0)
    def _():
        left_col(0)
        to_col(1)
        to_row(0)
        to_row(1)

    @pl.when((r == 0) & (c == 1))
    def _():
        send(ar, ar, c1_s.at[0], c1_r, 0, 0).wait_recv()

    def across(q):
        @pl.when(c != 1)
        def _():
            send(ar.at[q, core], ar.at[q, core], c3_s.at[q], c3_r.at[q], r, sibling).start()

    @pl.when((c > 0) & (r > 0))
    def _():
        send(ar.at[h, core], ar.at[h, core], c1_s.at[0], c1_r, r, 0).wait_recv()

        def spread(d):
            q = lax.rem(h + d, 8)

            @pl.when((q != 0) | (core != 0))
            def _():
                send(
                    ar.at[h, core], ar.at[h, core], c2_s.at[q], c2_r.at[h], r, 2 * q + core
                ).start()

        each(1, 8, spread)
        across(h)

        def collect(d):
            q = lax.rem(h + d, 8)
            send(
                ar.at[q, core], ar.at[q, core], c2_s.at[q], c2_r.at[q], r, 2 * q + core
            ).wait_recv()
            across(q)

        each(1, 8, collect)
        each(0, 8, lambda q: send(
            ar.at[q, 1 - core], ar.at[q, 1 - core], c3_s.at[q], c3_r.at[q], r, sibling
        ).wait_recv())

    @pl.when(c > 0)
    def _():
        @pl.when(r >= h)
        def _():
            move(ar, ar_out, 3).start()

        def match_along(piece):
            def on(d):
                q = 4 * z + lax.rem(y + d, 4)

                @pl.when(q > h)
                def _():
                    send(piece, ac.at[y], d2_s.at[lax.rem(q, 4)], d2_r.at[y], q, c).start()

            each(1, 4, on)

        def match_on(piece):
            @pl.when(z == 0)
            def _():
                send(piece, ac.at[y], dz_s, dz_r, partner, c).start()

            match_along(piece)

        @pl.when(r == h)
        def _():
            move(ar.at[pl.ds(4 * core, 4)], ac_out, 4).start()

            each(1, 4, lambda d: send(
                ar.at[4 * core + lax.rem(y + d, 4)], ac.at[lax.rem(y + d, 4)],
                d1_s.at[lax.rem(y + d, 4)], d1_r, 4 * z + lax.rem(y + d, 4), c,
            ).start())
            match_on(ar.at[4 * core + y])

        @pl.when((r != h) & (z == h // 4))
        def _():
            send(ac.at[y], ac.at[y], d1_s.at[0], d1_r, h, c).wait_recv()
            match_on(ac.at[y])

        @pl.when(z > h // 4)
        def _():
            send(ac.at[y], ac.at[y], dz_s, dz_r, partner, c).wait_recv()
            match_along(ac.at[y])

        def pivots_along(p, t, base):
            each(1, 4, lambda d: send(
                part(xb, p, t), part(xb, p, t), x3_s.at[12 * t + base + lax.rem(y + d, 4)],
                x3_r.at[8 * t + p], 4 * z + lax.rem(y + d, 4), c,
            ).start())

        for t in range(2):
            send(part(xb, r, t), part(xb, r, t), x2_s.at[0], x2_r.at[t], r, 0).wait_recv()
            send(
                part(xb, r, t), part(xb, r, t),
                x3_s.at[12 * t + partner], x3_r.at[8 * t + r], partner, c,
            ).start()
            pivots_along(r, t, 4 * z)
            send(
                part(xb, partner, t), part(xb, partner, t),
                x3_s.at[r], x3_r.at[8 * t + partner], partner, c,
            ).wait_recv()
            pivots_along(partner, t, 8)

        @pl.when(r > h)
        def _():
            each(1, 4, lambda d: send(
                ac.at[lax.rem(y + d, 4)], ac.at[lax.rem(y + d, 4)],
                d2_s.at[0], d2_r.at[lax.rem(y + d, 4)], 4 * z + lax.rem(y + d, 4), c,
            ).wait_recv())
            move(ac, ac_out, 4).start()

        @pl.when(r >= h)
        def _():
            def arrive(q):
                @pl.when(q != r)
                def _():
                    for m in range(2):
                        send(
                            wide_kids.at[pl.ds(0, 4)], kids.at[q, pl.ds(4 * m, 4)],
                            e2_s.at[0], e2_r.at[8 * m + q], q, c,
                        ).wait_recv()

            each(0, NR, arrive)

        def pieces(q):
            @pl.when((q != r) & (q != partner))
            def _():
                for t in range(2):
                    send(
                        part(xb, q, t), part(xb, q, t), x3_s.at[q], x3_r.at[8 * t + q], q, c
                    ).wait_recv()

        each(0, NR, pieces)
        move(xb, xb_out, 1).start()

    @pl.when(c == 0)
    def _():
        def pieces(q):
            @pl.when((q != r) & (r > 0))
            def _():
                for t in range(2):
                    send(
                        part(x3, q, t), part(x3, q, t), x3_s.at[q], x3_r.at[8 * t + q], q, c
                    ).wait_recv()

        each(0, NR, pieces)
        move(x3, x3_out, 1).start()

    def unless(condition, body):
        pl.when(jnp.logical_not(condition))(body)

    @pl.when(c < 2)
    def _():
        unless(root, lambda: sent(turned.at[pl.ds(0, 2)], k_s))
        each(0, NR, lambda q: when(
            (q != r) | (c == 1), lambda: sent(bs.at[q], b_s.at[q])
        ))

    when(c == 0, lambda: left_col(0))
    left_col(1)

    @pl.when(c == 0)
    def _():
        move(pf, panel, 0).wait()
        move(x3, x3_out, 1).wait()

        @pl.when(r == 0)
        def _():
            sent(ar, c1_s.at[1])
            for t in range(2):
                each(1, NR, lambda q: sent(part(x3, q, t), x1_s.at[8 * t + q]))

        @pl.when(r > 0)
        def _():
            each(1, NC, lambda q: sent(ar.at[0, 0], c1_s.at[q]))
            each(1, 8, lambda q: sent(ar.at[0, 0], c2_s.at[q]))
            each(0, 8, lambda q: sent(ar.at[q, 0], c3_s.at[q]))

        for t in range(2):
            each(1, NC, lambda q: sent(part(xb, 0, t), x2_s.at[16 * t + q]))
            each(1, NR, lambda q: when(
                q != r, lambda: sent(part(x3, 0, t), x3_s.at[12 * t + q])
            ))

    @pl.when(c > 0)
    def _():
        def left_row(q):
            for m in range(2):
                mine = wide_kids.at[pl.ds(8 * q + 4 * m, 4)]
                when(q != r, lambda: sent(mine, e2_s.at[8 * m + q]))
                when(q == r, lambda: move(mine, kids.at[r, pl.ds(4 * m, 4)], 5 + m).wait())

        each(h, NR, left_row)

        @pl.when(r > 0)
        def _():
            each(0, 8, lambda q: when(
                (q != h) & ((q != 0) | (core != 0)), lambda: sent(ar.at[0, 0], c2_s.at[q])
            ))
            when(c != 1, lambda: each(0, 8, lambda q: sent(ar.at[0, 0], c3_s.at[q])))

        for t in range(2):
            sent(part(xb, 0, t), x3_s.at[12 * t + partner])
            for base in (4 * z, 8):
                each(1, 4, lambda d: sent(
                    part(xb, 0, t), x3_s.at[12 * t + base + lax.rem(y + d, 4)]
                ))
        move(xb, xb_out, 1).wait()

        @pl.when(r >= h)
        def _():
            move(ar, ar_out, 3).wait()
            move(ac, ac_out, 4).wait()

        when(r == h, lambda: each(1, 4, lambda d: sent(ac.at[0], d1_s.at[lax.rem(y + d, 4)])))

        @pl.when(z >= h // 4)
        def _():
            when((z == 0) & (h < 4), lambda: sent(ac.at[0], dz_s))
            each(1, 4, lambda d: when(
                4 * z + lax.rem(y + d, 4) > h, lambda: sent(ac.at[0], d2_s.at[lax.rem(y + d, 4)])
            ))


def exchange(tab, fm, child, front):
    dma = pltpu.SemaphoreType.DMA
    sds = jax.ShapeDtypeStruct
    return pl.pallas_call(
        exchange_kernel,
        in_specs=[SM, SM, VM, ANY],
        out_specs=[ANY] * 6,
        out_shape=[
            sds((NR, 8, BS, BS), bf16),
            sds((8, 2, 128, 1024), bf16),
            sds((4, 2, 128, 1024), bf16),
            sds((8, 3, 64, 512), bf16),
            sds((8, 3, 64, 512), f32),
            sds((8, BS, 1024), f32),
        ],
        scratch_shapes=[
            pltpu.VMEM((16, BS, BS), bf16),
            pltpu.VMEM((16, BS, BS), bf16),
            pltpu.VMEM((16, 2, BS, BS), bf16),
            pltpu.VMEM((NC, 2, BS, BS), bf16),
            pltpu.VMEM((NC, BS, BS), bf16),
            pltpu.VMEM((NC, BS, BS), bf16),
            pltpu.VMEM((64, BS, BS), bf16),
            pltpu.VMEM((NR, 4, BS, BS), bf16),
            pltpu.VMEM((8, BS, 1024), f32),
            pltpu.VMEM((8, 2, 128, 1024), bf16),
            pltpu.VMEM((4, 2, 128, 1024), bf16),
            pltpu.VMEM((8, 3, 64, 512), f32),
            pltpu.VMEM((8, 3, 64, 512), bf16),
            pltpu.VMEM((512, 1536), f32),
            pltpu.VMEM((128, 256), f32),
            pltpu.VMEM((128, 1536), f32),
            dma, dma((16,)),
            dma((32,)), dma((32,)), dma((16,)), dma((16,)),
            dma((NR,)), dma((16,)),
            dma((NC,)), dma, dma((8,)), dma((8,)), dma((8,)), dma((8,)),
            dma((4,)), dma, dma((4,)), dma((4,)), dma, dma,
            dma((16,)), dma((2,)), dma((32,)), dma((2,)), dma((24,)), dma((16,)), dma((7,)),
        ],
        compiler_params=pltpu.CompilerParams(
            collective_id=1, has_side_effects=True, vmem_limit_bytes=58 << 20
        ),
        cost_estimate=pl.CostEstimate(flops=0, bytes_accessed=400_000_000, transcendentals=0),
        name="exchange",
    )(tab, fm, child, front)


def split(x):
    high = x.astype(bf16)
    return high, (x - high.astype(f32)).astype(bf16)


def update_kernel(
    tab, fm, front, panel, ar, ac, xb, x3, kids, out, inv0, low, inv1, low0, low1, low2, wc,
):
    r = lax.axis_index("row")
    c = lax.axis_index("col")
    i = pl.program_id(0)
    g = 8 * r + i
    active = g >= 4 * c

    def gather(ref, n):
        return jnp.concatenate([ref[p, n] for p in range(8)], axis=0)

    def solve(rows0, rows1, block_row):
        first = dot_t(rows0, inv0[...], None).astype(bf16)
        across = dot(first, low[...], None)
        second = jnp.concatenate(
            [
                rows1[:, BS * j : BS * j + BS].astype(f32)
                - fm[block_row, 2 + j].astype(f32) * across[:, BS * j : BS * j + BS]
                for j in range(2)
            ],
            axis=1,
        ).astype(bf16)
        return first, dot_t(second, inv1[...], None).astype(bf16)

    def thrice(product, x, high, rest):
        a, b = split(x)
        return (
            product(a, high[...], None) + product(a, rest[...], None) + product(b, high[...], None)
        )

    @pl.when((i == 0) & (c > 0) & (c // 2 <= r))
    def _():
        inv0[...] = gather(xb, 0)
        low[...] = gather(xb, 1)
        inv1[...] = gather(xb, 2)
        for j in range(4):
            block = jnp.concatenate([ac[j, 0], ac[j, 1]], axis=0)
            first, second = solve(block[:, :512], block[:, 512:], 4 * c + j)
            wc[BS * j : BS * j + BS, :512] = first
            wc[BS * j : BS * j + BS, 512:] = second

    @pl.when((i == 0) & (c == 0))
    def _():
        for n, (high, rest) in enumerate(((inv0, low0), (low, low1), (inv1, low2))):
            high[...], rest[...] = split(gather(x3, n))

    @pl.when(jnp.logical_not(active))
    def _():
        out[...] = jnp.zeros_like(out)

    @pl.when(active & (c == 0))
    def _():
        first = thrice(dot_t, panel[0, :, :512], inv0, low0)
        across = thrice(dot, first, low, low1)
        second = jnp.concatenate(
            [
                panel[0, :, 512 + BS * j : 768 + BS * j]
                - fm[g, 2 + j].astype(f32) * across[:, BS * j : BS * j + BS]
                for j in range(2)
            ],
            axis=1,
        )
        second = thrice(dot_t, second, inv1, low2)
        row = g * BS + lax.broadcasted_iota(jnp.int32, (BS, 512), 0)
        lane = lax.broadcasted_iota(jnp.int32, (BS, 512), 1)
        out[:, :512] = jnp.where(row >= lane, first, 0.0)
        out[:, 512:] = jnp.where(row >= lane + 512, second, 0.0)

    @pl.when(active & (c > 0))
    def _():
        block = jnp.concatenate([ar[0, 0], ar[0, 1]], axis=0)
        first, second = solve(block[:, :512], block[:, 512:], g)
        for j in range(4):
            at = pl.ds(BS * j, BS)
            keep = (fm[g, 4 * c + j] != 0) & (g >= 4 * c + j)

            @pl.when(keep)
            def _():
                product = dot_t(first, wc[BS * j : BS * j + BS, :512], None) + dot_t(
                    second, wc[BS * j : BS * j + BS, 512:], None
                )
                times = fm[g, 4 * c + j].astype(f32)
                out[:, at] = (front[:, at] - product) * times

                for k in range(NR):
                    slot = tab[24 + 8 * k + i]
                    side = tab[88 + 4 * k + j]

                    @pl.when(tab[120 + 8 * k + i] * tab[184 + 4 * k + j] > 0)
                    def _():
                        out[:, at] = out[:, at] + times * kids[k, 4 * side + slot].astype(f32)

            @pl.when(jnp.logical_not(keep))
            def _():
                out[:, at] = jnp.zeros((BS, BS), f32)


def update(tab, fm, front, panel, ar, ac, xb, x3, kids):
    whole = lambda shape: pl.BlockSpec(
        shape, lambda i: (0,) * len(shape), pipeline_mode=pl.Buffered(1)
    )
    return pl.pallas_call(
        update_kernel,
        grid=(8,),
        in_specs=[
            SM, SM,
            pl.BlockSpec((BS, 1024), lambda i: (i, 0)),
            pl.BlockSpec((1, BS, 1024), lambda i: (i, 0, 0)),
            pl.BlockSpec((1, 2, 128, 1024), lambda i: (i, 0, 0, 0)),
            whole((4, 2, 128, 1024)),
            whole((8, 3, 64, 512)),
            whole((8, 3, 64, 512)),
            whole((NR, 8, BS, BS)),
        ],
        out_specs=pl.BlockSpec((BS, 1024), lambda i: (i, 0)),
        out_shape=jax.ShapeDtypeStruct((2048, 1024), f32),
        scratch_shapes=[pltpu.VMEM((512, 512), bf16)] * 6 + [pltpu.VMEM((1024, 1024), bf16)],
        compiler_params=pltpu.CompilerParams(vmem_limit_bytes=48 << 20),
        name="update",
    )(tab, fm, front, panel, ar, ac, xb, x3, kids)


def tables(maps, r, c):
    own = lax.dynamic_index_in_dim(maps, r, 0, keepdims=False)
    row_start = jnp.minimum(jnp.sum(own[:, None] < 8 * jnp.arange(NR), axis=0), 12)
    col_start = jnp.minimum(jnp.sum(own[:, None] < 4 * jnp.arange(NC), axis=0), 14)
    index = jnp.arange(16)
    rows = maps[:, None, :] == 8 * r + jnp.arange(8)[None, :, None]
    row_first = jnp.minimum(jnp.sum(maps < 8 * r, axis=1), 12)
    row_slot = jnp.sum(rows * (index - row_first[:, None, None] + 1), axis=-1) - 1
    cols = maps[:, None, :] == 4 * c + jnp.arange(4)[None, :, None]
    col_first = jnp.minimum(jnp.sum(maps < 4 * c, axis=1), 14)
    col_slot = jnp.sum(cols * (index - col_first[:, None, None] + 1), axis=-1) - 1
    parts = [
        row_start,
        col_start,
        jnp.maximum(row_slot, 0).reshape(-1),
        jnp.maximum(col_slot, 0).reshape(-1),
        (row_slot >= 0).reshape(-1),
        (col_slot >= 0).reshape(-1),
    ]
    return jnp.concatenate([part.astype(jnp.int32) for part in parts])


def local(front, child_updates, child_maps, fill_mask):
    r = lax.axis_index("row")
    c = lax.axis_index("col")
    tab = tables(child_maps, r, c)
    kids, ar, ac, xb, x3, panel = exchange(
        tab, fill_mask, child_updates[0], front.reshape(8, BS, 1024)
    )
    return update(tab, fill_mask, front, panel, ar, ac, xb, x3, kids)


def solution(mesh):
    placed = (P("row", "col"), P("row", "col", None), P(), P())
    return jax.shard_map(
        local, mesh=mesh, in_specs=placed, out_specs=P("row", "col"), check_vma=False
    )
```

```python
import functools

import jax
import jax.numpy as jnp
from jax import lax
from jax.experimental import pallas as pl
from jax.experimental.pallas import tpu as pltpu
from jax.sharding import PartitionSpec as P

BS = 256
NR = 8
NC = 16
MESH = pl.DeviceIdType.MESH
HI = lax.Precision.HIGHEST
f32 = jnp.float32
bf16 = jnp.bfloat16
ANY = pl.BlockSpec(memory_space=pl.ANY)
VM = pl.BlockSpec(memory_space=pltpu.VMEM)
SM = pl.BlockSpec(memory_space=pltpu.SMEM)


def dot(a, b, precision=HI):
    return lax.dot_general(
        a, b, (((1,), (0,)), ((), ())), precision=precision, preferred_element_type=f32
    )


def dot_t(a, b, precision=HI):
    return lax.dot_general(
        a, b, (((1,), (1,)), ((), ())), precision=precision, preferred_element_type=f32
    )


def t_dot(a, b, precision=HI):
    return lax.dot_general(
        a, b, (((0,), (0,)), ((), ())), precision=precision, preferred_element_type=f32
    )


def row_of(x, k):
    return jnp.broadcast_to(x[k : k + 1, :], (8, 128))


def lane_of(x, k):
    return jnp.broadcast_to(x[:, k : k + 1], (8, 128))


def factor_128(m_ref, ahead=3):
    sub = lax.broadcasted_iota(jnp.int32, (8, 128), 0)
    lane = lax.broadcasted_iota(jnp.int32, (8, 128), 1)
    held = {}
    for s in range(16):
        last = min(s + ahead + 1, 16)
        for q in range(s, last):
            if q not in held:
                held[q] = (m_ref[8 * q : 8 * q + 8, :128], m_ref[8 * q : 8 * q + 8, 128:])
        left, right = held.pop(s)
        v = [lane_of(left, 8 * s + j) for j in range(8)]
        z = [jnp.where(sub == j, 1.0, 0.0).astype(f32) for j in range(8)]
        scale = jnp.zeros((8, 128), f32)
        rows, inverses = [], []
        for k in range(8):
            root = lax.rsqrt(row_of(v[k], k))
            scale = jnp.where(sub == k, root, scale)
            inverse = root * root
            inverses.append(inverse)
            below = jnp.where(sub > k, v[k], 0.0) * inverse
            row = {}
            for j in range(k + 1, 8):
                row[j] = row_of(v[j], k)
                v[j] = v[j] - below * row[j]
            rows.append(row)
            if k < 7:
                for j in range(k + 1):
                    z[j] = z[j] - below * row_of(z[j], k)
        new_left = z[0] * row_of(left, 0)
        new_right = z[0] * row_of(right, 0)
        for j in range(1, 8):
            new_left = new_left + z[j] * row_of(left, j)
            new_right = new_right + z[j] * row_of(right, j)
        new_left = jnp.where(lane >= 8 * s + sub, new_left, 0.0)
        rows_left = [row_of(new_left, k) for k in range(8)]
        rows_right = [row_of(new_right, k) for k in range(8)]
        for q in range(s + 1, last):
            x, y = held[q]
            w = [lane_of(x, 8 * s + j) for j in range(8)]
            for k in range(8):
                times = w[k] * inverses[k]
                for j in range(k + 1, 8):
                    w[j] = w[j] - times * rows[k][j]
                x = x - times * rows_left[k]
                y = y - times * rows_right[k]
            held[q] = (x, y)
        new_left = new_left * scale
        new_right = new_right * scale
        m_ref[8 * s : 8 * s + 8, :128] = new_left
        m_ref[8 * s : 8 * s + 8, 128:] = new_right
        low = 8 * last
        if low < 128:
            update = t_dot(new_left, jnp.concatenate([new_left, new_right], axis=1))
            m_ref[low:, :] = m_ref[low:, :] - update[low:, :]


def identity(count, dtype=f32):
    row = lax.broadcasted_iota(jnp.int32, (count, count), 0)
    lane = lax.broadcasted_iota(jnp.int32, (count, count), 1)
    return jnp.where(row == lane, 1.0, 0.0).astype(dtype)


def eliminate(wide, small, r_ref, width):
    def step(p, carry):
        at = pl.multiple_of(p * 128, 128)
        small[:, :128] = wide[pl.ds(at, 128), pl.ds(at, 128)]
        small[:, 128:] = identity(128)
        factor_128(small)
        r_ref[:, :width] = dot(small[:, 128:], wide[pl.ds(at, 128), :width])
        wide[pl.ds(at, 128), :width] = r_ref[:, :width]

        def trail(q, carry):
            down = pl.multiple_of(q * 128, 128)
            wide[pl.ds(down, 128), :width] = wide[pl.ds(down, 128), :width] - t_dot(
                r_ref[:, pl.ds(down, 128)], r_ref[:, :width]
            )
            return carry

        lax.fori_loop(p + 1, 4, trail, 0)
        return carry

    lax.fori_loop(0, 4, step, 0)


def first_pivot(x3, wide, small, r_ref):
    for p in range(8):
        wide[64 * p : 64 * p + 64, 0:512] = x3[p, 0]
        wide[64 * p : 64 * p + 64, 512:1024] = x3[p, 1]
    wide[:, 1024:] = identity(512)
    eliminate(wide, small, r_ref, 1536)
    for p in range(8):
        x3[p, 0] = wide[64 * p : 64 * p + 64, 1024:]
        x3[p, 1] = wide[64 * p : 64 * p + 64, 512:1024]


def second_matrix(x3, fm, wide):
    u = wide[:, 512:1024]
    for i in range(2):
        product = t_dot(u[:, 256 * i : 256 * i + 256], u)
        for j in range(2):
            keep = fm[2 + i, 2 + j].astype(f32)
            for p in range(4):
                wide[256 * i + 64 * p : 256 * i + 64 * p + 64, 256 * j : 256 * j + 256] = (
                    x3[4 * i + p, 2, :, 256 * j : 256 * j + 256]
                    - keep * product[64 * p : 64 * p + 64, 256 * j : 256 * j + 256]
                )
    wide[:, 512:1024] = identity(512)


def second_pivot(x3, wide, small, r_ref):
    eliminate(wide, small, r_ref, 1024)
    for p in range(8):
        x3[p, 2] = wide[64 * p : 64 * p + 64, 512:1024]


def exchange_kernel(
    tab, fm, child, front, kids, ar_out, ac_out, xb_out, x3_out, panel,
    blocks, turned, corners, e1s, e1r_0, e1r_1, held_0, held_1, bs, pf, ar, ac, x3, xb, wide, small, r_ref,
    k_s, k_r, e1_s, e1_r, e2_s, e2_r, b_s, b_r, c1_s, c1_r, c2_s, c2_r, c3_s, c3_r,
    d1_s, d1_r, d2_s, d2_r, dz_s, dz_r, x1_s, x1_r, x2_s, x2_r, x3_s, x3_r, here,
):
    r = lax.axis_index("row")
    c = lax.axis_index("col")
    h = c // 2
    core = lax.rem(c, 2)
    sibling = c + 1 - 2 * core
    e1r = (e1r_0, e1r_1)
    held = (held_0, held_1)
    z = r // 4
    y = lax.rem(r, 4)
    partner = lax.rem(r + 4, NR)
    root = (r == 0) & (c == 0)
    barrier = pltpu.get_barrier_semaphore()

    def send(src, dst, ss, rs, row, col):
        return pltpu.make_async_remote_copy(
            src_ref=src, dst_ref=dst, send_sem=ss, recv_sem=rs,
            device_id=(row, col), device_id_type=MESH,
        )

    def move(src, dst, n):
        return pltpu.make_async_copy(src, dst, here.at[n])

    def each(low, high, body):
        def run(i, carry):
            body(i)
            return carry

        lax.fori_loop(low, high, run, 0)

    def when(condition, body):
        pl.when(condition)(body)

    def greet(row, col):
        pl.semaphore_signal(barrier, inc=1, device_id=(row, col), device_id_type=MESH)

    each(1, NR, lambda d: greet(lax.rem(r + d, NR), c))
    each(1, NC, lambda d: greet(r, lax.rem(c + d, NC)))

    @pl.when(c < 2)
    def _():
        each(1, NR, lambda d: greet(lax.rem(r + d, NR), 1 - c))

    @pl.when(c == 0)
    def _():
        move(front.at[pl.ds(0, 4)], pf.at[pl.ds(0, 4)], 0).start()
        move(front.at[pl.ds(4, 4)], pf.at[pl.ds(4, 4)], 3).start()

    for a in range(16):
        blocks[a] = child[:, BS * a : BS * a + BS]

    def turn(a):
        turned[a] = dot_t(identity(BS, bf16), blocks[a], None).astype(bf16)

    when(c < 2, lambda: each(0, 16, turn))
    pl.semaphore_wait(barrier, jnp.where(c < 2, 29, 22))

    @pl.when((c < 2) & jnp.logical_not(root))
    def _():
        send(turned.at[pl.ds(0, 2)], corners.at[2 * r + c], k_s, k_r.at[2 * r + c], 0, 0).start()

    @pl.when(root)
    def _():
        for n in range(2):
            corners[0, n] = turned[n]

    @pl.when(c < 2)
    def _():
        def give(t, d):
            q = lax.rem(r + d, NR)
            for n in range(4):
                bs[t, q, n] = turned[tab[q] + n, 128 * t : 128 * t + 128, :]

            @pl.when((q != r) | (c == 1))
            def _():
                send(
                    bs.at[t, q], held[t].at[pl.ds(8 * r + 4 * c, 4)],
                    b_s.at[8 * t + q], b_r.at[16 * t + 2 * r + c], q, 0,
                ).start()

            @pl.when((q == r) & (c == 0))
            def _():
                for n in range(4):
                    held[t][8 * r + n] = bs[t, q, n]

        for t in range(2):
            each(1, NR + 1, functools.partial(give, t))

    def to_col(m):
        def run(d):
            q = lax.rem(c + d, NC)

            @pl.when((q >= 1) & (q <= h + 8))
            def _():
                @pl.when(q != c)
                def _():
                    e1s[q, m] = blocks[tab[8 + q] + m]
                    send(
                        e1s.at[q, m], e1r[m].at[c], e1_s.at[16 * m + q], e1_r.at[16 * m + c], r, q
                    ).start()

                @pl.when(q == c)
                def _():
                    e1r[m][c] = blocks[tab[8 + q] + m]

        each(1, NC + 1, run)

    def left_col(m):
        each(1, NC, lambda q: when(
            (q <= h + 8) & (q != c), lambda: sent(e1s.at[q, m], e1_s.at[16 * m + q])
        ))

    def sent(buffer, sem):
        send(buffer, buffer, sem, c1_r, r, sibling).wait_send()

    to_col(0)
    when(c == 0, lambda: to_col(1))

    def assemble_panel(give_rows):
        move(front.at[pl.ds(0, 4)], pf.at[pl.ds(0, 4)], 3).wait()

        def arrive(t, k):
            @pl.when(k != 2 * r)
            def _():
                send(
                    bs.at[0, 0], held[t].at[pl.ds(4 * k, 4)],
                    b_s.at[0], b_r.at[16 * t + k], k // 2, lax.rem(k, 2),
                ).wait_recv()

        def assemble(t, i):
            for j in range(4):
                at = pl.ds(j * BS, BS)
                keep = fm[8 * r + i, j].astype(f32)
                pairs = []
                for k in range(NR):
                    pairs.append((
                        (tab[120 + 8 * k + i] * tab[184 + 4 * k + j]).astype(f32),
                        8 * k + 4 * tab[88 + 4 * k + j] + tab[24 + 8 * k + i],
                    ))
                for n in range(2):
                    low = 128 * t + 64 * n
                    total = pf[i, low : low + 64, at]
                    for times, from_slot in pairs:
                        total = total + times * held[t][
                            from_slot, 64 * n : 64 * n + 64, :
                        ].astype(f32)
                    total = total * keep
                    pf[i, low : low + 64, at] = total
                    ar[i, t, 64 * n : 64 * n + 64, at] = total.astype(bf16)
            give_rows(t, i)

        for t in range(2):
            each(0, 16, functools.partial(arrive, t))
            each(0, 8, functools.partial(assemble, t))
        move(pf, panel, 0).start()

    def part(ref, q, t):
        return ref.at[q, pl.ds(2 * t, 2 - t)]

    def pivots_from_root(t):
        each(1, NR, lambda q: send(
            part(x3, q, t), part(x3, q, t), x1_s.at[8 * t + q], x1_r.at[t], q, 0
        ).start())

    def pivots_out(t):
        for n in ((0, 1), (2,))[t]:
            xb[r, n] = x3[r, n].astype(bf16)
        each(1, NC, lambda q: send(
            part(xb, r, t), part(xb, r, t), x2_s.at[16 * t + q], x2_r.at[t], r, q
        ).start())
        each(1, NR, lambda q: when(q != r, lambda: send(
            part(x3, r, t), part(x3, r, t), x3_s.at[12 * t + q], x3_r.at[8 * t + r], q, 0
        ).start()))

    @pl.when(root)
    def _():
        move(front.at[pl.ds(0, 4)], pf.at[pl.ds(0, 4)], 0).wait()
        each(1, 16, lambda k: send(
            turned.at[pl.ds(0, 2)], corners.at[k], k_s, k_r.at[k], k // 2, lax.rem(k, 2)
        ).wait_recv())
        for n, rows, cols in ((0, 0, 0), (1, 0, 2), (2, 2, 2)):

            def corner(i):
                for j in range(2):
                    keep = fm[rows + i, cols + j].astype(f32)
                    pairs = []
                    for k in range(NR):
                        pairs.append((
                            (tab[120 + 8 * k + rows + i] * tab[184 + 4 * k + cols + j]).astype(f32),
                            2 * k + tab[88 + 4 * k + cols + j],
                            tab[24 + 8 * k + rows + i],
                        ))
                    for p in range(4):
                        total = pf[
                            rows + i, 64 * p : 64 * p + 64,
                            BS * (cols + j) : BS * (cols + j) + BS,
                        ]
                        for times, side, slot in pairs:
                            total = total + times * corners[
                                side, slot, 64 * p : 64 * p + 64, :
                            ].astype(f32)
                        x3[4 * i + p, n, :, BS * j : BS * j + BS] = total * keep

            each(0, 2, corner)
        first_pivot(x3, wide, small, r_ref)
        pivots_from_root(0)
        pivots_out(0)
        second_matrix(x3, fm, wide)
        assemble_panel(lambda t, i: send(
            ar.at[i, t], ar.at[i, t], c1_s.at[1], c1_r, 0, 1
        ).start())
        second_pivot(x3, wide, small, r_ref)
        pivots_from_root(1)
        pivots_out(1)

    @pl.when((c == 0) & (r > 0))
    def _():
        move(front.at[pl.ds(0, 4)], pf.at[pl.ds(0, 4)], 0).wait()

        def give_rows(t, i):
            if t == 1:
                send(ar.at[i, 1], ar.at[i, 1], c1_s.at[2 * i + 1], c1_r, r, 2 * i + 1).start()
                return
            send(ar.at[i, 0], ar.at[i, 0], c3_s.at[i], c3_r.at[i], r, 1).start()

            @pl.when(i > 0)
            def _():
                send(ar.at[i, 0], ar.at[i, 0], c1_s.at[2 * i], c1_r, r, 2 * i).start()

            @pl.when(i == 0)
            def _():
                each(1, 8, lambda q: send(
                    ar.at[0, 0], ar.at[0, 0], c2_s.at[q], c2_r.at[0], r, 2 * q
                ).start())

        assemble_panel(give_rows)
        for t in range(2):
            send(part(x3, r, t), part(x3, r, t), x1_s.at[0], x1_r.at[t], 0, 0).wait_recv()
            pivots_out(t)

    def to_row(m):
        def arrive(a):
            @pl.when(a != c)
            def _():
                send(
                    e1s.at[0, m], e1r[m].at[a], e1_s.at[0], e1_r.at[16 * m + a], r, a
                ).wait_recv()

        each(jnp.maximum(2 * (c - 8), 0), NC, arrive)

        def run(d):
            q = lax.rem(r + d, NR)
            mine = held[m].at[pl.ds(8 * q, 8)]
            there = kids.at[r, pl.ds(8 * m, 8)]

            @pl.when(q >= h)
            def _():
                for n in range(4):
                    for u in range(2):
                        held[m][8 * q + 2 * n + u] = e1r[m][
                            tab[q] + n, 128 * u : 128 * u + 128, :
                        ]

                @pl.when(q != r)
                def _():
                    send(mine, there, e2_s.at[8 * m + q], e2_r.at[8 * m + r], q, c).start()

                @pl.when(q == r)
                def _():
                    move(mine, there, 5 + m).start()

        for d in (4, 5, 6, 7, 1, 3, 2, 8):
            run(d)

    @pl.when(c > 0)
    def _():
        left_col(0)
        to_col(1)
        to_row(0)
        to_row(1)

    @pl.when((r == 0) & (c == 1))
    def _():
        send(ar, ar, c1_s.at[0], c1_r, 0, 0).wait_recv()

    def across(q):
        @pl.when(c != 1)
        def _():
            send(ar.at[q, core], ar.at[q, core], c3_s.at[q], c3_r.at[q], r, sibling).start()

    def match_along(ref, row, t):
        def on(d):
            q = 4 * z + lax.rem(y + d, 4)

            @pl.when(q > h)
            def _():
                send(
                    ref.at[row, t], ac.at[y, t],
                    d2_s.at[4 * t + lax.rem(q, 4)], d2_r.at[4 * t + y], q, c,
                ).start()

        each(1, 4, on)

    def match_on(ref, row, t):
        @pl.when(z == 0)
        def _():
            send(ref.at[row, t], ac.at[y, t], dz_s.at[t], dz_r.at[t], partner, c).start()

        match_along(ref, row, t)

    def match_from(t):
        @pl.when((r == h) & (c > 0))
        def _():
            each(1, 4, lambda d: send(
                ar.at[4 * core + lax.rem(y + d, 4), t], ac.at[lax.rem(y + d, 4), t],
                d1_s.at[4 * t + lax.rem(y + d, 4)], d1_r.at[t], 4 * z + lax.rem(y + d, 4), c,
            ).start())
            match_on(ar, 4 * core + y, t)

    def own_half():
        send(ar.at[h, core], ar.at[h, core], c1_s.at[0], c1_r, r, 0).wait_recv()

        def spread(d):
            q = lax.rem(h + d, 8)

            @pl.when((q != 0) | (core != 0))
            def _():
                send(
                    ar.at[h, core], ar.at[h, core], c2_s.at[q], c2_r.at[h], r, 2 * q + core
                ).start()

        each(1, 8, spread)
        across(h)

        def collect(d):
            q = lax.rem(h + d, 8)
            send(
                ar.at[q, core], ar.at[q, core], c2_s.at[q], c2_r.at[q], r, 2 * q + core
            ).wait_recv()
            across(q)

        each(1, 8, collect)

    def other_half():
        each(0, 8, lambda q: send(
            ar.at[q, 1 - core], ar.at[q, 1 - core], c3_s.at[q], c3_r.at[q], r, sibling
        ).wait_recv())

    @pl.when((r > 0) & (c > 0) & (core == 0))
    def _():
        own_half()
        match_from(0)
        other_half()
        match_from(1)

    @pl.when((r > 0) & (core == 1))
    def _():
        other_half()
        match_from(0)
        own_half()
        match_from(1)

    @pl.when((r == 0) & (c == 1))
    def _():
        match_from(0)
        match_from(1)

    @pl.when(c > 0)
    def _():
        @pl.when(r >= h)
        def _():
            move(ar, ar_out, 3).start()

        @pl.when(r == h)
        def _():
            move(ar.at[pl.ds(4 * core, 4)], ac_out, 4).start()


        @pl.when((r != h) & (z == h // 4))
        def _():
            for t in range(2):
                send(ac.at[y, t], ac.at[y, t], d1_s.at[0], d1_r.at[t], h, c).wait_recv()
                match_on(ac, y, t)

        @pl.when(z > h // 4)
        def _():
            for t in range(2):
                send(ac.at[y, t], ac.at[y, t], dz_s.at[t], dz_r.at[t], partner, c).wait_recv()
                match_along(ac, y, t)

        def pivots_along(p, t, base):
            each(1, 4, lambda d: send(
                part(xb, p, t), part(xb, p, t), x3_s.at[12 * t + base + lax.rem(y + d, 4)],
                x3_r.at[8 * t + p], 4 * z + lax.rem(y + d, 4), c,
            ).start())

        for t in range(2):
            send(part(xb, r, t), part(xb, r, t), x2_s.at[0], x2_r.at[t], r, 0).wait_recv()
            send(
                part(xb, r, t), part(xb, r, t),
                x3_s.at[12 * t + partner], x3_r.at[8 * t + r], partner, c,
            ).start()
            pivots_along(r, t, 4 * z)
            send(
                part(xb, partner, t), part(xb, partner, t),
                x3_s.at[r], x3_r.at[8 * t + partner], partner, c,
            ).wait_recv()
            pivots_along(partner, t, 8)

        @pl.when(r > h)
        def _():
            for t in range(2):
                each(1, 4, lambda d: send(
                    ac.at[lax.rem(y + d, 4), t], ac.at[lax.rem(y + d, 4), t],
                    d2_s.at[0], d2_r.at[4 * t + lax.rem(y + d, 4)], 4 * z + lax.rem(y + d, 4), c,
                ).wait_recv())
            move(ac, ac_out, 4).start()

        @pl.when(r >= h)
        def _():
            def arrive(q):
                @pl.when(q != r)
                def _():
                    for m in range(2):
                        send(
                            held[m].at[pl.ds(0, 8)], kids.at[q, pl.ds(8 * m, 8)],
                            e2_s.at[0], e2_r.at[8 * m + q], q, c,
                        ).wait_recv()

            each(0, NR, arrive)

        def pieces(q):
            @pl.when((q != r) & (q != partner))
            def _():
                for t in range(2):
                    send(
                        part(xb, q, t), part(xb, q, t), x3_s.at[q], x3_r.at[8 * t + q], q, c
                    ).wait_recv()

        each(0, NR, pieces)
        move(xb, xb_out, 1).start()

    @pl.when(c == 0)
    def _():
        def pieces(q):
            @pl.when((q != r) & (r > 0))
            def _():
                for t in range(2):
                    send(
                        part(x3, q, t), part(x3, q, t), x3_s.at[q], x3_r.at[8 * t + q], q, c
                    ).wait_recv()

        each(0, NR, pieces)
        move(x3, x3_out, 1).start()

    def unless(condition, body):
        pl.when(jnp.logical_not(condition))(body)

    @pl.when(c < 2)
    def _():
        unless(root, lambda: sent(turned.at[pl.ds(0, 2)], k_s))
        for t in range(2):
            each(0, NR, lambda q: when(
                (q != r) | (c == 1), lambda: sent(bs.at[t, q], b_s.at[8 * t + q])
            ))

    when(c == 0, lambda: left_col(0))
    left_col(1)

    @pl.when(c == 0)
    def _():
        move(pf, panel, 0).wait()
        move(x3, x3_out, 1).wait()

        @pl.when(r == 0)
        def _():
            sent(ar, c1_s.at[1])
            for t in range(2):
                each(1, NR, lambda q: sent(part(x3, q, t), x1_s.at[8 * t + q]))

        @pl.when(r > 0)
        def _():
            each(1, NC, lambda q: sent(ar.at[0, 0], c1_s.at[q]))
            each(1, 8, lambda q: sent(ar.at[0, 0], c2_s.at[q]))
            each(0, 8, lambda q: sent(ar.at[q, 0], c3_s.at[q]))

        for t in range(2):
            each(1, NC, lambda q: sent(part(xb, 0, t), x2_s.at[16 * t + q]))
            each(1, NR, lambda q: when(
                q != r, lambda: sent(part(x3, 0, t), x3_s.at[12 * t + q])
            ))

    @pl.when(c > 0)
    def _():
        def left_row(q):
            for m in range(2):
                mine = held[m].at[pl.ds(8 * q, 8)]
                when(q != r, lambda: sent(mine, e2_s.at[8 * m + q]))
                when(q == r, lambda: move(mine, kids.at[r, pl.ds(8 * m, 8)], 5 + m).wait())

        each(h, NR, left_row)

        @pl.when(r > 0)
        def _():
            each(0, 8, lambda q: when(
                (q != h) & ((q != 0) | (core != 0)), lambda: sent(ar.at[0, 0], c2_s.at[q])
            ))
            when(c != 1, lambda: each(0, 8, lambda q: sent(ar.at[0, 0], c3_s.at[q])))

        for t in range(2):
            sent(part(xb, 0, t), x3_s.at[12 * t + partner])
            for base in (4 * z, 8):
                each(1, 4, lambda d: sent(
                    part(xb, 0, t), x3_s.at[12 * t + base + lax.rem(y + d, 4)]
                ))
        move(xb, xb_out, 1).wait()

        @pl.when(r >= h)
        def _():
            move(ar, ar_out, 3).wait()
            move(ac, ac_out, 4).wait()

        for t in range(2):
            when(r == h, lambda: each(1, 4, lambda d: sent(
                ac.at[0, 0], d1_s.at[4 * t + lax.rem(y + d, 4)]
            )))

        @pl.when(z >= h // 4)
        def _():
            for t in range(2):
                when((z == 0) & (h < 4), lambda: sent(ac.at[0, 0], dz_s.at[t]))
                each(1, 4, lambda d: when(
                    4 * z + lax.rem(y + d, 4) > h,
                    lambda: sent(ac.at[0, 0], d2_s.at[4 * t + lax.rem(y + d, 4)]),
                ))


def exchange(tab, fm, child, front):
    dma = pltpu.SemaphoreType.DMA
    sds = jax.ShapeDtypeStruct
    return pl.pallas_call(
        exchange_kernel,
        in_specs=[SM, SM, VM, ANY],
        out_specs=[ANY] * 6,
        out_shape=[
            sds((NR, 16, 128, BS), bf16),
            sds((8, 2, 128, 1024), bf16),
            sds((4, 2, 128, 1024), bf16),
            sds((8, 3, 64, 512), bf16),
            sds((8, 3, 64, 512), f32),
            sds((8, BS, 1024), f32),
        ],
        scratch_shapes=[
            pltpu.VMEM((16, BS, BS), bf16),
            pltpu.VMEM((16, BS, BS), bf16),
            pltpu.VMEM((16, 2, BS, BS), bf16),
            pltpu.VMEM((NC, 2, BS, BS), bf16),
            pltpu.VMEM((NC, BS, BS), bf16),
            pltpu.VMEM((NC, BS, BS), bf16),
            pltpu.VMEM((64, 128, BS), bf16),
            pltpu.VMEM((64, 128, BS), bf16),
            pltpu.VMEM((2, NR, 4, 128, BS), bf16),
            pltpu.VMEM((8, BS, 1024), f32),
            pltpu.VMEM((8, 2, 128, 1024), bf16),
            pltpu.VMEM((4, 2, 128, 1024), bf16),
            pltpu.VMEM((8, 3, 64, 512), f32),
            pltpu.VMEM((8, 3, 64, 512), bf16),
            pltpu.VMEM((512, 1536), f32),
            pltpu.VMEM((128, 256), f32),
            pltpu.VMEM((128, 1536), f32),
            dma, dma((16,)),
            dma((32,)), dma((32,)), dma((16,)), dma((16,)),
            dma((16,)), dma((32,)),
            dma((NC,)), dma, dma((8,)), dma((8,)), dma((8,)), dma((8,)),
            dma((8,)), dma((2,)), dma((8,)), dma((8,)), dma((2,)), dma((2,)),
            dma((16,)), dma((2,)), dma((32,)), dma((2,)), dma((24,)), dma((16,)), dma((7,)),
        ],
        compiler_params=pltpu.CompilerParams(
            collective_id=1, has_side_effects=True, vmem_limit_bytes=58 << 20
        ),
        cost_estimate=pl.CostEstimate(flops=0, bytes_accessed=400_000_000, transcendentals=0),
        name="exchange",
    )(tab, fm, child, front)


def split(x):
    high = x.astype(bf16)
    return high, (x - high.astype(f32)).astype(bf16)


def update_kernel(
    tab, fm, front, panel, ar, ac, xb, x3, kids, out, inv0, low, inv1, low0, low1, low2, wc,
):
    r = lax.axis_index("row")
    c = lax.axis_index("col")
    i = pl.program_id(0)
    g = 8 * r + i
    active = g >= 4 * c

    def gather(ref, n):
        return jnp.concatenate([ref[p, n] for p in range(8)], axis=0)

    def solve(rows0, rows1, block_row):
        first = dot_t(rows0, inv0[...], None).astype(bf16)
        across = dot(first, low[...], None)
        second = jnp.concatenate(
            [
                rows1[:, BS * j : BS * j + BS].astype(f32)
                - fm[block_row, 2 + j].astype(f32) * across[:, BS * j : BS * j + BS]
                for j in range(2)
            ],
            axis=1,
        ).astype(bf16)
        return first, dot_t(second, inv1[...], None).astype(bf16)

    def thrice(product, x, high, rest):
        a, b = split(x)
        return (
            product(a, high[...], None) + product(a, rest[...], None) + product(b, high[...], None)
        )

    @pl.when((i == 0) & (c > 0) & (c // 2 <= r))
    def _():
        inv0[...] = gather(xb, 0)
        low[...] = gather(xb, 1)
        inv1[...] = gather(xb, 2)
        for j in range(4):
            block = jnp.concatenate([ac[j, 0], ac[j, 1]], axis=0)
            first, second = solve(block[:, :512], block[:, 512:], 4 * c + j)
            wc[BS * j : BS * j + BS, :512] = first
            wc[BS * j : BS * j + BS, 512:] = second

    @pl.when((i == 0) & (c == 0))
    def _():
        for n, (high, rest) in enumerate(((inv0, low0), (low, low1), (inv1, low2))):
            high[...], rest[...] = split(gather(x3, n))

    @pl.when(jnp.logical_not(active))
    def _():
        out[...] = jnp.zeros_like(out)

    @pl.when(active & (c == 0))
    def _():
        first = thrice(dot_t, panel[0, :, :512], inv0, low0)
        across = thrice(dot, first, low, low1)
        second = jnp.concatenate(
            [
                panel[0, :, 512 + BS * j : 768 + BS * j]
                - fm[g, 2 + j].astype(f32) * across[:, BS * j : BS * j + BS]
                for j in range(2)
            ],
            axis=1,
        )
        second = thrice(dot_t, second, inv1, low2)
        row = g * BS + lax.broadcasted_iota(jnp.int32, (BS, 512), 0)
        lane = lax.broadcasted_iota(jnp.int32, (BS, 512), 1)
        out[:, :512] = jnp.where(row >= lane, first, 0.0)
        out[:, 512:] = jnp.where(row >= lane + 512, second, 0.0)

    @pl.when(active & (c > 0))
    def _():
        block = jnp.concatenate([ar[0, 0], ar[0, 1]], axis=0)
        first, second = solve(block[:, :512], block[:, 512:], g)
        for j in range(4):
            at = pl.ds(BS * j, BS)
            keep = (fm[g, 4 * c + j] != 0) & (g >= 4 * c + j)

            @pl.when(keep)
            def _():
                product = dot_t(first, wc[BS * j : BS * j + BS, :512], None) + dot_t(
                    second, wc[BS * j : BS * j + BS, 512:], None
                )
                times = fm[g, 4 * c + j].astype(f32)
                out[:, at] = (front[:, at] - product) * times

                for k in range(NR):
                    slot = tab[24 + 8 * k + i]
                    side = tab[88 + 4 * k + j]

                    @pl.when(tab[120 + 8 * k + i] * tab[184 + 4 * k + j] > 0)
                    def _():
                        for u in range(2):
                            half = pl.ds(128 * u, 128)
                            out[half, at] = out[half, at] + times * kids[
                                k, 8 * side + 2 * slot + u
                            ].astype(f32)

            @pl.when(jnp.logical_not(keep))
            def _():
                out[:, at] = jnp.zeros((BS, BS), f32)


def update(tab, fm, front, panel, ar, ac, xb, x3, kids):
    whole = lambda shape: pl.BlockSpec(
        shape, lambda i: (0,) * len(shape), pipeline_mode=pl.Buffered(1)
    )
    return pl.pallas_call(
        update_kernel,
        grid=(8,),
        in_specs=[
            SM, SM,
            pl.BlockSpec((BS, 1024), lambda i: (i, 0)),
            pl.BlockSpec((1, BS, 1024), lambda i: (i, 0, 0)),
            pl.BlockSpec((1, 2, 128, 1024), lambda i: (i, 0, 0, 0)),
            whole((4, 2, 128, 1024)),
            whole((8, 3, 64, 512)),
            whole((8, 3, 64, 512)),
            whole((NR, 16, 128, BS)),
        ],
        out_specs=pl.BlockSpec((BS, 1024), lambda i: (i, 0)),
        out_shape=jax.ShapeDtypeStruct((2048, 1024), f32),
        scratch_shapes=[pltpu.VMEM((512, 512), bf16)] * 6 + [pltpu.VMEM((1024, 1024), bf16)],
        compiler_params=pltpu.CompilerParams(vmem_limit_bytes=48 << 20),
        name="update",
    )(tab, fm, front, panel, ar, ac, xb, x3, kids)


def tables(maps, r, c):
    own = lax.dynamic_index_in_dim(maps, r, 0, keepdims=False)
    row_start = jnp.minimum(jnp.sum(own[:, None] < 8 * jnp.arange(NR), axis=0), 12)
    col_start = jnp.minimum(jnp.sum(own[:, None] < 4 * jnp.arange(NC), axis=0), 14)
    index = jnp.arange(16)
    rows = maps[:, None, :] == 8 * r + jnp.arange(8)[None, :, None]
    row_first = jnp.minimum(jnp.sum(maps < 8 * r, axis=1), 12)
    row_slot = jnp.sum(rows * (index - row_first[:, None, None] + 1), axis=-1) - 1
    cols = maps[:, None, :] == 4 * c + jnp.arange(4)[None, :, None]
    col_first = jnp.minimum(jnp.sum(maps < 4 * c, axis=1), 14)
    col_slot = jnp.sum(cols * (index - col_first[:, None, None] + 1), axis=-1) - 1
    parts = [
        row_start,
        col_start,
        jnp.maximum(row_slot, 0).reshape(-1),
        jnp.maximum(col_slot, 0).reshape(-1),
        (row_slot >= 0).reshape(-1),
        (col_slot >= 0).reshape(-1),
    ]
    return jnp.concatenate([part.astype(jnp.int32) for part in parts])


def local(front, child_updates, child_maps, fill_mask):
    r = lax.axis_index("row")
    c = lax.axis_index("col")
    tab = tables(child_maps, r, c)
    kids, ar, ac, xb, x3, panel = exchange(
        tab, fill_mask, child_updates[0], front.reshape(8, BS, 1024)
    )
    return update(tab, fill_mask, front, panel, ar, ac, xb, x3, kids)


def solution(mesh):
    placed = (P("row", "col"), P("row", "col", None), P(), P())
    return jax.shard_map(
        local, mesh=mesh, in_specs=placed, out_specs=P("row", "col"), check_vma=False
    )
```

```python
import functools

import jax
import jax.numpy as jnp
from jax import lax
from jax.experimental import pallas as pl
from jax.experimental.pallas import tpu as pltpu
from jax.sharding import PartitionSpec as P

BS = 256
NR = 8
NC = 16
MESH = pl.DeviceIdType.MESH
HI = lax.Precision.HIGHEST
f32 = jnp.float32
bf16 = jnp.bfloat16
ANY = pl.BlockSpec(memory_space=pl.ANY)
VM = pl.BlockSpec(memory_space=pltpu.VMEM)
SM = pl.BlockSpec(memory_space=pltpu.SMEM)


def dot(a, b, precision=HI):
    return lax.dot_general(
        a, b, (((1,), (0,)), ((), ())), precision=precision, preferred_element_type=f32
    )


def dot_t(a, b, precision=HI):
    return lax.dot_general(
        a, b, (((1,), (1,)), ((), ())), precision=precision, preferred_element_type=f32
    )


def t_dot(a, b, precision=HI):
    return lax.dot_general(
        a, b, (((0,), (0,)), ((), ())), precision=precision, preferred_element_type=f32
    )


def row_of(x, k):
    return jnp.broadcast_to(x[k : k + 1, :], (8, 128))


def lane_of(x, k):
    return jnp.broadcast_to(x[:, k : k + 1], (8, 128))


def factor_128(m_ref, ahead=3):
    sub = lax.broadcasted_iota(jnp.int32, (8, 128), 0)
    lane = lax.broadcasted_iota(jnp.int32, (8, 128), 1)
    held = {}
    for s in range(16):
        last = min(s + ahead + 1, 16)
        for q in range(s, last):
            if q not in held:
                held[q] = (m_ref[8 * q : 8 * q + 8, :128], m_ref[8 * q : 8 * q + 8, 128:])
        left, right = held.pop(s)
        v = [lane_of(left, 8 * s + j) for j in range(8)]
        z = [jnp.where(sub == j, 1.0, 0.0).astype(f32) for j in range(8)]
        scale = jnp.zeros((8, 128), f32)
        rows, inverses = [], []
        for k in range(8):
            root = lax.rsqrt(row_of(v[k], k))
            scale = jnp.where(sub == k, root, scale)
            inverse = root * root
            inverses.append(inverse)
            below = jnp.where(sub > k, v[k], 0.0) * inverse
            row = {}
            for j in range(k + 1, 8):
                row[j] = row_of(v[j], k)
                v[j] = v[j] - below * row[j]
            rows.append(row)
            if k < 7:
                for j in range(k + 1):
                    z[j] = z[j] - below * row_of(z[j], k)
        new_left = z[0] * row_of(left, 0)
        new_right = z[0] * row_of(right, 0)
        for j in range(1, 8):
            new_left = new_left + z[j] * row_of(left, j)
            new_right = new_right + z[j] * row_of(right, j)
        new_left = jnp.where(lane >= 8 * s + sub, new_left, 0.0)
        rows_left = [row_of(new_left, k) for k in range(8)]
        rows_right = [row_of(new_right, k) for k in range(8)]
        for q in range(s + 1, last):
            x, y = held[q]
            w = [lane_of(x, 8 * s + j) for j in range(8)]
            for k in range(8):
                times = w[k] * inverses[k]
                for j in range(k + 1, 8):
                    w[j] = w[j] - times * rows[k][j]
                x = x - times * rows_left[k]
                y = y - times * rows_right[k]
            held[q] = (x, y)
        new_left = new_left * scale
        new_right = new_right * scale
        m_ref[8 * s : 8 * s + 8, :128] = new_left
        m_ref[8 * s : 8 * s + 8, 128:] = new_right
        low = 8 * last
        if low < 128:
            update = t_dot(new_left, jnp.concatenate([new_left, new_right], axis=1))
            m_ref[low:, :] = m_ref[low:, :] - update[low:, :]


def identity(count, dtype=f32):
    row = lax.broadcasted_iota(jnp.int32, (count, count), 0)
    lane = lax.broadcasted_iota(jnp.int32, (count, count), 1)
    return jnp.where(row == lane, 1.0, 0.0).astype(dtype)


def eliminate(wide, small, r_ref, width):
    def step(p, carry):
        at = pl.multiple_of(p * 128, 128)
        small[:, :128] = wide[pl.ds(at, 128), pl.ds(at, 128)]
        small[:, 128:] = identity(128)
        factor_128(small)
        r_ref[:, :width] = dot(small[:, 128:], wide[pl.ds(at, 128), :width])
        wide[pl.ds(at, 128), :width] = r_ref[:, :width]

        def trail(q, carry):
            down = pl.multiple_of(q * 128, 128)
            wide[pl.ds(down, 128), :width] = wide[pl.ds(down, 128), :width] - t_dot(
                r_ref[:, pl.ds(down, 128)], r_ref[:, :width]
            )
            return carry

        lax.fori_loop(p + 1, 4, trail, 0)
        return carry

    lax.fori_loop(0, 4, step, 0)


def first_pivot(x3, wide, small, r_ref):
    for p in range(8):
        wide[64 * p : 64 * p + 64, 0:512] = x3[p, 0]
        wide[64 * p : 64 * p + 64, 512:1024] = x3[p, 1]
    wide[:, 1024:] = identity(512)
    eliminate(wide, small, r_ref, 1536)
    for p in range(8):
        x3[p, 0] = wide[64 * p : 64 * p + 64, 1024:]
        x3[p, 1] = wide[64 * p : 64 * p + 64, 512:1024]


def second_matrix(x3, fm, wide):
    u = wide[:, 512:1024]
    for i in range(2):
        product = t_dot(u[:, 256 * i : 256 * i + 256], u)
        for j in range(2):
            keep = fm[2 + i, 2 + j].astype(f32)
            for p in range(4):
                wide[256 * i + 64 * p : 256 * i + 64 * p + 64, 256 * j : 256 * j + 256] = (
                    x3[4 * i + p, 2, :, 256 * j : 256 * j + 256]
                    - keep * product[64 * p : 64 * p + 64, 256 * j : 256 * j + 256]
                )
    wide[:, 512:1024] = identity(512)


def second_pivot(x3, wide, small, r_ref):
    eliminate(wide, small, r_ref, 1024)
    for p in range(8):
        x3[p, 2] = wide[64 * p : 64 * p + 64, 512:1024]


def exchange_kernel(
    tab, fm, child, front, kids, ar_out, ac_out, xb_out, x3_out, panel,
    blocks, turned, corners, e1s, e1r_0, e1r_1, held_0, held_1, bs, pf, ar, ac, x3, xb, wide, small, r_ref,
    k_s, k_r, e1_s, e1_r, e2_s, e2_r, b_s, b_r, c1_s, c1_r, c2_s, c2_r, c3_s, c3_r,
    d1_s, d1_r, d2_s, d2_r, dz_s, dz_r, x1_s, x1_r, x2_s, x2_r, x3_s, x3_r, here,
):
    r = lax.axis_index("row")
    c = lax.axis_index("col")
    h = c // 2
    core = lax.rem(c, 2)
    sibling = c + 1 - 2 * core
    e1r = (e1r_0, e1r_1)
    held = (held_0, held_1)
    z = r // 4
    y = lax.rem(r, 4)
    partner = lax.rem(r + 4, NR)
    root = (r == 0) & (c == 0)
    barrier = pltpu.get_barrier_semaphore()

    def send(src, dst, ss, rs, row, col):
        return pltpu.make_async_remote_copy(
            src_ref=src, dst_ref=dst, send_sem=ss, recv_sem=rs,
            device_id=(row, col), device_id_type=MESH,
        )

    def move(src, dst, n):
        return pltpu.make_async_copy(src, dst, here.at[n])

    def each(low, high, body):
        def run(i, carry):
            body(i)
            return carry

        lax.fori_loop(low, high, run, 0)

    def when(condition, body):
        pl.when(condition)(body)

    def greet(row, col):
        pl.semaphore_signal(barrier, inc=1, device_id=(row, col), device_id_type=MESH)

    each(1, NR, lambda d: greet(lax.rem(r + d, NR), c))
    each(1, NC, lambda d: greet(r, lax.rem(c + d, NC)))

    @pl.when(c < 2)
    def _():
        each(1, NR, lambda d: greet(lax.rem(r + d, NR), 1 - c))

    @pl.when(c == 0)
    def _():
        move(front.at[pl.ds(0, 4)], pf.at[pl.ds(0, 4)], 0).start()
        move(front.at[pl.ds(4, 4)], pf.at[pl.ds(4, 4)], 3).start()

    for a in range(16):
        blocks[a] = child[:, BS * a : BS * a + BS]

    def turn(a):
        turned[a] = dot_t(identity(BS, bf16), blocks[a], None).astype(bf16)

    when(c < 2, lambda: each(0, 16, turn))
    pl.semaphore_wait(barrier, jnp.where(c < 2, 29, 22))

    @pl.when((c < 2) & jnp.logical_not(root))
    def _():
        send(turned.at[pl.ds(0, 2)], corners.at[2 * r + c], k_s, k_r.at[2 * r + c], 0, 0).start()

    @pl.when(root)
    def _():
        for n in range(2):
            corners[0, n] = turned[n]

    @pl.when(c < 2)
    def _():
        def give(t, d):
            q = lax.rem(r + d, NR)
            for n in range(4):
                bs[t, q, n] = turned[tab[q] + n, 128 * t : 128 * t + 128, :]

            @pl.when((q != r) | (c == 1))
            def _():
                send(
                    bs.at[t, q], held[t].at[pl.ds(8 * r + 4 * c, 4)],
                    b_s.at[8 * t + q], b_r.at[16 * t + 2 * r + c], q, 0,
                ).start()

            @pl.when((q == r) & (c == 0))
            def _():
                for n in range(4):
                    held[t][8 * r + n] = bs[t, q, n]

        for t in range(2):
            each(1, NR + 1, functools.partial(give, t))

    def to_col(m):
        def run(d):
            q = lax.rem(c + d, NC)

            @pl.when((q >= 1) & (q <= h + 8))
            def _():
                @pl.when(q != c)
                def _():
                    e1s[q, m] = blocks[tab[8 + q] + m]
                    send(
                        e1s.at[q, m], e1r[m].at[c], e1_s.at[16 * m + q], e1_r.at[16 * m + c], r, q
                    ).start()

                @pl.when(q == c)
                def _():
                    e1r[m][c] = blocks[tab[8 + q] + m]

        each(1, NC + 1, run)

    def left_col(m):
        each(1, NC, lambda q: when(
            (q <= h + 8) & (q != c), lambda: sent(e1s.at[q, m], e1_s.at[16 * m + q])
        ))

    def sent(buffer, sem):
        send(buffer, buffer, sem, c1_r, r, sibling).wait_send()

    to_col(0)
    when(c == 0, lambda: to_col(1))

    def assemble_panel(give_rows):
        move(front.at[pl.ds(0, 4)], pf.at[pl.ds(0, 4)], 3).wait()

        def arrive(t, k):
            @pl.when(k != 2 * r)
            def _():
                send(
                    bs.at[0, 0], held[t].at[pl.ds(4 * k, 4)],
                    b_s.at[0], b_r.at[16 * t + k], k // 2, lax.rem(k, 2),
                ).wait_recv()

        def assemble(t, i):
            for j in range(4):
                at = pl.ds(j * BS, BS)
                keep = fm[8 * r + i, j].astype(f32)
                pairs = []
                for k in range(NR):
                    pairs.append((
                        (tab[120 + 8 * k + i] * tab[184 + 4 * k + j]).astype(f32),
                        8 * k + 4 * tab[88 + 4 * k + j] + tab[24 + 8 * k + i],
                    ))
                for n in range(2):
                    low = 128 * t + 64 * n
                    total = pf[i, low : low + 64, at]
                    for times, from_slot in pairs:
                        total = total + times * held[t][
                            from_slot, 64 * n : 64 * n + 64, :
                        ].astype(f32)
                    total = total * keep
                    pf[i, low : low + 64, at] = total
                    ar[i, t, 64 * n : 64 * n + 64, at] = total.astype(bf16)
            give_rows(t, i)

        for t in range(2):
            each(0, 16, functools.partial(arrive, t))
            each(0, 8, functools.partial(assemble, t))
        move(pf, panel, 0).start()

    def part(ref, q, t):
        return ref.at[q, pl.ds(2 * t, 2 - t)]

    def pivots_from_root(t):
        each(1, NR, lambda q: send(
            part(x3, q, t), part(x3, q, t), x1_s.at[8 * t + q], x1_r.at[t], q, 0
        ).start())

    def pivots_out(t):
        for n in ((0, 1), (2,))[t]:
            xb[r, n] = x3[r, n].astype(bf16)
        each(1, NC, lambda q: send(
            part(xb, r, t), part(xb, r, t), x2_s.at[16 * t + q], x2_r.at[t], r, q
        ).start())
        each(1, NR, lambda q: when(q != r, lambda: send(
            part(x3, r, t), part(x3, r, t), x3_s.at[12 * t + q], x3_r.at[8 * t + r], q, 0
        ).start()))

    @pl.when(root)
    def _():
        move(front.at[pl.ds(0, 4)], pf.at[pl.ds(0, 4)], 0).wait()
        each(1, 16, lambda k: send(
            turned.at[pl.ds(0, 2)], corners.at[k], k_s, k_r.at[k], k // 2, lax.rem(k, 2)
        ).wait_recv())
        for n, rows, cols in ((0, 0, 0), (1, 0, 2), (2, 2, 2)):

            def corner(i):
                for j in range(2):
                    keep = fm[rows + i, cols + j].astype(f32)
                    pairs = []
                    for k in range(NR):
                        pairs.append((
                            (tab[120 + 8 * k + rows + i] * tab[184 + 4 * k + cols + j]).astype(f32),
                            2 * k + tab[88 + 4 * k + cols + j],
                            tab[24 + 8 * k + rows + i],
                        ))
                    for p in range(4):
                        total = pf[
                            rows + i, 64 * p : 64 * p + 64,
                            BS * (cols + j) : BS * (cols + j) + BS,
                        ]
                        for times, side, slot in pairs:
                            total = total + times * corners[
                                side, slot, 64 * p : 64 * p + 64, :
                            ].astype(f32)
                        x3[4 * i + p, n, :, BS * j : BS * j + BS] = total * keep

            each(0, 2, corner)
        first_pivot(x3, wide, small, r_ref)
        pivots_from_root(0)
        pivots_out(0)
        second_matrix(x3, fm, wide)
        assemble_panel(lambda t, i: send(
            ar.at[i, t], ar.at[i, t], c1_s.at[1], c1_r, 0, 1
        ).start())
        second_pivot(x3, wide, small, r_ref)
        pivots_from_root(1)
        pivots_out(1)

    @pl.when((c == 0) & (r > 0))
    def _():
        move(front.at[pl.ds(0, 4)], pf.at[pl.ds(0, 4)], 0).wait()

        def give_rows(t, i):
            if t == 1:
                send(ar.at[i, 1], ar.at[i, 1], c1_s.at[2 * i + 1], c1_r, r, 2 * i + 1).start()
                return
            send(ar.at[i, 0], ar.at[i, 0], c3_s.at[i], c3_r.at[i], r, 1).start()

            @pl.when(i > 0)
            def _():
                send(ar.at[i, 0], ar.at[i, 0], c1_s.at[2 * i], c1_r, r, 2 * i).start()

            @pl.when(i == 0)
            def _():
                each(1, r + 1, lambda q: send(
                    ar.at[0, 0], ar.at[0, 0], c2_s.at[q], c2_r.at[0], r, 2 * q
                ).start())

        assemble_panel(give_rows)
        for t in range(2):
            send(part(x3, r, t), part(x3, r, t), x1_s.at[0], x1_r.at[t], 0, 0).wait_recv()
            pivots_out(t)

    def to_row(m):
        def arrive(a):
            @pl.when(a != c)
            def _():
                send(
                    e1s.at[0, m], e1r[m].at[a], e1_s.at[0], e1_r.at[16 * m + a], r, a
                ).wait_recv()

        each(jnp.maximum(2 * (c - 8), 0), NC, arrive)

        def run(d):
            q = lax.rem(r + d, NR)
            mine = held[m].at[pl.ds(8 * q, 8)]
            there = kids.at[r, pl.ds(8 * m, 8)]

            @pl.when(q >= h)
            def _():
                for n in range(4):
                    for u in range(2):
                        held[m][8 * q + 2 * n + u] = e1r[m][
                            tab[q] + n, 128 * u : 128 * u + 128, :
                        ]

                @pl.when(q != r)
                def _():
                    send(mine, there, e2_s.at[8 * m + q], e2_r.at[8 * m + r], q, c).start()

                @pl.when(q == r)
                def _():
                    move(mine, there, 5 + m).start()

        for d in (4, 5, 6, 7, 1, 3, 2, 8):
            run(d)

    @pl.when(c > 0)
    def _():
        left_col(0)
        to_col(1)
        to_row(0)
        to_row(1)

    @pl.when((r == 0) & (c == 1))
    def _():
        send(ar, ar, c1_s.at[0], c1_r, 0, 0).wait_recv()

    def across(q):
        @pl.when((c != 1) & (h <= r))
        def _():
            send(ar.at[q, core], ar.at[q, core], c3_s.at[q], c3_r.at[q], r, sibling).start()

    def match_along(ref, row, t):
        def on(d):
            q = 4 * z + lax.rem(y + d, 4)

            @pl.when(q > h)
            def _():
                send(
                    ref.at[row, t], ac.at[y, t],
                    d2_s.at[4 * t + lax.rem(q, 4)], d2_r.at[4 * t + y], q, c,
                ).start()

        each(1, 4, on)

    def match_on(ref, row, t):
        @pl.when(z == 0)
        def _():
            send(ref.at[row, t], ac.at[y, t], dz_s.at[t], dz_r.at[t], partner, c).start()

        match_along(ref, row, t)

    def match_from(t):
        @pl.when((r == h) & (c > 0))
        def _():
            each(1, 4, lambda d: send(
                ar.at[4 * core + lax.rem(y + d, 4), t], ac.at[lax.rem(y + d, 4), t],
                d1_s.at[4 * t + lax.rem(y + d, 4)], d1_r.at[t], 4 * z + lax.rem(y + d, 4), c,
            ).start())
            match_on(ar, 4 * core + y, t)

    def own_half():
        send(ar.at[h, core], ar.at[h, core], c1_s.at[0], c1_r, r, 0).wait_recv()

        def spread(d):
            q = lax.rem(h + d, 8)

            @pl.when((q <= r) & ((q != 0) | (core != 0)))
            def _():
                send(
                    ar.at[h, core], ar.at[h, core], c2_s.at[q], c2_r.at[h], r, 2 * q + core
                ).start()

        each(1, 8, spread)
        across(h)

        def collect(d):
            q = lax.rem(h + d, 8)
            send(
                ar.at[q, core], ar.at[q, core], c2_s.at[q], c2_r.at[q], r, 2 * q + core
            ).wait_recv()
            across(q)

        when(h <= r, lambda: each(1, 8, collect))

    def other_half():
        when(h <= r, lambda: each(0, 8, lambda q: send(
            ar.at[q, 1 - core], ar.at[q, 1 - core], c3_s.at[q], c3_r.at[q], r, sibling
        ).wait_recv()))

    @pl.when((r > 0) & (c > 0) & (core == 0))
    def _():
        own_half()
        match_from(0)
        other_half()
        match_from(1)

    @pl.when((r > 0) & (core == 1))
    def _():
        other_half()
        match_from(0)
        own_half()
        match_from(1)

    @pl.when((r == 0) & (c == 1))
    def _():
        match_from(0)
        match_from(1)

    @pl.when(c > 0)
    def _():
        @pl.when(r >= h)
        def _():
            move(ar, ar_out, 3).start()

        @pl.when(r == h)
        def _():
            move(ar.at[pl.ds(4 * core, 4)], ac_out, 4).start()


        @pl.when((r != h) & (z == h // 4))
        def _():
            for t in range(2):
                send(ac.at[y, t], ac.at[y, t], d1_s.at[0], d1_r.at[t], h, c).wait_recv()
                match_on(ac, y, t)

        @pl.when(z > h // 4)
        def _():
            for t in range(2):
                send(ac.at[y, t], ac.at[y, t], dz_s.at[t], dz_r.at[t], partner, c).wait_recv()
                match_along(ac, y, t)

        def pivots_along(p, t, base):
            each(1, 4, lambda d: send(
                part(xb, p, t), part(xb, p, t), x3_s.at[12 * t + base + lax.rem(y + d, 4)],
                x3_r.at[8 * t + p], 4 * z + lax.rem(y + d, 4), c,
            ).start())

        for t in range(2):
            send(part(xb, r, t), part(xb, r, t), x2_s.at[0], x2_r.at[t], r, 0).wait_recv()
            send(
                part(xb, r, t), part(xb, r, t),
                x3_s.at[12 * t + partner], x3_r.at[8 * t + r], partner, c,
            ).start()
            pivots_along(r, t, 4 * z)
            send(
                part(xb, partner, t), part(xb, partner, t),
                x3_s.at[r], x3_r.at[8 * t + partner], partner, c,
            ).wait_recv()
            pivots_along(partner, t, 8)

        @pl.when(r > h)
        def _():
            for t in range(2):
                each(1, 4, lambda d: send(
                    ac.at[lax.rem(y + d, 4), t], ac.at[lax.rem(y + d, 4), t],
                    d2_s.at[0], d2_r.at[4 * t + lax.rem(y + d, 4)], 4 * z + lax.rem(y + d, 4), c,
                ).wait_recv())
            move(ac, ac_out, 4).start()

        @pl.when(r >= h)
        def _():
            def arrive(q):
                @pl.when(q != r)
                def _():
                    for m in range(2):
                        send(
                            held[m].at[pl.ds(0, 8)], kids.at[q, pl.ds(8 * m, 8)],
                            e2_s.at[0], e2_r.at[8 * m + q], q, c,
                        ).wait_recv()

            each(0, NR, arrive)

        def pieces(q):
            @pl.when((q != r) & (q != partner))
            def _():
                for t in range(2):
                    send(
                        part(xb, q, t), part(xb, q, t), x3_s.at[q], x3_r.at[8 * t + q], q, c
                    ).wait_recv()

        each(0, NR, pieces)
        move(xb, xb_out, 1).start()

    @pl.when(c == 0)
    def _():
        def pieces(q):
            @pl.when((q != r) & (r > 0))
            def _():
                for t in range(2):
                    send(
                        part(x3, q, t), part(x3, q, t), x3_s.at[q], x3_r.at[8 * t + q], q, c
                    ).wait_recv()

        each(0, NR, pieces)
        move(x3, x3_out, 1).start()

    def unless(condition, body):
        pl.when(jnp.logical_not(condition))(body)

    @pl.when(c < 2)
    def _():
        unless(root, lambda: sent(turned.at[pl.ds(0, 2)], k_s))
        for t in range(2):
            each(0, NR, lambda q: when(
                (q != r) | (c == 1), lambda: sent(bs.at[t, q], b_s.at[8 * t + q])
            ))

    when(c == 0, lambda: left_col(0))
    left_col(1)

    @pl.when(c == 0)
    def _():
        move(pf, panel, 0).wait()
        move(x3, x3_out, 1).wait()

        @pl.when(r == 0)
        def _():
            sent(ar, c1_s.at[1])
            for t in range(2):
                each(1, NR, lambda q: sent(part(x3, q, t), x1_s.at[8 * t + q]))

        @pl.when(r > 0)
        def _():
            each(1, NC, lambda q: sent(ar.at[0, 0], c1_s.at[q]))
            each(1, r + 1, lambda q: sent(ar.at[0, 0], c2_s.at[q]))
            each(0, 8, lambda q: sent(ar.at[q, 0], c3_s.at[q]))

        for t in range(2):
            each(1, NC, lambda q: sent(part(xb, 0, t), x2_s.at[16 * t + q]))
            each(1, NR, lambda q: when(
                q != r, lambda: sent(part(x3, 0, t), x3_s.at[12 * t + q])
            ))

    @pl.when(c > 0)
    def _():
        def left_row(q):
            for m in range(2):
                mine = held[m].at[pl.ds(8 * q, 8)]
                when(q != r, lambda: sent(mine, e2_s.at[8 * m + q]))
                when(q == r, lambda: move(mine, kids.at[r, pl.ds(8 * m, 8)], 5 + m).wait())

        each(h, NR, left_row)

        @pl.when(r > 0)
        def _():
            each(0, r + 1, lambda q: when(
                (q != h) & ((q != 0) | (core != 0)), lambda: sent(ar.at[0, 0], c2_s.at[q])
            ))
            when(
                (c != 1) & (h <= r),
                lambda: each(0, 8, lambda q: sent(ar.at[0, 0], c3_s.at[q])),
            )

        for t in range(2):
            sent(part(xb, 0, t), x3_s.at[12 * t + partner])
            for base in (4 * z, 8):
                each(1, 4, lambda d: sent(
                    part(xb, 0, t), x3_s.at[12 * t + base + lax.rem(y + d, 4)]
                ))
        move(xb, xb_out, 1).wait()

        @pl.when(r >= h)
        def _():
            move(ar, ar_out, 3).wait()
            move(ac, ac_out, 4).wait()

        for t in range(2):
            when(r == h, lambda: each(1, 4, lambda d: sent(
                ac.at[0, 0], d1_s.at[4 * t + lax.rem(y + d, 4)]
            )))

        @pl.when(z >= h // 4)
        def _():
            for t in range(2):
                when((z == 0) & (h < 4), lambda: sent(ac.at[0, 0], dz_s.at[t]))
                each(1, 4, lambda d: when(
                    4 * z + lax.rem(y + d, 4) > h,
                    lambda: sent(ac.at[0, 0], d2_s.at[4 * t + lax.rem(y + d, 4)]),
                ))


def exchange(tab, fm, child, front):
    dma = pltpu.SemaphoreType.DMA
    sds = jax.ShapeDtypeStruct
    return pl.pallas_call(
        exchange_kernel,
        in_specs=[SM, SM, VM, ANY],
        out_specs=[ANY] * 6,
        out_shape=[
            sds((NR, 16, 128, BS), bf16),
            sds((8, 2, 128, 1024), bf16),
            sds((4, 2, 128, 1024), bf16),
            sds((8, 3, 64, 512), bf16),
            sds((8, 3, 64, 512), f32),
            sds((8, BS, 1024), f32),
        ],
        scratch_shapes=[
            pltpu.VMEM((16, BS, BS), bf16),
            pltpu.VMEM((16, BS, BS), bf16),
            pltpu.VMEM((16, 2, BS, BS), bf16),
            pltpu.VMEM((NC, 2, BS, BS), bf16),
            pltpu.VMEM((NC, BS, BS), bf16),
            pltpu.VMEM((NC, BS, BS), bf16),
            pltpu.VMEM((64, 128, BS), bf16),
            pltpu.VMEM((64, 128, BS), bf16),
            pltpu.VMEM((2, NR, 4, 128, BS), bf16),
            pltpu.VMEM((8, BS, 1024), f32),
            pltpu.VMEM((8, 2, 128, 1024), bf16),
            pltpu.VMEM((4, 2, 128, 1024), bf16),
            pltpu.VMEM((8, 3, 64, 512), f32),
            pltpu.VMEM((8, 3, 64, 512), bf16),
            pltpu.VMEM((512, 1536), f32),
            pltpu.VMEM((128, 256), f32),
            pltpu.VMEM((128, 1536), f32),
            dma, dma((16,)),
            dma((32,)), dma((32,)), dma((16,)), dma((16,)),
            dma((16,)), dma((32,)),
            dma((NC,)), dma, dma((8,)), dma((8,)), dma((8,)), dma((8,)),
            dma((8,)), dma((2,)), dma((8,)), dma((8,)), dma((2,)), dma((2,)),
            dma((16,)), dma((2,)), dma((32,)), dma((2,)), dma((24,)), dma((16,)), dma((7,)),
        ],
        compiler_params=pltpu.CompilerParams(
            collective_id=1, has_side_effects=True, vmem_limit_bytes=58 << 20
        ),
        cost_estimate=pl.CostEstimate(flops=0, bytes_accessed=400_000_000, transcendentals=0),
        name="exchange",
    )(tab, fm, child, front)


def split(x):
    high = x.astype(bf16)
    return high, (x - high.astype(f32)).astype(bf16)


def update_kernel(
    tab, fm, front, panel, ar, ac, xb, x3, kids_in, out,
    inv0, low, inv1, low0, low1, low2, wc, kids, came,
):
    r = lax.axis_index("row")
    c = lax.axis_index("col")
    i = pl.program_id(0)
    g = 8 * r + i
    active = g >= 4 * c

    def gather(ref, n):
        return jnp.concatenate([ref[p, n] for p in range(8)], axis=0)

    def solve(rows0, rows1, block_row):
        first = dot_t(rows0, inv0[...], None).astype(bf16)
        across = dot(first, low[...], None)
        second = jnp.concatenate(
            [
                rows1[:, BS * j : BS * j + BS].astype(f32)
                - fm[block_row, 2 + j].astype(f32) * across[:, BS * j : BS * j + BS]
                for j in range(2)
            ],
            axis=1,
        ).astype(bf16)
        return first, dot_t(second, inv1[...], None).astype(bf16)

    def thrice(product, x, high, rest):
        a, b = split(x)
        return (
            product(a, high[...], None) + product(a, rest[...], None) + product(b, high[...], None)
        )

    @pl.when((i == 0) & (c > 0) & (c // 2 <= r))
    def _():
        fetch = pltpu.make_async_copy(kids_in, kids, came)
        fetch.start()
        inv0[...] = gather(xb, 0)
        low[...] = gather(xb, 1)
        inv1[...] = gather(xb, 2)
        for j in range(4):
            block = jnp.concatenate([ac[j, 0], ac[j, 1]], axis=0)
            first, second = solve(block[:, :512], block[:, 512:], 4 * c + j)
            wc[BS * j : BS * j + BS, :512] = first
            wc[BS * j : BS * j + BS, 512:] = second
        fetch.wait()

    @pl.when((i == 0) & (c == 0))
    def _():
        for n, (high, rest) in enumerate(((inv0, low0), (low, low1), (inv1, low2))):
            high[...], rest[...] = split(gather(x3, n))

    @pl.when(jnp.logical_not(active))
    def _():
        out[...] = jnp.zeros_like(out)

    @pl.when(active & (c == 0))
    def _():
        first = thrice(dot_t, panel[0, :, :512], inv0, low0)
        across = thrice(dot, first, low, low1)
        second = jnp.concatenate(
            [
                panel[0, :, 512 + BS * j : 768 + BS * j]
                - fm[g, 2 + j].astype(f32) * across[:, BS * j : BS * j + BS]
                for j in range(2)
            ],
            axis=1,
        )
        second = thrice(dot_t, second, inv1, low2)
        row = g * BS + lax.broadcasted_iota(jnp.int32, (BS, 512), 0)
        lane = lax.broadcasted_iota(jnp.int32, (BS, 512), 1)
        out[:, :512] = jnp.where(row >= lane, first, 0.0)
        out[:, 512:] = jnp.where(row >= lane + 512, second, 0.0)

    @pl.when(active & (c > 0))
    def _():
        block = jnp.concatenate([ar[0, 0], ar[0, 1]], axis=0)
        first, second = solve(block[:, :512], block[:, 512:], g)
        for j in range(4):
            at = pl.ds(BS * j, BS)
            keep = (fm[g, 4 * c + j] != 0) & (g >= 4 * c + j)

            @pl.when(keep)
            def _():
                product = dot_t(first, wc[BS * j : BS * j + BS, :512], None) + dot_t(
                    second, wc[BS * j : BS * j + BS, 512:], None
                )
                times = fm[g, 4 * c + j].astype(f32)
                out[:, at] = (front[:, at] - product) * times

                for k in range(NR):
                    slot = tab[24 + 8 * k + i]
                    side = tab[88 + 4 * k + j]

                    @pl.when(tab[120 + 8 * k + i] * tab[184 + 4 * k + j] > 0)
                    def _():
                        for u in range(2):
                            half = pl.ds(128 * u, 128)
                            out[half, at] = out[half, at] + times * kids[
                                k, 8 * side + 2 * slot + u
                            ].astype(f32)

            @pl.when(jnp.logical_not(keep))
            def _():
                out[:, at] = jnp.zeros((BS, BS), f32)


def update(tab, fm, front, panel, ar, ac, xb, x3, kids):
    whole = lambda shape: pl.BlockSpec(
        shape, lambda i: (0,) * len(shape), pipeline_mode=pl.Buffered(1)
    )
    return pl.pallas_call(
        update_kernel,
        grid=(8,),
        in_specs=[
            SM, SM,
            pl.BlockSpec((BS, 1024), lambda i: (i, 0)),
            pl.BlockSpec((1, BS, 1024), lambda i: (i, 0, 0)),
            pl.BlockSpec((1, 2, 128, 1024), lambda i: (i, 0, 0, 0)),
            whole((4, 2, 128, 1024)),
            whole((8, 3, 64, 512)),
            whole((8, 3, 64, 512)),
            ANY,
        ],
        out_specs=pl.BlockSpec((BS, 1024), lambda i: (i, 0)),
        out_shape=jax.ShapeDtypeStruct((2048, 1024), f32),
        scratch_shapes=[pltpu.VMEM((512, 512), bf16)] * 6
        + [
            pltpu.VMEM((1024, 1024), bf16),
            pltpu.VMEM((NR, 16, 128, BS), bf16),
            pltpu.SemaphoreType.DMA,
        ],
        compiler_params=pltpu.CompilerParams(vmem_limit_bytes=48 << 20),
        name="update",
    )(tab, fm, front, panel, ar, ac, xb, x3, kids)


def tables(maps, r, c):
    own = lax.dynamic_index_in_dim(maps, r, 0, keepdims=False)
    row_start = jnp.minimum(jnp.sum(own[:, None] < 8 * jnp.arange(NR), axis=0), 12)
    col_start = jnp.minimum(jnp.sum(own[:, None] < 4 * jnp.arange(NC), axis=0), 14)
    index = jnp.arange(16)
    rows = maps[:, None, :] == 8 * r + jnp.arange(8)[None, :, None]
    row_first = jnp.minimum(jnp.sum(maps < 8 * r, axis=1), 12)
    row_slot = jnp.sum(rows * (index - row_first[:, None, None] + 1), axis=-1) - 1
    cols = maps[:, None, :] == 4 * c + jnp.arange(4)[None, :, None]
    col_first = jnp.minimum(jnp.sum(maps < 4 * c, axis=1), 14)
    col_slot = jnp.sum(cols * (index - col_first[:, None, None] + 1), axis=-1) - 1
    parts = [
        row_start,
        col_start,
        jnp.maximum(row_slot, 0).reshape(-1),
        jnp.maximum(col_slot, 0).reshape(-1),
        (row_slot >= 0).reshape(-1),
        (col_slot >= 0).reshape(-1),
    ]
    return jnp.concatenate([part.astype(jnp.int32) for part in parts])


def local(front, child_updates, child_maps, fill_mask):
    r = lax.axis_index("row")
    c = lax.axis_index("col")
    tab = tables(child_maps, r, c)
    kids, ar, ac, xb, x3, panel = exchange(
        tab, fill_mask, child_updates[0], front.reshape(8, BS, 1024)
    )
    return update(tab, fill_mask, front, panel, ar, ac, xb, x3, kids)


def solution(mesh):
    placed = (P("row", "col"), P("row", "col", None), P(), P())
    return jax.shard_map(
        local, mesh=mesh, in_specs=placed, out_specs=P("row", "col"), check_vma=False
    )
```

```python
import functools

import jax
import jax.numpy as jnp
import numpy as np
from jax import lax
from jax.experimental import pallas as pl
from jax.experimental.pallas import tpu as pltpu
from jax.sharding import PartitionSpec as P

BS = 256
NR = 8
NC = 16
MESH = pl.DeviceIdType.MESH
HI = lax.Precision.HIGHEST
f32 = jnp.float32
bf16 = jnp.bfloat16
ANY = pl.BlockSpec(memory_space=pl.ANY)
VM = pl.BlockSpec(memory_space=pltpu.VMEM)
SM = pl.BlockSpec(memory_space=pltpu.SMEM)


def dot(a, b, precision=HI):
    return lax.dot_general(
        a, b, (((1,), (0,)), ((), ())), precision=precision, preferred_element_type=f32
    )


def dot_t(a, b, precision=HI):
    return lax.dot_general(
        a, b, (((1,), (1,)), ((), ())), precision=precision, preferred_element_type=f32
    )


def t_dot(a, b, precision=HI):
    return lax.dot_general(
        a, b, (((0,), (0,)), ((), ())), precision=precision, preferred_element_type=f32
    )


def row_of(x, k):
    return jnp.broadcast_to(x[k : k + 1, :], (8, 128))


def lane_of(x, k):
    return jnp.broadcast_to(x[:, k : k + 1], (8, 128))


def factor_128(m_ref, ahead=3):
    sub = lax.broadcasted_iota(jnp.int32, (8, 128), 0)
    lane = lax.broadcasted_iota(jnp.int32, (8, 128), 1)
    held = {}
    for s in range(16):
        last = min(s + ahead + 1, 16)
        for q in range(s, last):
            if q not in held:
                held[q] = (m_ref[8 * q : 8 * q + 8, :128], m_ref[8 * q : 8 * q + 8, 128:])
        left, right = held.pop(s)
        v = [lane_of(left, 8 * s + j) for j in range(8)]
        z = [jnp.where(sub == j, 1.0, 0.0).astype(f32) for j in range(8)]
        scale = jnp.zeros((8, 128), f32)
        rows, inverses = [], []
        for k in range(8):
            root = lax.rsqrt(row_of(v[k], k))
            scale = jnp.where(sub == k, root, scale)
            inverse = root * root
            inverses.append(inverse)
            below = jnp.where(sub > k, v[k], 0.0) * inverse
            row = {}
            for j in range(k + 1, 8):
                row[j] = row_of(v[j], k)
                v[j] = v[j] - below * row[j]
            rows.append(row)
            if k < 7:
                for j in range(k + 1):
                    z[j] = z[j] - below * row_of(z[j], k)
        new_left = z[0] * row_of(left, 0)
        new_right = z[0] * row_of(right, 0)
        for j in range(1, 8):
            new_left = new_left + z[j] * row_of(left, j)
            new_right = new_right + z[j] * row_of(right, j)
        new_left = jnp.where(lane >= 8 * s + sub, new_left, 0.0)
        rows_left = [row_of(new_left, k) for k in range(8)]
        rows_right = [row_of(new_right, k) for k in range(8)]
        for q in range(s + 1, last):
            x, y = held[q]
            w = [lane_of(x, 8 * s + j) for j in range(8)]
            for k in range(8):
                times = w[k] * inverses[k]
                for j in range(k + 1, 8):
                    w[j] = w[j] - times * rows[k][j]
                x = x - times * rows_left[k]
                y = y - times * rows_right[k]
            held[q] = (x, y)
        new_left = new_left * scale
        new_right = new_right * scale
        m_ref[8 * s : 8 * s + 8, :128] = new_left
        m_ref[8 * s : 8 * s + 8, 128:] = new_right
        low = 8 * last
        if low < 128:
            update = t_dot(new_left, jnp.concatenate([new_left, new_right], axis=1))
            m_ref[low:, :] = m_ref[low:, :] - update[low:, :]


def identity(count, dtype=f32):
    row = lax.broadcasted_iota(jnp.int32, (count, count), 0)
    lane = lax.broadcasted_iota(jnp.int32, (count, count), 1)
    return jnp.where(row == lane, 1.0, 0.0).astype(dtype)


def eliminate(wide, small, r_ref, width):
    def step(p, carry):
        at = pl.multiple_of(p * 128, 128)
        small[:, :128] = wide[pl.ds(at, 128), pl.ds(at, 128)]
        small[:, 128:] = identity(128)
        factor_128(small)
        r_ref[:, :width] = dot(small[:, 128:], wide[pl.ds(at, 128), :width])
        wide[pl.ds(at, 128), :width] = r_ref[:, :width]

        def trail(q, carry):
            down = pl.multiple_of(q * 128, 128)
            wide[pl.ds(down, 128), :width] = wide[pl.ds(down, 128), :width] - t_dot(
                r_ref[:, pl.ds(down, 128)], r_ref[:, :width]
            )
            return carry

        lax.fori_loop(p + 1, 4, trail, 0)
        return carry

    lax.fori_loop(0, 4, step, 0)


def first_pivot(x3, wide, small, r_ref):
    for p in range(8):
        wide[64 * p : 64 * p + 64, 0:512] = x3[p, 0]
        wide[64 * p : 64 * p + 64, 512:1024] = x3[p, 1]
    wide[:, 1024:] = identity(512)
    eliminate(wide, small, r_ref, 1536)
    for p in range(8):
        x3[p, 0] = wide[64 * p : 64 * p + 64, 1024:]
        x3[p, 1] = wide[64 * p : 64 * p + 64, 512:1024]


def second_matrix(x3, fm, wide):
    u = wide[:, 512:1024]
    for i in range(2):
        product = t_dot(u[:, 256 * i : 256 * i + 256], u)
        for j in range(2):
            keep = fm[2 + i, 2 + j].astype(f32)
            for p in range(4):
                wide[256 * i + 64 * p : 256 * i + 64 * p + 64, 256 * j : 256 * j + 256] = (
                    x3[4 * i + p, 2, :, 256 * j : 256 * j + 256]
                    - keep * product[64 * p : 64 * p + 64, 256 * j : 256 * j + 256]
                )
    wide[:, 512:1024] = identity(512)


def second_pivot(x3, wide, small, r_ref):
    eliminate(wide, small, r_ref, 1024)
    for p in range(8):
        x3[p, 2] = wide[64 * p : 64 * p + 64, 512:1024]


def exchange_kernel(
    tab, fm, child, front, kids, ar_out, ac_out, xb_out, x3_out, panel,
    blocks, turned, corners, e1s, e1r_0, e1r_1, held_0, held_1, bs, pf, ar, ac, x3, xb, wide, small, r_ref,
    k_s, k_r, e1_s, e1_r, e2_s, e2_r, b_s, b_r, c1_s, c1_r, c2_s, c2_r, c3_s, c3_r,
    d1_s, d1_r, d2_s, d2_r, dz_s, dz_r, x1_s, x1_r, x2_s, x2_r, x3_s, x3_r, here,
):
    r = lax.axis_index("row")
    c = lax.axis_index("col")
    h = c // 2
    core = lax.rem(c, 2)
    sibling = c + 1 - 2 * core
    e1r = (e1r_0, e1r_1)
    held = (held_0, held_1)
    z = r // 4
    y = lax.rem(r, 4)
    partner = lax.rem(r + 4, NR)
    root = (r == 0) & (c == 0)
    barrier = pltpu.get_barrier_semaphore()

    def send(src, dst, ss, rs, row, col):
        return pltpu.make_async_remote_copy(
            src_ref=src, dst_ref=dst, send_sem=ss, recv_sem=rs,
            device_id=(row, col), device_id_type=MESH,
        )

    def move(src, dst, n):
        return pltpu.make_async_copy(src, dst, here.at[n])

    def each(low, high, body):
        def run(i, carry):
            body(i)
            return carry

        lax.fori_loop(low, high, run, 0)

    def when(condition, body):
        pl.when(condition)(body)

    def greet(row, col):
        pl.semaphore_signal(barrier, inc=1, device_id=(row, col), device_id_type=MESH)

    each(1, NR, lambda d: greet(lax.rem(r + d, NR), c))
    each(1, NC, lambda d: greet(r, lax.rem(c + d, NC)))

    @pl.when(c < 2)
    def _():
        each(1, NR, lambda d: greet(lax.rem(r + d, NR), 1 - c))

    @pl.when(c == 0)
    def _():
        move(front.at[pl.ds(0, 4)], pf.at[pl.ds(0, 4)], 0).start()
        move(front.at[pl.ds(4, 4)], pf.at[pl.ds(4, 4)], 3).start()

    for a in range(16):
        blocks[a] = child[:, BS * a : BS * a + BS]

    def turn(a):
        turned[a] = dot_t(identity(BS, bf16), blocks[a], None).astype(bf16)

    when(c < 2, lambda: each(0, 16, turn))
    pl.semaphore_wait(barrier, jnp.where(c < 2, 29, 22))

    @pl.when((c < 2) & jnp.logical_not(root))
    def _():
        send(turned.at[pl.ds(0, 2)], corners.at[2 * r + c], k_s, k_r.at[2 * r + c], 0, 0).start()

    @pl.when(root)
    def _():
        for n in range(2):
            corners[0, n] = turned[n]

    @pl.when(c < 2)
    def _():
        def give(t, d):
            q = lax.rem(r + d, NR)
            for n in range(4):
                bs[t, q, n] = turned[tab[q] + n, 128 * t : 128 * t + 128, :]

            @pl.when((q != r) | (c == 1))
            def _():
                send(
                    bs.at[t, q], held[t].at[pl.ds(8 * r + 4 * c, 4)],
                    b_s.at[8 * t + q], b_r.at[16 * t + 2 * r + c], q, 0,
                ).start()

            @pl.when((q == r) & (c == 0))
            def _():
                for n in range(4):
                    held[t][8 * r + n] = bs[t, q, n]

        for t in range(2):
            each(1, NR + 1, functools.partial(give, t))

    def to_col(m):
        def run(d):
            q = lax.rem(c + d, NC)

            @pl.when((q >= 1) & (q <= h + 8))
            def _():
                @pl.when(q != c)
                def _():
                    e1s[q, m] = blocks[tab[8 + q] + m]
                    send(
                        e1s.at[q, m], e1r[m].at[c], e1_s.at[16 * m + q], e1_r.at[16 * m + c], r, q
                    ).start()

                @pl.when(q == c)
                def _():
                    e1r[m][c] = blocks[tab[8 + q] + m]

        each(1, NC + 1, run)

    def left_col(m):
        each(1, NC, lambda q: when(
            (q <= h + 8) & (q != c), lambda: sent(e1s.at[q, m], e1_s.at[16 * m + q])
        ))

    def sent(buffer, sem):
        send(buffer, buffer, sem, c1_r, r, sibling).wait_send()

    to_col(0)
    when(c == 0, lambda: to_col(1))

    def assemble_panel(give_rows):
        move(front.at[pl.ds(0, 4)], pf.at[pl.ds(0, 4)], 3).wait()

        def arrive(t, k):
            @pl.when(k != 2 * r)
            def _():
                send(
                    bs.at[0, 0], held[t].at[pl.ds(4 * k, 4)],
                    b_s.at[0], b_r.at[16 * t + k], k // 2, lax.rem(k, 2),
                ).wait_recv()

        def assemble(t, i):
            for j in range(4):
                at = pl.ds(j * BS, BS)
                keep = fm[8 * r + i, j].astype(f32)
                pairs = []
                for k in range(NR):
                    pairs.append((
                        (tab[120 + 8 * k + i] * tab[184 + 4 * k + j]).astype(f32),
                        8 * k + 4 * tab[88 + 4 * k + j] + tab[24 + 8 * k + i],
                    ))
                for n in range(2):
                    low = 128 * t + 64 * n
                    total = pf[i, low : low + 64, at]
                    for times, from_slot in pairs:
                        total = total + times * held[t][
                            from_slot, 64 * n : 64 * n + 64, :
                        ].astype(f32)
                    total = total * keep
                    pf[i, low : low + 64, at] = total
                    ar[i, t, 64 * n : 64 * n + 64, at] = total.astype(bf16)
            give_rows(t, i)

        for t in range(2):
            each(0, 16, functools.partial(arrive, t))
            each(0, 8, functools.partial(assemble, t))
        move(pf, panel, 0).start()

    def part(ref, q, t):
        return ref.at[q, pl.ds(2 * t, 2 - t)]

    def pivots_from_root(t):
        each(1, NR, lambda q: send(
            part(x3, q, t), part(x3, q, t), x1_s.at[8 * t + q], x1_r.at[t], q, 0
        ).start())

    def pivots_out(t):
        for n in ((0, 1), (2,))[t]:
            xb[r, n] = x3[r, n].astype(bf16)
        each(1, NC, lambda q: send(
            part(xb, r, t), part(xb, r, t), x2_s.at[16 * t + q], x2_r.at[t], r, q
        ).start())
        each(1, NR, lambda q: when(q != r, lambda: send(
            part(x3, r, t), part(x3, r, t), x3_s.at[12 * t + q], x3_r.at[8 * t + r], q, 0
        ).start()))

    @pl.when(root)
    def _():
        move(front.at[pl.ds(0, 4)], pf.at[pl.ds(0, 4)], 0).wait()
        each(1, 16, lambda k: send(
            turned.at[pl.ds(0, 2)], corners.at[k], k_s, k_r.at[k], k // 2, lax.rem(k, 2)
        ).wait_recv())
        for n, rows, cols in ((0, 0, 0), (1, 0, 2), (2, 2, 2)):

            def corner(i):
                for j in range(2):
                    keep = fm[rows + i, cols + j].astype(f32)
                    pairs = []
                    for k in range(NR):
                        pairs.append((
                            (tab[120 + 8 * k + rows + i] * tab[184 + 4 * k + cols + j]).astype(f32),
                            2 * k + tab[88 + 4 * k + cols + j],
                            tab[24 + 8 * k + rows + i],
                        ))
                    for p in range(4):
                        total = pf[
                            rows + i, 64 * p : 64 * p + 64,
                            BS * (cols + j) : BS * (cols + j) + BS,
                        ]
                        for times, side, slot in pairs:
                            total = total + times * corners[
                                side, slot, 64 * p : 64 * p + 64, :
                            ].astype(f32)
                        x3[4 * i + p, n, :, BS * j : BS * j + BS] = total * keep

            each(0, 2, corner)
        first_pivot(x3, wide, small, r_ref)
        pivots_from_root(0)
        pivots_out(0)
        second_matrix(x3, fm, wide)
        assemble_panel(lambda t, i: send(
            ar.at[i, t], ar.at[i, t], c1_s.at[1], c1_r, 0, 1
        ).start())
        second_pivot(x3, wide, small, r_ref)
        pivots_from_root(1)
        pivots_out(1)

    @pl.when((c == 0) & (r > 0))
    def _():
        move(front.at[pl.ds(0, 4)], pf.at[pl.ds(0, 4)], 0).wait()

        def give_rows(t, i):
            if t == 1:
                send(ar.at[i, 1], ar.at[i, 1], c1_s.at[2 * i + 1], c1_r, r, 2 * i + 1).start()
                return
            send(ar.at[i, 0], ar.at[i, 0], c3_s.at[i], c3_r.at[i], r, 1).start()

            @pl.when(i > 0)
            def _():
                send(ar.at[i, 0], ar.at[i, 0], c1_s.at[2 * i], c1_r, r, 2 * i).start()

            @pl.when(i == 0)
            def _():
                each(1, r + 1, lambda q: send(
                    ar.at[0, 0], ar.at[0, 0], c2_s.at[q], c2_r.at[0], r, 2 * q
                ).start())

        assemble_panel(give_rows)
        for t in range(2):
            send(part(x3, r, t), part(x3, r, t), x1_s.at[0], x1_r.at[t], 0, 0).wait_recv()
            pivots_out(t)

    def to_row(m):
        def arrive(a):
            @pl.when(a != c)
            def _():
                send(
                    e1s.at[0, m], e1r[m].at[a], e1_s.at[0], e1_r.at[16 * m + a], r, a
                ).wait_recv()

        each(jnp.maximum(2 * (c - 8), 0), NC, arrive)

        def run(d):
            q = lax.rem(r + d, NR)
            mine = held[m].at[pl.ds(8 * q, 8)]
            there = kids.at[r, pl.ds(8 * m, 8)]

            @pl.when(q >= h)
            def _():
                for n in range(4):
                    for u in range(2):
                        held[m][8 * q + 2 * n + u] = e1r[m][
                            tab[q] + n, 128 * u : 128 * u + 128, :
                        ]

                @pl.when(q != r)
                def _():
                    send(mine, there, e2_s.at[8 * m + q], e2_r.at[8 * m + r], q, c).start()

                @pl.when(q == r)
                def _():
                    move(mine, there, 5 + m).start()

        for d in (4, 5, 6, 7, 1, 3, 2, 8):
            run(d)

    @pl.when(c > 0)
    def _():
        left_col(0)
        to_col(1)
        to_row(0)
        to_row(1)

    @pl.when((r == 0) & (c == 1))
    def _():
        send(ar, ar, c1_s.at[0], c1_r, 0, 0).wait_recv()

    def across(q):
        @pl.when((c != 1) & (h <= r))
        def _():
            send(ar.at[q, core], ar.at[q, core], c3_s.at[q], c3_r.at[q], r, sibling).start()

    def match_along(ref, row, t):
        def on(d):
            q = 4 * z + lax.rem(y + d, 4)

            @pl.when(q > h)
            def _():
                send(
                    ref.at[row, t], ac.at[y, t],
                    d2_s.at[4 * t + lax.rem(q, 4)], d2_r.at[4 * t + y], q, c,
                ).start()

        each(1, 4, on)

    def match_on(ref, row, t):
        @pl.when(z == 0)
        def _():
            send(ref.at[row, t], ac.at[y, t], dz_s.at[t], dz_r.at[t], partner, c).start()

        match_along(ref, row, t)

    def match_from(t):
        @pl.when((r == h) & (c > 0))
        def _():
            each(1, 4, lambda d: send(
                ar.at[4 * core + lax.rem(y + d, 4), t], ac.at[lax.rem(y + d, 4), t],
                d1_s.at[4 * t + lax.rem(y + d, 4)], d1_r.at[t], 4 * z + lax.rem(y + d, 4), c,
            ).start())
            match_on(ar, 4 * core + y, t)

    def own_half():
        send(ar.at[h, core], ar.at[h, core], c1_s.at[0], c1_r, r, 0).wait_recv()

        def spread(d):
            q = lax.rem(h + d, 8)

            @pl.when((q <= r) & ((q != 0) | (core != 0)))
            def _():
                send(
                    ar.at[h, core], ar.at[h, core], c2_s.at[q], c2_r.at[h], r, 2 * q + core
                ).start()

        each(1, 8, spread)
        across(h)

        def collect(d):
            q = lax.rem(h + d, 8)
            send(
                ar.at[q, core], ar.at[q, core], c2_s.at[q], c2_r.at[q], r, 2 * q + core
            ).wait_recv()
            across(q)

        when(h <= r, lambda: each(1, 8, collect))

    def other_half():
        when(h <= r, lambda: each(0, 8, lambda q: send(
            ar.at[q, 1 - core], ar.at[q, 1 - core], c3_s.at[q], c3_r.at[q], r, sibling
        ).wait_recv()))

    @pl.when((r > 0) & (c > 0) & (core == 0))
    def _():
        own_half()
        match_from(0)
        other_half()
        match_from(1)

    @pl.when((r > 0) & (core == 1))
    def _():
        other_half()
        match_from(0)
        own_half()
        match_from(1)

    @pl.when((r == 0) & (c == 1))
    def _():
        match_from(0)
        match_from(1)

    @pl.when(c > 0)
    def _():
        @pl.when(r >= h)
        def _():
            move(ar, ar_out, 3).start()

        @pl.when(r == h)
        def _():
            move(ar.at[pl.ds(4 * core, 4)], ac_out, 4).start()


        @pl.when((r != h) & (z == h // 4))
        def _():
            for t in range(2):
                send(ac.at[y, t], ac.at[y, t], d1_s.at[0], d1_r.at[t], h, c).wait_recv()
                match_on(ac, y, t)

        @pl.when(z > h // 4)
        def _():
            for t in range(2):
                send(ac.at[y, t], ac.at[y, t], dz_s.at[t], dz_r.at[t], partner, c).wait_recv()
                match_along(ac, y, t)

        def pivots_along(p, t, base):
            each(1, 4, lambda d: send(
                part(xb, p, t), part(xb, p, t), x3_s.at[12 * t + base + lax.rem(y + d, 4)],
                x3_r.at[8 * t + p], 4 * z + lax.rem(y + d, 4), c,
            ).start())

        for t in range(2):
            send(part(xb, r, t), part(xb, r, t), x2_s.at[0], x2_r.at[t], r, 0).wait_recv()
            send(
                part(xb, r, t), part(xb, r, t),
                x3_s.at[12 * t + partner], x3_r.at[8 * t + r], partner, c,
            ).start()
            pivots_along(r, t, 4 * z)
            send(
                part(xb, partner, t), part(xb, partner, t),
                x3_s.at[r], x3_r.at[8 * t + partner], partner, c,
            ).wait_recv()
            pivots_along(partner, t, 8)

        @pl.when(r > h)
        def _():
            for t in range(2):
                each(1, 4, lambda d: send(
                    ac.at[lax.rem(y + d, 4), t], ac.at[lax.rem(y + d, 4), t],
                    d2_s.at[0], d2_r.at[4 * t + lax.rem(y + d, 4)], 4 * z + lax.rem(y + d, 4), c,
                ).wait_recv())
            move(ac, ac_out, 4).start()

        @pl.when(r >= h)
        def _():
            def arrive(q):
                @pl.when(q != r)
                def _():
                    for m in range(2):
                        send(
                            held[m].at[pl.ds(0, 8)], kids.at[q, pl.ds(8 * m, 8)],
                            e2_s.at[0], e2_r.at[8 * m + q], q, c,
                        ).wait_recv()

            each(0, NR, arrive)

        def pieces(q):
            @pl.when((q != r) & (q != partner))
            def _():
                for t in range(2):
                    send(
                        part(xb, q, t), part(xb, q, t), x3_s.at[q], x3_r.at[8 * t + q], q, c
                    ).wait_recv()

        each(0, NR, pieces)
        move(xb, xb_out, 1).start()

    @pl.when(c == 0)
    def _():
        def pieces(q):
            @pl.when((q != r) & (r > 0))
            def _():
                for t in range(2):
                    send(
                        part(x3, q, t), part(x3, q, t), x3_s.at[q], x3_r.at[8 * t + q], q, c
                    ).wait_recv()

        each(0, NR, pieces)
        move(x3, x3_out, 1).start()

    def unless(condition, body):
        pl.when(jnp.logical_not(condition))(body)

    @pl.when(c < 2)
    def _():
        unless(root, lambda: sent(turned.at[pl.ds(0, 2)], k_s))
        for t in range(2):
            each(0, NR, lambda q: when(
                (q != r) | (c == 1), lambda: sent(bs.at[t, q], b_s.at[8 * t + q])
            ))

    when(c == 0, lambda: left_col(0))
    left_col(1)

    @pl.when(c == 0)
    def _():
        move(pf, panel, 0).wait()
        move(x3, x3_out, 1).wait()

        @pl.when(r == 0)
        def _():
            sent(ar, c1_s.at[1])
            for t in range(2):
                each(1, NR, lambda q: sent(part(x3, q, t), x1_s.at[8 * t + q]))

        @pl.when(r > 0)
        def _():
            each(1, NC, lambda q: sent(ar.at[0, 0], c1_s.at[q]))
            each(1, r + 1, lambda q: sent(ar.at[0, 0], c2_s.at[q]))
            each(0, 8, lambda q: sent(ar.at[q, 0], c3_s.at[q]))

        for t in range(2):
            each(1, NC, lambda q: sent(part(xb, 0, t), x2_s.at[16 * t + q]))
            each(1, NR, lambda q: when(
                q != r, lambda: sent(part(x3, 0, t), x3_s.at[12 * t + q])
            ))

    @pl.when(c > 0)
    def _():
        def left_row(q):
            for m in range(2):
                mine = held[m].at[pl.ds(8 * q, 8)]
                when(q != r, lambda: sent(mine, e2_s.at[8 * m + q]))
                when(q == r, lambda: move(mine, kids.at[r, pl.ds(8 * m, 8)], 5 + m).wait())

        each(h, NR, left_row)

        @pl.when(r > 0)
        def _():
            each(0, r + 1, lambda q: when(
                (q != h) & ((q != 0) | (core != 0)), lambda: sent(ar.at[0, 0], c2_s.at[q])
            ))
            when(
                (c != 1) & (h <= r),
                lambda: each(0, 8, lambda q: sent(ar.at[0, 0], c3_s.at[q])),
            )

        for t in range(2):
            sent(part(xb, 0, t), x3_s.at[12 * t + partner])
            for base in (4 * z, 8):
                each(1, 4, lambda d: sent(
                    part(xb, 0, t), x3_s.at[12 * t + base + lax.rem(y + d, 4)]
                ))
        move(xb, xb_out, 1).wait()

        @pl.when(r >= h)
        def _():
            move(ar, ar_out, 3).wait()
            move(ac, ac_out, 4).wait()

        for t in range(2):
            when(r == h, lambda: each(1, 4, lambda d: sent(
                ac.at[0, 0], d1_s.at[4 * t + lax.rem(y + d, 4)]
            )))

        @pl.when(z >= h // 4)
        def _():
            for t in range(2):
                when((z == 0) & (h < 4), lambda: sent(ac.at[0, 0], dz_s.at[t]))
                each(1, 4, lambda d: when(
                    4 * z + lax.rem(y + d, 4) > h,
                    lambda: sent(ac.at[0, 0], d2_s.at[4 * t + lax.rem(y + d, 4)]),
                ))


def exchange(tab, fm, child, front):
    dma = pltpu.SemaphoreType.DMA
    sds = jax.ShapeDtypeStruct
    return pl.pallas_call(
        exchange_kernel,
        in_specs=[SM, SM, VM, ANY],
        out_specs=[ANY] * 6,
        out_shape=[
            sds((NR, 16, 128, BS), bf16),
            sds((8, 2, 128, 1024), bf16),
            sds((4, 2, 128, 1024), bf16),
            sds((8, 3, 64, 512), bf16),
            sds((8, 3, 64, 512), f32),
            sds((8, BS, 1024), f32),
        ],
        scratch_shapes=[
            pltpu.VMEM((16, BS, BS), bf16),
            pltpu.VMEM((16, BS, BS), bf16),
            pltpu.VMEM((16, 2, BS, BS), bf16),
            pltpu.VMEM((NC, 2, BS, BS), bf16),
            pltpu.VMEM((NC, BS, BS), bf16),
            pltpu.VMEM((NC, BS, BS), bf16),
            pltpu.VMEM((64, 128, BS), bf16),
            pltpu.VMEM((64, 128, BS), bf16),
            pltpu.VMEM((2, NR, 4, 128, BS), bf16),
            pltpu.VMEM((8, BS, 1024), f32),
            pltpu.VMEM((8, 2, 128, 1024), bf16),
            pltpu.VMEM((4, 2, 128, 1024), bf16),
            pltpu.VMEM((8, 3, 64, 512), f32),
            pltpu.VMEM((8, 3, 64, 512), bf16),
            pltpu.VMEM((512, 1536), f32),
            pltpu.VMEM((128, 256), f32),
            pltpu.VMEM((128, 1536), f32),
            dma, dma((16,)),
            dma((32,)), dma((32,)), dma((16,)), dma((16,)),
            dma((16,)), dma((32,)),
            dma((NC,)), dma, dma((8,)), dma((8,)), dma((8,)), dma((8,)),
            dma((8,)), dma((2,)), dma((8,)), dma((8,)), dma((2,)), dma((2,)),
            dma((16,)), dma((2,)), dma((32,)), dma((2,)), dma((24,)), dma((16,)), dma((7,)),
        ],
        compiler_params=pltpu.CompilerParams(
            collective_id=1, has_side_effects=True, vmem_limit_bytes=58 << 20
        ),
        cost_estimate=pl.CostEstimate(flops=0, bytes_accessed=400_000_000, transcendentals=0),
        name="exchange",
    )(tab, fm, child, front)


def split(x):
    high = x.astype(bf16)
    return high, (x - high.astype(f32)).astype(bf16)


def update_kernel(
    tab, fm, front, panel, ar, ac, xb, x3, kids_in, out,
    inv0, low, inv1, low0, low1, low2, wc, kids, came,
):
    r = lax.axis_index("row")
    c = lax.axis_index("col")
    i = pl.program_id(0)
    g = 8 * r + i
    active = g >= 4 * c

    def gather(ref, n):
        return jnp.concatenate([ref[p, n] for p in range(8)], axis=0)

    def solve(rows0, rows1, block_row):
        first = dot_t(rows0, inv0[...], None).astype(bf16)
        across = dot(first, low[...], None)
        second = jnp.concatenate(
            [
                rows1[:, BS * j : BS * j + BS].astype(f32)
                - fm[block_row, 2 + j].astype(f32) * across[:, BS * j : BS * j + BS]
                for j in range(2)
            ],
            axis=1,
        ).astype(bf16)
        return first, dot_t(second, inv1[...], None).astype(bf16)

    def thrice(product, x, high, rest):
        a, b = split(x)
        return (
            product(a, high[...], None) + product(a, rest[...], None) + product(b, high[...], None)
        )

    @pl.when((i == 0) & (c > 0) & (c // 2 <= r))
    def _():
        fetch = pltpu.make_async_copy(kids_in, kids, came)
        fetch.start()
        inv0[...] = gather(xb, 0)
        low[...] = gather(xb, 1)
        inv1[...] = gather(xb, 2)
        for j in range(4):
            block = jnp.concatenate([ac[j, 0], ac[j, 1]], axis=0)
            first, second = solve(block[:, :512], block[:, 512:], 4 * c + j)
            wc[BS * j : BS * j + BS, :512] = first
            wc[BS * j : BS * j + BS, 512:] = second
        fetch.wait()

    @pl.when((i == 0) & (c == 0))
    def _():
        for n, (high, rest) in enumerate(((inv0, low0), (low, low1), (inv1, low2))):
            high[...], rest[...] = split(gather(x3, n))

    @pl.when(jnp.logical_not(active))
    def _():
        out[...] = jnp.zeros_like(out)

    @pl.when(active & (c == 0))
    def _():
        first = thrice(dot_t, panel[0, :, :512], inv0, low0)
        across = thrice(dot, first, low, low1)
        second = jnp.concatenate(
            [
                panel[0, :, 512 + BS * j : 768 + BS * j]
                - fm[g, 2 + j].astype(f32) * across[:, BS * j : BS * j + BS]
                for j in range(2)
            ],
            axis=1,
        )
        second = thrice(dot_t, second, inv1, low2)
        row = g * BS + lax.broadcasted_iota(jnp.int32, (BS, 512), 0)
        lane = lax.broadcasted_iota(jnp.int32, (BS, 512), 1)
        out[:, :512] = jnp.where(row >= lane, first, 0.0)
        out[:, 512:] = jnp.where(row >= lane + 512, second, 0.0)

    @pl.when(active & (c > 0))
    def _():
        block = jnp.concatenate([ar[0, 0], ar[0, 1]], axis=0)
        first, second = solve(block[:, :512], block[:, 512:], g)
        for j in range(4):
            at = pl.ds(BS * j, BS)
            keep = (fm[g, 4 * c + j] != 0) & (g >= 4 * c + j)

            @pl.when(keep)
            def _():
                product = dot_t(first, wc[BS * j : BS * j + BS, :512], None) + dot_t(
                    second, wc[BS * j : BS * j + BS, 512:], None
                )
                times = fm[g, 4 * c + j].astype(f32)
                out[:, at] = (front[:, at] - product) * times

                for k in range(NR):
                    slot = tab[24 + 8 * k + i]
                    side = tab[88 + 4 * k + j]

                    @pl.when(tab[120 + 8 * k + i] * tab[184 + 4 * k + j] > 0)
                    def _():
                        for u in range(2):
                            half = pl.ds(128 * u, 128)
                            out[half, at] = out[half, at] + times * kids[
                                k, 8 * side + 2 * slot + u
                            ].astype(f32)

            @pl.when(jnp.logical_not(keep))
            def _():
                out[:, at] = jnp.zeros((BS, BS), f32)


def update(tab, fm, front, panel, ar, ac, xb, x3, kids):
    whole = lambda shape: pl.BlockSpec(
        shape, lambda i: (0,) * len(shape), pipeline_mode=pl.Buffered(1)
    )
    return pl.pallas_call(
        update_kernel,
        grid=(8,),
        in_specs=[
            SM, SM,
            pl.BlockSpec((BS, 1024), lambda i: (i, 0)),
            pl.BlockSpec((1, BS, 1024), lambda i: (i, 0, 0)),
            pl.BlockSpec((1, 2, 128, 1024), lambda i: (i, 0, 0, 0)),
            whole((4, 2, 128, 1024)),
            whole((8, 3, 64, 512)),
            whole((8, 3, 64, 512)),
            ANY,
        ],
        out_specs=pl.BlockSpec((BS, 1024), lambda i: (i, 0)),
        out_shape=jax.ShapeDtypeStruct((2048, 1024), f32),
        scratch_shapes=[pltpu.VMEM((512, 512), bf16)] * 6
        + [
            pltpu.VMEM((1024, 1024), bf16),
            pltpu.VMEM((NR, 16, 128, BS), bf16),
            pltpu.SemaphoreType.DMA,
        ],
        compiler_params=pltpu.CompilerParams(vmem_limit_bytes=48 << 20),
        name="update",
    )(tab, fm, front, panel, ar, ac, xb, x3, kids)


def tables(maps, r, c):
    q8, q16 = np.arange(NR), np.arange(NC)
    kr, ir = np.repeat(q8, 8), np.tile(q8, 8)
    kc, jc = np.repeat(q8, 4), np.tile(np.arange(4), 8)
    nothing = np.zeros(24, np.int32)
    join = lambda *parts: np.concatenate(parts).astype(np.int32)
    own = join(nothing + 1, 0 * kr, 0 * kc, 0 * kr, 0 * kc)
    child = join(nothing, kr, kc, kr, kc)
    per_row = join(nothing, 8 + 0 * kr, 0 * kc, 8 + 0 * kr, 0 * kc)
    per_col = join(nothing, 0 * kr, 4 + 0 * kc, 0 * kr, 4 + 0 * kc)
    start = join(8 * q8, 4 * q16, 0 * kr, 0 * kc, 0 * kr, 0 * kc)
    block = join(nothing, ir, jc, ir, jc)
    cap = join(12 + 0 * q8, 14 + 0 * q16, 12 + 0 * kr, 14 + 0 * kc, 0 * kr, 0 * kc)
    base = start + per_row * r + per_col * c
    mine = jnp.where(own == 1, r, child)[:, None, None] == jnp.arange(NR)[:, None]
    below = jnp.sum(mine & (maps < base[:, None, None]), axis=(1, 2), dtype=jnp.int32)
    found = jnp.sum(
        (mine & (maps == (base + block)[:, None, None])) * jnp.arange(1, 17, dtype=jnp.int32),
        axis=(1, 2), dtype=jnp.int32,
    )
    first = jnp.minimum(below, cap)
    return jnp.where(
        own == 1,
        first,
        jnp.where(cap == 0, (found > 0).astype(jnp.int32), jnp.where(found > 0, found - 1 - first, 0)),
    )


def local(front, child_updates, child_maps, fill_mask):
    r = lax.axis_index("row")
    c = lax.axis_index("col")
    tab = tables(child_maps, r, c)
    kids, ar, ac, xb, x3, panel = exchange(
        tab, fill_mask, child_updates[0], front.reshape(8, BS, 1024)
    )
    return update(tab, fill_mask, front, panel, ar, ac, xb, x3, kids)


def solution(mesh):
    placed = (P("row", "col"), P("row", "col", None), P(), P())
    return jax.shard_map(
        local, mesh=mesh, in_specs=placed, out_specs=P("row", "col"), check_vma=False
    )
```
